256 devices in a mesh: scen: 32 (over x, y, core), fs: 8 (over z).
Axes of the slice: x: 4, y: 4, z: 8, core: 2. Of those that a mesh axis runs over, the one named last changes fastest.
Arguments:
- scen_rhs: float32 [256, 64, 64, 128], P('scen', 'fs')
- first_rhs: float32 [8, 2048, 128], P('fs', 'scen'), may hold values from -6 to 6
- diag_blocks: float32 [256, 64, 64, 64], P('scen', 'fs')
- diag_inverse: bfloat16 [256, 64, 64, 64], P('scen', 'fs')
- couplings: float32 [256, 64, 2, 64, 64], P('scen', 'fs'), may hold values from -0.125 to 0.125
- border: float32 [256, 64, 64, 64], P('scen', 'fs'), may hold values from -0.125 to 0.125
- border_block: int32 [256, 64], P('scen', 'fs'), may hold values from 0 to 31
- first_diag: float32 [8, 2048], P('fs', 'scen'), may hold values from 0.5 to 2
- schur_inverse: bfloat16 [8, 2048, 8, 2048], P(None, 'scen', 'fs')
Outputs:
- scen_sol: float32 [256, 64, 64, 128], P('scen', 'fs')
- first_sol: float32 [8, 2048, 128], P('fs', 'scen')
- first_res: float32 [8, 2048, 128], P('fs', 'scen')
The draws below stay inside these ranges and needn't reach their ends.
All inputs are finite; a program needn't handle non-finite values.
Results may differ from the reference program's by a relative error of at most 0.0049.
Values may be sent and summed in bfloat16 or wider, within the bound.
No kernel may reach another device: no remote copies, remote signals or barrier semaphores. Data moves between devices by JAX's collectives and lax.ppermute only.
A program may use at most 128 MiB of HBM per device.

```python
import math
import jax
import jax.numpy as jnp
from jax import lax

N0 = 16384
WINDOWS = 64
WIN = 64
R = 128
ROUNDS = 2
SCEN = 256
GROUPS = 8
GROUP_ROWS = 2048
BLOCKS = 32


def scenario_ramp():
    count = max(SCEN - 1, 1)
    return jnp.arange(SCEN, dtype=jnp.float32) / count


def draw_scen_rhs(key, part):
    base = jax.random.fold_in(key, 41)
    shape = (SCEN, WINDOWS, WIN, R)
    ramp = scenario_ramp()
    values = jnp.clip(jax.random.normal(base, shape, jnp.float32), -5.0, 5.0)
    rise = jnp.exp(math.log(4.0) * ramp)
    return values * rise[:, None, None, None]


def window_parts(key):
    base = jax.random.fold_in(key, 17)
    key_scale, key_mix = jax.random.split(base)
    scales = jnp.exp(jax.random.uniform(key_scale, (SCEN, WINDOWS, WIN), jnp.float32, math.log(2.0), math.log(16.0)))
    ramp = scenario_ramp()
    spread = ((0.05 + 0.3 * ramp) / math.sqrt(WIN))[:, None, None, None]
    mixing = jnp.clip(jax.random.normal(key_mix, (SCEN, WINDOWS, WIN, WIN), jnp.float32), -4.0, 4.0) * spread
    return (scales, mixing)


def draw_diag_blocks(key, part):
    scales, mixing = window_parts(key)
    ident = jnp.eye(WIN, dtype=jnp.float32)
    return scales[..., :, None] * (ident + mixing)


def draw_diag_inverse(key, part):
    scales, mixing = window_parts(key)
    ident = jnp.eye(WIN, dtype=jnp.float32)
    return ((ident - mixing) / scales[..., None, :]).astype(jnp.bfloat16)


def draw_schur_inverse(key, part):
    base = jax.random.fold_in(key, 29)
    key_diag, key_off = jax.random.split(base)
    shape = (GROUPS, GROUP_ROWS, GROUPS, GROUP_ROWS)
    spread = 0.08 / math.sqrt(N0)
    off_part = jnp.clip(jax.random.normal(key_off, shape, jnp.float32), -5.0, 5.0) * spread
    diag_vals = jnp.exp(jax.random.uniform(key_diag, (GROUPS, GROUP_ROWS), jnp.float32, math.log(0.15), math.log(0.45)))
    same_group = lax_eq(0, 2, shape)
    same_row = lax_eq(1, 3, shape)
    on_diag = jnp.logical_and(same_group, same_row).astype(jnp.float32)
    return (off_part + on_diag * diag_vals[None, None, :, :]).astype(jnp.bfloat16)


def lax_eq(first_dim, second_dim, shape):
    first_idx = jax.lax.broadcasted_iota(jnp.int32, shape, first_dim)
    second_idx = jax.lax.broadcasted_iota(jnp.int32, shape, second_dim)
    return first_idx == second_idx


def plant(values, rng, least, top_value):
    spot = [jax.random.randint(jax.random.fold_in(rng, axis), (), 0, length) for axis, length in enumerate(values.shape)]
    widest = values.shape.index(max(values.shape))
    next_to = spot[:widest] + [(spot[widest] + 1) % values.shape[widest]] + spot[widest + 1:]
    return values.at[tuple(spot)].set(least).at[tuple(next_to)].set(top_value)


def block_scale(rng, dims, pieces, least, top_value):
    factor_of, own = 1.0, jax.random.fold_in(rng, 6)
    for axis_at, shards_of in pieces:
        steps = jnp.exp(jax.random.uniform(jax.random.fold_in(own, axis_at), (shards_of,), jnp.float32, least / len(pieces), top_value / len(pieces)))
        factor_of = factor_of * jnp.repeat(steps, dims[axis_at] // shards_of).reshape([-1 if axis == axis_at else 1 for axis in range(len(dims))])
    return factor_of


def bell_draw(stream_key, shape, width, limit, pieces=(), kind=jnp.bfloat16):
    values = jax.random.normal(stream_key, shape, jnp.float32) * width
    if len(pieces) > 0:
        values = block_scale(stream_key, shape, pieces, -0.22, 0.18) * values
    return jnp.clip(values, min=-limit, max=limit).astype(kind)


def setup_inputs(seed: int = 0) -> dict:
    seeds = jax.random.split(jax.random.key(seed), 10)
    scen_rhs = draw_scen_rhs(jax.random.fold_in(seeds[9], 71), 0)
    first_rhs = bell_draw(seeds[1], (GROUPS, GROUP_ROWS, R), 1.0, 6.0, ((0, 8), (1, 32)), jnp.float32)
    diag_blocks = draw_diag_blocks(jax.random.fold_in(seeds[9], 71), 0)
    diag_inverse = draw_diag_inverse(jax.random.fold_in(seeds[9], 71), 0)
    couplings = bell_draw(seeds[4], (SCEN, WINDOWS, 2, WIN, WIN), (0.25 * WIN ** -0.5), 0.125, ((0, 32), (1, 8)), jnp.float32)
    border = bell_draw(seeds[5], (SCEN, WINDOWS, WIN, WIN), (0.25 * WIN ** -0.5), 0.125, ((0, 32), (1, 8)), jnp.float32)
    border_block = plant(jax.random.randint(seeds[6], (SCEN, WINDOWS), 0, BLOCKS), jax.random.fold_in(seeds[6], 1), 0, BLOCKS - 1).astype(jnp.int32)
    first_diag = jnp.clip(jnp.exp(math.log(2.0) - 1.3862944 * jax.random.uniform(seeds[7], (GROUPS, GROUP_ROWS), jnp.float32) ** block_scale(seeds[7], (GROUPS, GROUP_ROWS), ((0, 8), (1, 32)), -0.2, 0.2)), 0.5, 2.0)
    schur_inverse = draw_schur_inverse(jax.random.fold_in(seeds[9], 71), 0)
    return {"scen_rhs": scen_rhs, "first_rhs": first_rhs, "diag_blocks": diag_blocks, "diag_inverse": diag_inverse, "couplings": couplings, "border": border, "border_block": border_block, "first_diag": first_diag, "schur_inverse": schur_inverse}


EXACT = lax.Precision.HIGHEST


def tile_product(mats, values):
    return jnp.einsum('swij,swjr->swir', mats, values, precision=EXACT)


def tile_transpose(mats, values):
    return jnp.einsum('swji,swjr->swir', mats, values, precision=EXACT)


def low_product(mats, values):
    return jnp.einsum('swij,swjr->swir', mats, values, preferred_element_type=jnp.float32)


def reference(scen_rhs, first_rhs, diag_blocks, diag_inverse, couplings, border, border_block, first_diag, schur_inverse):
    per_group = WINDOWS // GROUPS
    group_of = jnp.arange(WINDOWS, dtype=jnp.int32) // per_group
    global_block = (group_of[None, :] * BLOCKS + border_block).reshape(-1).astype(jnp.int32)
    block_total = N0 // WIN
    schur_flat = schur_inverse.reshape(N0, N0)
    first_gain = first_diag.reshape(N0, 1)

    def border_gather(values):
        terms = tile_transpose(border, values).reshape(SCEN * WINDOWS, WIN, R)
        summed = jax.ops.segment_sum(terms, global_block, num_segments=block_total)
        return summed.reshape(N0, R)

    def spread(first_vec):
        blocks = first_vec.reshape(block_total, WIN, R)
        return jnp.take(blocks, global_block, axis=0).reshape(SCEN, WINDOWS, WIN, R)

    scen_res = scen_rhs
    first_res = first_rhs.reshape(N0, R)
    scen_sol = jnp.zeros((SCEN, WINDOWS, WIN, R), jnp.float32)
    first_sol = jnp.zeros((N0, R), jnp.float32)
    for round_index in range(ROUNDS):
        guess = low_product(diag_inverse, scen_res.astype(jnp.bfloat16))
        schur_rhs = (first_res + border_gather(guess)).astype(jnp.bfloat16)
        first_step = lax.dot_general(schur_flat, schur_rhs, (((0,), (0,)), ((), ())), preferred_element_type=jnp.float32)
        widened = spread(first_step)
        coupled = tile_product(border, widened)
        lift = coupled.astype(jnp.bfloat16)
        scen_step = guess - low_product(diag_inverse, lift)
        before = jnp.pad(scen_step, ((0, 0), (1, 0), (0, 0), (0, 0)))[:, :-1]
        after = jnp.pad(scen_step, ((0, 0), (0, 1), (0, 0), (0, 0)))[:, 1:]
        image_scen = tile_product(diag_blocks, scen_step) + tile_product(couplings[:, :, 0], before)
        image_scen = image_scen + tile_product(couplings[:, :, 1], after) + coupled
        image_first = first_gain * first_step - border_gather(scen_step)
        along = jnp.sum(scen_res * image_scen, axis=(0, 1, 2)) + jnp.sum(first_res * image_first, axis=0)
        energy = jnp.sum(image_scen * image_scen, axis=(0, 1, 2)) + jnp.sum(image_first * image_first, axis=0)
        step_size = along / (energy + 1e-6)
        scen_sol = scen_sol + step_size * scen_step
        first_sol = first_sol + step_size * first_step
        scen_res = scen_res - step_size * image_scen
        first_res = first_res - step_size * image_first
    return scen_sol, first_sol.reshape(GROUPS, GROUP_ROWS, R), first_res.reshape(GROUPS, GROUP_ROWS, R)
```

```python
import jax
import jax.numpy as jnp
from jax import lax
from jax.sharding import Mesh
from jax.sharding import PartitionSpec as P

EXACT = lax.Precision.HIGHEST
CHIP_X = 4
CHIP_Y = 4
CORES = 2
PLANE = ("x", "y")
SCEN = ("x", "y", "core")
SWAP = [(0, 1), (1, 0)]


def tile_product(mats, values):
    return jnp.einsum("swij,swjr->swir", mats, values, precision=EXACT)


def tile_transpose(mats, values):
    return jnp.einsum("swji,swjr->swir", mats, values, precision=EXACT)


def round_half(values):
    return lax.reduce_precision(values, 8, 7)


def split_three(values):
    high = round_half(values)
    rest = values - high
    mid = round_half(rest)
    low = round_half(rest - mid)
    return jnp.concatenate([high, mid, low], axis=0).astype(jnp.bfloat16)


def join_three(pieces):
    count = pieces.shape[-2] // 3
    wide = pieces.astype(jnp.float32)
    return wide[..., :count, :] + wide[..., count : 2 * count, :] + wide[..., 2 * count :, :]


def per_device(
    scen_rhs,
    first_rhs,
    diag_blocks,
    diag_inverse,
    couplings,
    border,
    border_block,
    first_diag,
    schur_inverse,
):
    core = lax.axis_index("core")
    window_size = diag_blocks.shape[-1]
    group_rows = schur_inverse.shape[-1]
    own_rows = first_rhs.shape[1]
    rhs_count = scen_rhs.shape[-1]
    block_count = group_rows // window_size
    half = block_count // CORES
    groups = lax.axis_size("fs")
    plane = CHIP_X * CHIP_Y
    scen_local, window_local = border_block.shape
    slot_count = scen_local * window_local
    columns = schur_inverse.shape[0] * schur_inverse.shape[1]
    schur_flat = schur_inverse.reshape(columns, group_rows)
    gain = first_diag.reshape(own_rows, 1)
    first_res = first_rhs.reshape(own_rows, rhs_count)

    address = ((border_block & 1) ^ core) * half + (border_block >> 1)
    selector = (
        address.reshape(1, slot_count) == jnp.arange(block_count, dtype=jnp.int32)[:, None]
    ).astype(jnp.float32)
    inverse_wide = diag_inverse.astype(jnp.float32)

    def collect(values):
        width = values.shape[-1]
        terms = tile_transpose(border, values).reshape(slot_count, window_size * width)
        return jnp.dot(selector, terms, precision=EXACT).reshape(block_count, window_size, width)

    def swap(values):
        return lax.ppermute(values, "core", SWAP)

    def spread_plane(values):
        return lax.all_to_all(values, PLANE, 0, 0)

    def scatter_sum(partial_value):
        mine = partial_value[:half] + swap(partial_value[half:])
        return jnp.sum(spread_plane(mine), axis=0)

    def gather_fs(values):
        copies = jnp.broadcast_to(values[None], (groups,) + values.shape)
        return lax.all_to_all(copies, "fs", 0, 0)

    def gather_blocks(values):
        copies = jnp.broadcast_to(values[None], (plane,) + values.shape)
        mine = spread_plane(copies)
        return jnp.concatenate([mine, swap(mine)], axis=0)

    def solve(operand):
        value = lax.dot_general(
            schur_flat, operand, (((0,), (0,)), ((), ())), preferred_element_type=jnp.float32
        )
        value = value.reshape(half, CORES, window_size, rhs_count)
        first, second = value[:, 0], value[:, 1]
        on_first = core == 0
        return jnp.where(on_first, first, second), jnp.where(on_first, second, first)

    def lift_of(blocks):
        wide = lax.dot_general(
            selector.astype(jnp.bfloat16),
            blocks.reshape(block_count, window_size * rhs_count),
            (((0,), (0,)), ((), ())),
            preferred_element_type=jnp.float32,
        )
        return tile_product(
            border, wide.reshape(scen_local, window_local, window_size, rhs_count)
        )

    def scen_image(step, lift):
        ends = groups - 1
        head = lax.ppermute(step[:, -1:], "fs", [(i, i + 1) for i in range(ends)])
        tail = lax.ppermute(step[:, :1], "fs", [(i + 1, i) for i in range(ends)])
        before = jnp.concatenate([head, step[:, :-1]], axis=1)
        after = jnp.concatenate([step[:, 1:], tail], axis=1)
        image = tile_product(diag_blocks, step) + tile_product(couplings[:, :, 0], before)
        return image + tile_product(couplings[:, :, 1], after) + lift

    def dots(res, image, res_first, image_first):
        along = jnp.sum(res * image, axis=(0, 1, 2)) + jnp.sum(res_first * image_first, axis=0)
        energy = jnp.sum(image * image, axis=(0, 1, 2)) + jnp.sum(image_first * image_first, axis=0)
        return jnp.stack([along, energy])

    guess = tile_product(inverse_wide, scen_rhs)
    weight_terms = collect(tile_product(inverse_wide, border))
    quarter = window_size // 2
    weight_packed = jnp.concatenate([weight_terms[:, :quarter], weight_terms[:, quarter:]], axis=2)
    sums = scatter_sum(jnp.concatenate([collect(guess), weight_packed], axis=1))
    guess_sum = sums[:window_size]
    weight_rows = sums[window_size:]
    weight = jnp.concatenate([weight_rows[:, :window_size], weight_rows[:, window_size:]], axis=0)

    def first_image(step, summed):
        return gain * step - summed + jnp.dot(weight, step, precision=EXACT)

    schur_rhs = first_res + guess_sum
    gathered = gather_fs(schur_rhs.astype(jnp.bfloat16)).reshape(columns, rhs_count)
    mine, theirs = solve(gathered)
    mine = mine + swap(theirs)
    first_step = jnp.sum(spread_plane(mine.astype(jnp.bfloat16)).astype(jnp.float32), axis=0)
    first_step = round_half(first_step)
    lift = lift_of(gather_blocks(first_step.astype(jnp.bfloat16)))
    scen_step = guess - tile_product(inverse_wide, lift)
    image = scen_image(scen_step, lift)
    image_first = first_image(first_step, guess_sum)
    turn = tile_product(inverse_wide, image)
    turn_sum = scatter_sum(collect(turn))
    local_dots = split_three(dots(scen_rhs, image, first_res, image_first))

    change = schur_rhs - (image_first + turn_sum)
    pad = jnp.zeros((16 - local_dots.shape[0], rhs_count), jnp.bfloat16)
    message = jnp.concatenate([change.astype(jnp.bfloat16), local_dots, pad], axis=0)
    arrived = gather_fs(message)
    plane_dots = jnp.sum(join_three(arrived[:, own_rows : own_rows + 6]), axis=0)
    mine, theirs = solve(arrived[:, :own_rows].reshape(columns, rhs_count))
    mine = mine + swap(theirs)
    pair_dots = plane_dots + swap(plane_dots)
    tail = jnp.concatenate([split_three(pair_dots), pad], axis=0)
    tail = jnp.broadcast_to(tail[None], (plane,) + tail.shape)
    arrived = spread_plane(jnp.concatenate([mine.astype(jnp.bfloat16), tail], axis=1))
    solved = jnp.sum(arrived[:, :own_rows].astype(jnp.float32), axis=0)
    along, energy = jnp.sum(join_three(arrived[:, own_rows : own_rows + 6]), axis=0)
    size = along / (energy + 1e-06)

    next_step = round_half((1.0 - size) * first_step + size * solved)
    lift = lift_of(gather_blocks(next_step.astype(jnp.bfloat16)))
    next_scen = guess - size * turn - tile_product(inverse_wide, lift)
    next_image = scen_image(next_scen, lift)
    next_first = first_image(next_step, guess_sum - size * turn_sum)
    scen_res = scen_rhs - size * image
    first_res = first_res - size * image_first
    local_dots = dots(scen_res, next_image, first_res, next_first)
    everyone = SCEN + ("fs",)
    total = plane * CORES * groups
    copies = jnp.broadcast_to(local_dots[None], (total,) + local_dots.shape)
    along, energy = jnp.sum(lax.all_to_all(copies, everyone, 0, 0), axis=0)
    next_size = along / (energy + 1e-06)
    scen_sol = size * scen_step + next_size * next_scen
    first_sol = size * first_step + next_size * next_step
    first_res = first_res - next_size * next_first
    return (
        scen_sol,
        first_sol.reshape(1, own_rows, rhs_count),
        first_res.reshape(1, own_rows, rhs_count),
    )


def solution(mesh):
    groups = mesh.shape["fs"]
    grid = Mesh(
        mesh.devices.reshape(CHIP_X, CHIP_Y, CORES, groups), ("x", "y", "core", "fs")
    )
    return jax.shard_map(
        per_device,
        mesh=grid,
        in_specs=(
            P(SCEN, "fs", None, None),
            P("fs", SCEN, None),
            P(SCEN, "fs", None, None),
            P(SCEN, "fs", None, None),
            P(SCEN, "fs", None, None, None),
            P(SCEN, "fs", None, None),
            P(SCEN, "fs"),
            P("fs", SCEN),
            P(None, SCEN, "fs", None),
        ),
        out_specs=(
            P(SCEN, "fs", None, None),
            P("fs", SCEN, None),
            P("fs", SCEN, None),
        ),
        check_vma=False,
    )
```

```python
import functools

import jax
import jax.numpy as jnp
from jax import lax
from jax.experimental import pallas as pl
from jax.experimental.pallas import tpu as pltpu
from jax.sharding import Mesh
from jax.sharding import PartitionSpec as P

CHIP_X = 4
CHIP_Y = 4
CORES = 2
PLANE = ("x", "y")
SCEN = ("x", "y", "core")
SWAP = [(0, 1), (1, 0)]
F32 = jnp.float32
HALF = jnp.bfloat16
DOT_ROWS = 16
BATCH = 2
EXACT = lax.Precision.HIGHEST
PARAMS = pltpu.CompilerParams(
    dimension_semantics=("arbitrary",), vmem_limit_bytes=24 * 1024 * 1024
)
WIDE = pltpu.CompilerParams(
    dimension_semantics=("arbitrary",), vmem_limit_bytes=56 * 1024 * 1024
)
PLAIN = pltpu.CompilerParams(vmem_limit_bytes=16 * 1024 * 1024)


def split(values):
    high = values.astype(HALF)
    return high, (values - high.astype(F32)).astype(HALF)


def dot(left, right):
    return jnp.dot(left, right, preferred_element_type=F32)


def dot_t(left, right):
    return lax.dot_general(left, right, (((0,), (0,)), ((), ())), preferred_element_type=F32)


def wide2(pieces):
    return jnp.concatenate([pieces[0], pieces[1]], axis=1)


def wide3(pieces):
    return jnp.concatenate([pieces[0], pieces[0], pieces[1]], axis=1)


def tall2(pieces):
    return jnp.concatenate([pieces[0], pieces[1]], axis=0)


def tall3(pieces):
    return jnp.concatenate([pieces[0], pieces[1], pieces[0]], axis=0)


def pieces_of(vectors):
    rows = []
    for vector in vectors:
        high = vector.astype(HALF).astype(F32)
        rest = vector - high
        mid = rest.astype(HALF).astype(F32)
        rows += [high, mid, rest - mid]
    return stack_rows(rows)


def stack_rows(rows):
    width = rows[0].shape[-1]
    place = lax.broadcasted_iota(jnp.int32, (DOT_ROWS, width), 0)
    total = jnp.zeros((DOT_ROWS, width), F32)
    for index, row in enumerate(rows):
        total = jnp.where(place == index, jnp.broadcast_to(row, (DOT_ROWS, width)), total)
    return total


def join_pieces(rows):
    return rows[0:1] + rows[1:2] + rows[2:3], rows[3:4] + rows[4:5] + rows[5:6]


def fold(values):
    return jnp.sum(values.reshape(values.shape[0] // 8, 8, values.shape[1]), axis=0)


def first_block(*shape):
    return pl.BlockSpec((1,) + shape, lambda s, *_: (s,) + (0,) * len(shape))


def whole(*shape):
    return pl.BlockSpec(shape, lambda *_: (0,) * len(shape))


def table():
    return pl.BlockSpec(memory_space=pltpu.SMEM)


def prepare_kernel(where_ref, res_ref, inv_ref, border_ref, factor_ref, keep_ref, send_ref, acc):
    step = pl.program_id(0)
    scens, windows, size, rhs = res_ref.shape
    half = keep_ref.shape[0]

    @pl.when(step == 0)
    def _():
        acc[...] = jnp.zeros_like(acc)

    spots = [(s, w) for s in range(scens) for w in range(windows)]
    tiles = [split(border_ref[s, w]) for s, w in spots]
    products = []
    for (s, w), tile in zip(spots, tiles):
        inverse = inv_ref[s, w]
        products.append(dot_t(tall2(tile), tall2((inverse, inverse))))
    terms = []
    for (s, w), tile, product in zip(spots, tiles, products):
        factor = wide3(split(product))
        factor_ref[s, w] = factor
        right = jnp.concatenate([tall3(split(res_ref[s, w])), tall3(tile)], axis=1)
        terms.append(dot(factor, right))
    for index, term in enumerate(terms):
        slot = where_ref[step * scens * windows + index]
        acc[slot] += term

    @pl.when(step == pl.num_programs(0) - 1)
    def _():
        for start, out in ((0, keep_ref), (half, send_ref)):
            out[:, 0:size, :] = acc[start : start + half, :, 0:rhs]
            out[:, size:, 0:size] = acc[start : start + half, 0 : size // 2, rhs : rhs + size]
            out[:, size:, size:] = acc[start : start + half, size // 2 :, rhs : rhs + size]


def begin_kernel(arrived_ref, first_ref, diag_ref, sum_ref, weight_ref, message_ref):
    size = first_ref.shape[0]
    total = jnp.sum(arrived_ref[...], axis=0)
    summed = total[:size]
    sum_ref[...] = summed
    side = size // 2
    diag = jnp.concatenate([diag_ref[...], diag_ref[...]], axis=1)
    row = lax.broadcasted_iota(jnp.int32, (side, 2 * size), 0)
    lane = lax.broadcasted_iota(jnp.int32, (side, 2 * size), 1)
    spot = jnp.logical_or(lane == row, lane == row + side + size)
    weight_ref[...] = total[size:] + jnp.where(spot, jnp.broadcast_to(diag, (side, 2 * size)), 0.0)
    message = (first_ref[...] + summed).astype(HALF)
    message_ref[...] = jnp.broadcast_to(message[None], message_ref.shape)


def solve_kernel(core_ref, arrived_ref, schur_ref, mine_ref, theirs_ref, *rest, with_dots):
    groups, _, rhs = arrived_ref.shape
    size = mine_ref.shape[1]
    tile = pl.program_id(0)
    per_tile = schur_ref.shape[1] // size
    operand = rest[-1]

    @pl.when(tile == 0)
    def _():
        for g in range(groups):
            operand[g * size : (g + 1) * size, :] = arrived_ref[g, 0:size, :]
        if with_dots:
            rows = jnp.sum(arrived_ref[:, size:, :].astype(F32), axis=0)
            dots = stack_rows(list(join_pieces(rows)))
            rest[0][...] = dots
            theirs_ref[theirs_ref.shape[0] - 1, 0:DOT_ROWS, :] = dots

    value = dot_t(schur_ref[...], operand[...])
    for pair in range(per_tile // CORES):
        even = value[(2 * pair) * size : (2 * pair + 1) * size]
        odd = value[(2 * pair + 1) * size : (2 * pair + 2) * size]
        slot = tile * (per_tile // CORES) + pair

        @pl.when(core_ref[0] == 0)
        def _():
            mine_ref[slot] = even
            theirs_ref[slot] = odd

        @pl.when(core_ref[0] != 0)
        def _():
            mine_ref[slot] = odd
            theirs_ref[slot] = even


def pair_kernel(mine_ref, got_ref, *rest):
    message_ref = rest[-1]
    plane, size, rhs = mine_ref.shape
    message_ref[:, 0:size, :] = (mine_ref[...] + got_ref[0:plane]).astype(HALF)
    if len(rest) > 1:
        dots = rest[0][...] + got_ref[plane, 0:DOT_ROWS, :]
        pieces = pieces_of([dots[0:1], dots[1:2]]).astype(HALF)
        message_ref[:, size:, :] = jnp.broadcast_to(pieces[None], (plane,) + pieces.shape)


def owned_kernel(arrived_ref, step_ref, message_ref):
    total = jnp.sum(arrived_ref[...].astype(F32), axis=0).astype(HALF)
    step_ref[...] = total.astype(F32)
    message_ref[...] = jnp.broadcast_to(total[None], message_ref.shape)


def residual(res_ref, last, s, w):
    if last is None:
        return res_ref[s, w]
    image_ref, side_ref, size_ref = last
    windows = res_ref.shape[1]
    if w == 0:
        image = side_ref[s, 0]
    elif w == windows - 1:
        image = side_ref[s, 1]
    else:
        image = image_ref[s, w]
    return res_ref[s, w] - size_ref[0:1] * image


def window_steps(tables, mine_ref, other_ref, border_ref, inv_ref, spots, values):
    slot_ref, side_ref = tables
    tiles, blocks, lifts = [], [], []
    for s, w in spots:
        index = s * border_ref.shape[1] + w
        slot = slot_ref[index]
        mine = mine_ref[slot].astype(F32)
        other = other_ref[slot].astype(F32)
        block = jnp.where(side_ref[index] == 0, mine, other).astype(HALF)
        tiles.append(wide2(split(border_ref[s, w])))
        blocks.append(tall2((block, block)))
        lifts.append(dot(tiles[-1], blocks[-1]))
    steps = []
    for (s, w), res, lift in zip(spots, values, lifts):
        inverse = inv_ref[s, w]
        steps.append(dot(wide2((inverse, inverse)), tall2(split(res - lift))))
    return steps, tiles, blocks


def edge_kernel(slot_ref, side_ref, mine_ref, other_ref, border_ref, inv_ref, res_ref, *rest):
    head_ref, tail_ref = rest[-2:]
    last = rest[:3] if len(rest) > 2 else None
    scens, windows = res_ref.shape[:2]
    tables = (slot_ref, side_ref)
    spots = [(s, w) for s in range(scens) for w in (0, windows - 1)]
    values = [residual(res_ref, last, s, w) for s, w in spots]
    steps, _, _ = window_steps(tables, mine_ref, other_ref, border_ref, inv_ref, spots, values)
    for (s, w), step in zip(spots, steps):
        out = head_ref if w == 0 else tail_ref
        out[s] = step.astype(HALF)


def step_kernel(
    slot_ref, side_ref, where_ref, mine_ref, other_ref, border_ref, inv_ref, res_ref, diag_ref, pair_ref, *rest, first
):
    scens, windows, size, rhs = res_ref.shape
    if first:
        factor_ref, step_ref, image_ref, dots_ref, acc_ref = rest
        last = None
        acc_ref[...] = jnp.zeros_like(acc_ref)
    else:
        last = rest[:3]
        step_ref, left_ref, image_ref, dots_ref = rest[3:]
    tables = (slot_ref, side_ref)

    def body(step, totals):
        along, energy = totals
        spots = [(step * BATCH + s, w) for s in range(BATCH) for w in range(windows)]
        left = [residual(res_ref, last, s, w) for s, w in spots]
        found, tiles, blocks = window_steps(tables, mine_ref, other_ref, border_ref, inv_ref, spots, left)
        steps = []
        for (s, w), value in zip(spots, found):
            step_ref[s, w] = value
            steps.append(tall3(split(value)))
        images = []
        for at, (s, w) in enumerate(spots):
            mats = [tiles[at], wide3(split(diag_ref[s, w]))]
            values = [blocks[at], steps[at]]
            if w > 0:
                mats.append(wide3(split(pair_ref[s, w, 0])))
                values.append(steps[at - 1])
            if w < windows - 1:
                mats.append(wide3(split(pair_ref[s, w, 1])))
                values.append(steps[at + 1])
            images.append(dot(jnp.concatenate(mats, axis=1), jnp.concatenate(values, axis=0)))
        terms = []
        for (s, w), res, image in zip(spots, left, images):
            inner = 0 < w < windows - 1
            if inner:
                along += fold(res * image)
                energy += fold(image * image)
            if first:
                image_ref[s, w] = image
                if inner:
                    terms.append((s * windows + w, dot(factor_ref[s, w], tall3(split(image)))))
            elif not inner:
                spot = 0 if w == 0 else 1
                image_ref[s, spot] = image
                left_ref[s, spot] = res
        for index, term in terms:
            acc_ref[where_ref[index]] += term
        return along, energy

    zero = jnp.zeros((8, rhs), F32)
    along, energy = lax.fori_loop(0, scens // BATCH, body, (zero, zero))
    dots_ref[0:8, :] = along
    dots_ref[8:16, :] = energy


def finish_kernel(where_ref, image_ref, before_ref, after_ref, pair_ref, res_ref, dots_ref, *rest, first):
    scens, windows, _, size, _ = pair_ref.shape
    rhs = before_ref.shape[2]
    if first:
        factor_ref, acc_ref, side_ref, out_ref, keep_ref, send_ref, acc = rest
        acc[...] = acc_ref[...]
    else:
        (out_ref,) = rest
    along = jnp.zeros((8, rhs), F32)
    energy = jnp.zeros((8, rhs), F32)
    terms = []
    spots = [(s, spot) for s in range(scens) for spot in (0, 1)]
    halos = []
    for s, spot in spots:
        w = (windows - 1) * spot
        halo = (before_ref, after_ref)[spot][s]
        halos.append(dot(wide2(split(pair_ref[s, w, spot])), tall2((halo, halo))))
    for (s, spot), halo in zip(spots, halos):
        w = (windows - 1) * spot
        at = w if first else spot
        image = halo + image_ref[s, at]
        along += fold(res_ref[s, at] * image)
        energy += fold(image * image)
        if first:
            side_ref[s, spot] = image
            terms.append((s * windows + w, dot(factor_ref[s, w], tall3(split(image)))))
    out_ref[0:8, :] = dots_ref[0:8, :] + along
    out_ref[8:16, :] = dots_ref[8:16, :] + energy
    if first:
        for index, term in terms:
            acc[where_ref[index]] += term
        half = keep_ref.shape[0]
        keep_ref[...] = acc[0:half]
        send_ref[...] = acc[half:]


def first_image(weight, step, summed):
    size = step.shape[0]
    top = jnp.dot(weight[:, :size], step, precision=EXACT, preferred_element_type=F32)
    low = jnp.dot(weight[:, size:], step, precision=EXACT, preferred_element_type=F32)
    return jnp.concatenate([top, low], axis=0) - summed


def local_dots(dots, res, image):
    along = jnp.sum(dots[0:8] + fold(res * image), axis=0, keepdims=True)
    energy = jnp.sum(dots[8:16] + fold(image * image), axis=0, keepdims=True)
    return along, energy


def turn_kernel(arrived_ref, step_ref, sum_ref, weight_ref, first_ref, dots_ref, turn_ref, image_ref, message_ref):
    size = step_ref.shape[0]
    turn = jnp.sum(arrived_ref[...], axis=0)
    image = first_image(weight_ref[...], step_ref[...], sum_ref[...])
    turn_ref[...] = turn
    image_ref[...] = image
    change = (first_ref[...] + sum_ref[...]) - (image + turn)
    pieces = pieces_of(local_dots(dots_ref[...], first_ref[...], image)).astype(HALF)
    message = jnp.concatenate([change.astype(HALF), pieces], axis=0)
    message_ref[...] = jnp.broadcast_to(message[None], message_ref.shape)


def next_kernel(arrived_ref, step_ref, size_ref, next_ref, message_ref):
    rows = step_ref.shape[0]
    total = jnp.sum(arrived_ref[...].astype(F32), axis=0)
    along, energy = join_pieces(total[rows:])
    size = along / (energy + 1e-06)
    size_ref[...] = jnp.broadcast_to(size, size_ref.shape)
    step = ((1.0 - size) * step_ref[...] + size * total[:rows]).astype(HALF)
    next_ref[...] = step.astype(F32)
    message_ref[...] = jnp.broadcast_to(step[None], message_ref.shape)


def ending_kernel(
    size_ref, step_ref, sum_ref, turn_ref, weight_ref, first_ref, image_ref, dots_ref, next_ref, res_ref, out_ref
):
    size = size_ref[0:1]
    image = first_image(weight_ref[...], step_ref[...], sum_ref[...] - size * turn_ref[...])
    res = first_ref[...] - size * image_ref[...]
    next_ref[...] = image
    res_ref[...] = res
    along, energy = local_dots(dots_ref[...], res, image)
    row = lax.broadcasted_iota(jnp.int32, (2, along.shape[1]), 0)
    both = jnp.where(row == 0, jnp.broadcast_to(along, row.shape), jnp.broadcast_to(energy, row.shape))
    out_ref[...] = both


def final_kernel(
    arrived_ref, size_ref, step_ref, later_ref, first_ref, next_ref, res_ref, image_ref, sol_ref, head_ref, out_ref, later_size
):
    scen = pl.program_id(0)
    size = size_ref[0:1]

    @pl.when(scen == 0)
    def _():
        total = jnp.sum(arrived_ref[...], axis=0)
        later = total[0:1] / (total[1:2] + 1e-06)
        later_size[...] = jnp.broadcast_to(later, later_size.shape)
        head_ref[...] = size * first_ref[...] + later * next_ref[...]
        out_ref[...] = res_ref[...] - later * image_ref[...]

    scens = sol_ref.shape[0]
    for s in range(scens):
        at = scen * scens + s
        sol_ref[s] = size * step_ref[at] + later_size[0:1] * later_ref[at]


def shape(*dims, kind=F32):
    return jax.ShapeDtypeStruct(dims, kind)


def per_device(
    scen_rhs,
    first_rhs,
    diag_blocks,
    diag_inverse,
    couplings,
    border,
    border_block,
    first_diag,
    schur_inverse,
):
    core = lax.axis_index("core").astype(jnp.int32)
    scen_local, window_local, size, rhs = scen_rhs.shape
    group_rows = schur_inverse.shape[-1]
    blocks = group_rows // size
    half = blocks // CORES
    groups = lax.axis_size("fs")
    plane = CHIP_X * CHIP_Y
    columns = schur_inverse.shape[0] * schur_inverse.shape[1]
    schur_flat = schur_inverse.reshape(columns, group_rows)
    first_res = first_rhs.reshape(size, rhs)
    slots = (border_block >> 1).reshape(-1)
    sides = ((border_block & 1) ^ core).reshape(-1)
    address = sides * half + slots
    core_table = core.reshape(1)
    field = (window_local, size, rhs)
    tile = (window_local, size, size)
    grid = (scen_local,)
    fields = shape(scen_local, *field)
    edges = shape(scen_local, size, rhs)
    vector = shape(size, rhs)

    def swap(values):
        return lax.ppermute(values, "core", SWAP)

    def spread_plane(values):
        return lax.all_to_all(values, PLANE, 0, 0)

    def spread_fs(values):
        return lax.all_to_all(values, "fs", 0, 0)

    def solve(arrived, with_dots):
        rows = arrived.shape[1]
        tiles = 4
        wide = group_rows // tiles
        extra = 1 if with_dots else 0
        out_shape = [shape(half, size, rhs), shape(half + extra, size, rhs)]
        if with_dots:
            out_shape.append(shape(DOT_ROWS, rhs))
        out = pl.pallas_call(
            functools.partial(solve_kernel, with_dots=with_dots),
            out_shape=out_shape,
            grid=(tiles,),
            in_specs=[table(), whole(groups, rows, rhs), pl.BlockSpec((columns, wide), lambda t: (0, t))],
            out_specs=[whole(*o.shape) for o in out_shape],
            scratch_shapes=[pltpu.VMEM((columns, rhs), HALF)],
            compiler_params=PARAMS,
            name="solve",
        )(core_table, arrived, schur_flat)
        got = swap(out[1])
        rows_out = size + (DOT_ROWS if with_dots else 0)
        message = pl.pallas_call(
            pair_kernel,
            out_shape=shape(plane, rows_out, rhs, kind=HALF),
            compiler_params=PLAIN,
            name="pair",
        )(out[0], got, *out[2:])
        return spread_plane(message)

    def window_pass(message, last):
        first = last is None
        mine = spread_plane(message)
        other = swap(mine)
        extra = () if first else last
        args = (slots, sides, mine, other, border, diag_inverse, scen_rhs)
        head, tail = resident(
            edge_kernel, [shape(scen_local, size, rhs, kind=HALF)] * 2, 2, (), *args, *extra
        )
        ends = groups - 1
        before = lax.ppermute(tail, "fs", [(i, i + 1) for i in range(ends)])
        after = lax.ppermute(head, "fs", [(i + 1, i) for i in range(ends)])
        sides_shape = shape(scen_local, 2, size, rhs)
        dots_shape = shape(DOT_ROWS, rhs)
        args = (slots, sides, address, mine, other, border, diag_inverse, scen_rhs, diag_blocks, couplings)
        kernel = functools.partial(step_kernel, first=first)
        finish = functools.partial(finish_kernel, first=first)
        if first:
            out_shape = [fields, fields, dots_shape, shape(blocks, size, rhs)]
            step, image, dots, acc = resident(kernel, out_shape, 3, (), *args, factor)
            out_shape = [sides_shape, dots_shape] + [shape(half, size, rhs)] * 2
            scratch = (pltpu.VMEM((blocks, size, rhs), F32),)
            args = (address, image, before, after, couplings, scen_rhs, dots, factor, acc)
            side, dots, keep, send = resident(finish, out_shape, 1, scratch, *args)
            return step, image, side, dots, keep, send
        out_shape = [fields, sides_shape, sides_shape, dots_shape]
        step, left, image, dots = resident(kernel, out_shape, 3, (), *args, *extra)
        args = (address, image, before, after, couplings, left, dots)
        (dots,) = resident(finish, [dots_shape], 1, (), *args)
        return step, dots

    def resident(kernel, out_shape, tables, scratch, *args):
        vmem = pl.BlockSpec(memory_space=pltpu.VMEM)
        return pl.pallas_call(
            kernel,
            out_shape=out_shape,
            in_specs=[table()] * tables + [vmem] * (len(args) - tables),
            out_specs=[vmem] * len(out_shape),
            scratch_shapes=scratch,
            compiler_params=PLAIN,
            name=getattr(kernel, "func", kernel).__name__,
        )(*args)

    def small(kernel, out_shape, *args):
        return pl.pallas_call(
            kernel, out_shape=out_shape, compiler_params=PLAIN, name=kernel.__name__
        )(*args)

    tall = size + size // 2
    batch = 2

    def batch_block(*dims):
        return pl.BlockSpec((batch,) + dims, lambda s: (s,) + (0,) * len(dims))

    factor, keep, send = pl.pallas_call(
        prepare_kernel,
        out_shape=[shape(*scen_rhs.shape[:3], 3 * size, kind=HALF)] + [shape(half, tall, rhs)] * 2,
        grid=(scen_local // batch,),
        in_specs=[table(), batch_block(*field), batch_block(*tile), batch_block(*tile)],
        out_specs=[batch_block(window_local, size, 3 * size)] + [whole(half, tall, rhs)] * 2,
        scratch_shapes=[pltpu.VMEM((blocks, size, rhs + size), F32)],
        compiler_params=WIDE,
        name="prepare",
    )(address, scen_rhs, diag_inverse, border)
    arrived = spread_plane(keep + swap(send))
    guess_sum, weight, message = small(
        begin_kernel,
        [vector, shape(size // 2, 2 * size), shape(groups, size, rhs, kind=HALF)],
        arrived,
        first_res,
        first_diag,
    )
    arrived = solve(spread_fs(message), False)
    first_step, message = small(owned_kernel, [vector, shape(plane, size, rhs, kind=HALF)], arrived)
    scen_step, image, side, dots, keep, send = window_pass(message, None)
    arrived = spread_plane(keep + swap(send))
    turn, image_first, message = small(
        turn_kernel,
        [vector, vector, shape(groups, size + DOT_ROWS, rhs, kind=HALF)],
        arrived,
        first_step,
        guess_sum,
        weight,
        first_res,
        dots,
    )
    arrived = solve(spread_fs(message), True)
    step_size, next_step, message = small(
        next_kernel, [shape(8, rhs), vector, shape(plane, size, rhs, kind=HALF)], arrived, first_step
    )
    later_step, dots = window_pass(message, (image, side, step_size))
    next_image, first_left, both = small(
        ending_kernel,
        [vector, vector, shape(2, rhs)],
        step_size,
        next_step,
        guess_sum,
        turn,
        weight,
        first_res,
        image_first,
        dots,
    )
    both = both + swap(both)
    message = jnp.broadcast_to(both[None], (plane * groups, 2, rhs))
    arrived = lax.all_to_all(message, ("x", "y", "fs"), 0, 0)
    vmem = pl.BlockSpec(memory_space=pltpu.VMEM)
    scen_sol, first_sol, first_left = pl.pallas_call(
        final_kernel,
        out_shape=[fields, vector, vector],
        grid=(scen_local // batch,),
        in_specs=[vmem] * 8,
        out_specs=[batch_block(*field), whole(size, rhs), whole(size, rhs)],
        scratch_shapes=[pltpu.VMEM((8, rhs), F32)],
        compiler_params=PARAMS,
        name="final",
    )(arrived, step_size, scen_step, later_step, first_step, next_step, first_left, next_image)
    return (scen_sol, first_sol.reshape(1, size, rhs), first_left.reshape(1, size, rhs))


def solution(mesh):
    groups = mesh.shape["fs"]
    grid = Mesh(
        mesh.devices.reshape(CHIP_X, CHIP_Y, CORES, groups), ("x", "y", "core", "fs")
    )
    return jax.shard_map(
        per_device,
        mesh=grid,
        in_specs=(
            P(SCEN, "fs", None, None),
            P("fs", SCEN, None),
            P(SCEN, "fs", None, None),
            P(SCEN, "fs", None, None),
            P(SCEN, "fs", None, None, None),
            P(SCEN, "fs", None, None),
            P(SCEN, "fs"),
            P("fs", SCEN),
            P(None, SCEN, "fs", None),
        ),
        out_specs=(
            P(SCEN, "fs", None, None),
            P("fs", SCEN, None),
            P("fs", SCEN, None),
        ),
        check_vma=False,
    )
```

```python
import functools

import jax
import jax.numpy as jnp
from jax import lax
from jax.experimental import pallas as pl
from jax.experimental.pallas import tpu as pltpu
from jax.sharding import Mesh
from jax.sharding import PartitionSpec as P

CHIP_X = 4
CHIP_Y = 4
CORES = 2
PLANE = ("x", "y")
SCEN = ("x", "y", "core")
SWAP = [(0, 1), (1, 0)]
F32 = jnp.float32
HALF = jnp.bfloat16
DOT_ROWS = 16
BATCH = 2
EXACT = lax.Precision.HIGHEST
PARAMS = pltpu.CompilerParams(
    dimension_semantics=("arbitrary",), vmem_limit_bytes=24 * 1024 * 1024
)
PLAIN = pltpu.CompilerParams(vmem_limit_bytes=16 * 1024 * 1024)


def split(values):
    high = values.astype(HALF)
    return high, (values - high.astype(F32)).astype(HALF)


def dot(left, right):
    return jnp.dot(left, right, preferred_element_type=F32)


def dot_t(left, right):
    return lax.dot_general(left, right, (((0,), (0,)), ((), ())), preferred_element_type=F32)


def wide2(pieces):
    return jnp.concatenate([pieces[0], pieces[1]], axis=1)


def wide3(pieces):
    return jnp.concatenate([pieces[0], pieces[0], pieces[1]], axis=1)


def tall2(pieces):
    return jnp.concatenate([pieces[0], pieces[1]], axis=0)


def tall3(pieces):
    return jnp.concatenate([pieces[0], pieces[1], pieces[0]], axis=0)


def pieces_of(vectors):
    rows = []
    for vector in vectors:
        high = vector.astype(HALF).astype(F32)
        rest = vector - high
        mid = rest.astype(HALF).astype(F32)
        rows += [high, mid, rest - mid]
    return stack_rows(rows)


def stack_rows(rows):
    width = rows[0].shape[-1]
    place = lax.broadcasted_iota(jnp.int32, (DOT_ROWS, width), 0)
    total = jnp.zeros((DOT_ROWS, width), F32)
    for index, row in enumerate(rows):
        total = jnp.where(place == index, jnp.broadcast_to(row, (DOT_ROWS, width)), total)
    return total


def join_pieces(rows):
    return rows[0:1] + rows[1:2] + rows[2:3], rows[3:4] + rows[4:5] + rows[5:6]


def fold(values):
    return jnp.sum(values.reshape(values.shape[0] // 8, 8, values.shape[1]), axis=0)


def first_block(*shape):
    return pl.BlockSpec((1,) + shape, lambda s, *_: (s,) + (0,) * len(shape))


def whole(*shape):
    return pl.BlockSpec(shape, lambda *_: (0,) * len(shape))


def table():
    return pl.BlockSpec(memory_space=pltpu.SMEM)


def place(block_ref, core_ref, s, w):
    block = block_ref[s, w]
    return block >> 1, jnp.bitwise_xor(block & 1, core_ref[0])


def address(block_ref, core_ref, half, s, w):
    slot, side = place(block_ref, core_ref, s, w)
    return side * half + slot


def prepare_kernel(
    core_ref, block_ref, res_hbm, inv_hbm, border_hbm, factor_ref, keep_ref, send_ref, res_ref, inv_ref, border_ref, acc, sem
):
    scens, windows, size, rhs = res_ref.shape
    half = keep_ref.shape[0]
    batches = scens // BATCH
    pairs = ((res_hbm, res_ref), (inv_hbm, inv_ref), (border_hbm, border_ref))

    def copies(batch):
        part = pl.ds(batch * BATCH, BATCH)
        return [
            pltpu.make_async_copy(source.at[part], target.at[part], sem.at[batch, index])
            for index, (source, target) in enumerate(pairs)
        ]

    for batch in range(batches):
        for copy in copies(batch):
            copy.start()
    acc[...] = jnp.zeros_like(acc)

    def body(batch, carry):
        for copy in copies(batch):
            copy.wait()
        spots = [(batch * BATCH + s, w) for s in range(BATCH) for w in range(windows)]
        tiles = [split(border_ref[s, w]) for s, w in spots]
        products = []
        for (s, w), tile in zip(spots, tiles):
            inverse = inv_ref[s, w]
            products.append(dot_t(tall2(tile), tall2((inverse, inverse))))
        terms = []
        for (s, w), tile, product in zip(spots, tiles, products):
            factor = wide3(split(product))
            factor_ref[s, w] = factor
            right = jnp.concatenate([tall3(split(res_ref[s, w])), tall3(tile)], axis=1)
            terms.append(dot(factor, right))
        for (s, w), term in zip(spots, terms):
            acc[address(block_ref, core_ref, half, s, w)] += term
        return carry

    lax.fori_loop(0, batches, body, 0)
    for start, out in ((0, keep_ref), (half, send_ref)):
        out[:, 0:size, :] = acc[start : start + half, :, 0:rhs]
        out[:, size:, 0:size] = acc[start : start + half, 0 : size // 2, rhs : rhs + size]
        out[:, size:, size:] = acc[start : start + half, size // 2 :, rhs : rhs + size]


def begin_kernel(arrived_ref, first_ref, diag_ref, sum_ref, weight_ref, message_ref):
    size = first_ref.shape[0]
    total = jnp.sum(arrived_ref[...], axis=0)
    summed = total[:size]
    sum_ref[...] = summed
    side = size // 2
    diag = jnp.concatenate([diag_ref[...], diag_ref[...]], axis=1)
    row = lax.broadcasted_iota(jnp.int32, (side, 2 * size), 0)
    lane = lax.broadcasted_iota(jnp.int32, (side, 2 * size), 1)
    spot = jnp.logical_or(lane == row, lane == row + side + size)
    weight_ref[...] = total[size:] + jnp.where(spot, jnp.broadcast_to(diag, (side, 2 * size)), 0.0)
    message = (first_ref[...] + summed).astype(HALF)
    message_ref[...] = jnp.broadcast_to(message[None], message_ref.shape)


def solve_kernel(core_ref, arrived_ref, schur_ref, mine_ref, theirs_ref, *rest, with_dots):
    groups, _, rhs = arrived_ref.shape
    size = mine_ref.shape[1]
    tile = pl.program_id(0)
    per_tile = schur_ref.shape[1] // size
    operand = rest[-1]

    @pl.when(tile == 0)
    def _():
        for g in range(groups):
            operand[g * size : (g + 1) * size, :] = arrived_ref[g, 0:size, :]
        if with_dots:
            rows = jnp.sum(arrived_ref[:, size:, :].astype(F32), axis=0)
            dots = stack_rows(list(join_pieces(rows)))
            rest[0][...] = dots
            theirs_ref[theirs_ref.shape[0] - 1, 0:DOT_ROWS, :] = dots

    value = dot_t(schur_ref[...], operand[...])
    for pair in range(per_tile // CORES):
        even = value[(2 * pair) * size : (2 * pair + 1) * size]
        odd = value[(2 * pair + 1) * size : (2 * pair + 2) * size]
        slot = tile * (per_tile // CORES) + pair

        @pl.when(core_ref[0] == 0)
        def _():
            mine_ref[slot] = even
            theirs_ref[slot] = odd

        @pl.when(core_ref[0] != 0)
        def _():
            mine_ref[slot] = odd
            theirs_ref[slot] = even


def pair_kernel(mine_ref, got_ref, *rest):
    message_ref = rest[-1]
    plane, size, rhs = mine_ref.shape
    message_ref[:, 0:size, :] = (mine_ref[...] + got_ref[0:plane]).astype(HALF)
    if len(rest) > 1:
        dots = rest[0][...] + got_ref[plane, 0:DOT_ROWS, :]
        pieces = pieces_of([dots[0:1], dots[1:2]]).astype(HALF)
        message_ref[:, size:, :] = jnp.broadcast_to(pieces[None], (plane,) + pieces.shape)


def owned_kernel(arrived_ref, step_ref, message_ref):
    total = jnp.sum(arrived_ref[...].astype(F32), axis=0).astype(HALF)
    step_ref[...] = total.astype(F32)
    message_ref[...] = jnp.broadcast_to(total[None], message_ref.shape)


def residual(res_ref, last, s, w):
    if last is None:
        return res_ref[s, w]
    image_ref, side_ref, size_ref = last
    windows = res_ref.shape[1]
    if w == 0:
        image = side_ref[s, 0]
    elif w == windows - 1:
        image = side_ref[s, 1]
    else:
        image = image_ref[s, w]
    return res_ref[s, w] - size_ref[0:1] * image


def window_steps(tables, mine_ref, other_ref, border_ref, inv_ref, spots, values):
    core_ref, block_ref = tables
    tiles, blocks, lifts = [], [], []
    for s, w in spots:
        slot, side = place(block_ref, core_ref, s, w)
        mine = mine_ref[slot].astype(F32)
        other = other_ref[slot].astype(F32)
        block = jnp.where(side == 0, mine, other).astype(HALF)
        tiles.append(wide2(split(border_ref[s, w])))
        blocks.append(tall2((block, block)))
        lifts.append(dot(tiles[-1], blocks[-1]))
    steps = []
    for (s, w), res, lift in zip(spots, values, lifts):
        inverse = inv_ref[s, w]
        steps.append(dot(wide2((inverse, inverse)), tall2(split(res - lift))))
    return steps, tiles, blocks


def edge_kernel(core_ref, block_ref, mine_ref, other_ref, border_ref, inv_ref, res_ref, *rest):
    head_ref, tail_ref = rest[-2:]
    last = rest[:3] if len(rest) > 2 else None
    scens, windows = res_ref.shape[:2]
    tables = (core_ref, block_ref)
    spots = [(s, w) for s in range(scens) for w in (0, windows - 1)]
    values = [residual(res_ref, last, s, w) for s, w in spots]
    steps, _, _ = window_steps(tables, mine_ref, other_ref, border_ref, inv_ref, spots, values)
    for (s, w), step in zip(spots, steps):
        out = head_ref if w == 0 else tail_ref
        out[s] = step.astype(HALF)


def step_kernel(
    core_ref, block_ref, mine_ref, other_ref, border_ref, inv_ref, res_ref, diag_ref, pair_ref, *rest, first
):
    scens, windows, size, rhs = res_ref.shape
    if first:
        factor_ref, step_ref, image_ref, dots_ref, acc_ref = rest
        last = None
        acc_ref[...] = jnp.zeros_like(acc_ref)
    else:
        last = rest[:3]
        step_ref, left_ref, image_ref, dots_ref = rest[3:]
    tables = (core_ref, block_ref)

    def body(step, totals):
        along, energy = totals
        spots = [(step * BATCH + s, w) for s in range(BATCH) for w in range(windows)]
        left = [residual(res_ref, last, s, w) for s, w in spots]
        found, tiles, blocks = window_steps(tables, mine_ref, other_ref, border_ref, inv_ref, spots, left)
        steps = []
        for (s, w), value in zip(spots, found):
            step_ref[s, w] = value
            steps.append(tall3(split(value)))
        images = []
        for at, (s, w) in enumerate(spots):
            mats = [tiles[at], wide3(split(diag_ref[s, w]))]
            values = [blocks[at], steps[at]]
            if w > 0:
                mats.append(wide3(split(pair_ref[s, w, 0])))
                values.append(steps[at - 1])
            if w < windows - 1:
                mats.append(wide3(split(pair_ref[s, w, 1])))
                values.append(steps[at + 1])
            images.append(dot(jnp.concatenate(mats, axis=1), jnp.concatenate(values, axis=0)))
        terms = []
        for (s, w), res, image in zip(spots, left, images):
            inner = 0 < w < windows - 1
            if inner:
                along += fold(res * image)
                energy += fold(image * image)
            if first:
                image_ref[s, w] = image
                if inner:
                    terms.append((s, w, dot(factor_ref[s, w], tall3(split(image)))))
            elif not inner:
                spot = 0 if w == 0 else 1
                image_ref[s, spot] = image
                left_ref[s, spot] = res
        for s, w, term in terms:
            acc_ref[address(block_ref, core_ref, acc_ref.shape[0] // CORES, s, w)] += term
        return along, energy

    zero = jnp.zeros((8, rhs), F32)
    along, energy = lax.fori_loop(0, scens // BATCH, body, (zero, zero))
    dots_ref[0:8, :] = along
    dots_ref[8:16, :] = energy


def finish_kernel(core_ref, block_ref, image_ref, before_ref, after_ref, pair_ref, res_ref, dots_ref, *rest, first):
    scens, windows, _, size, _ = pair_ref.shape
    rhs = before_ref.shape[2]
    if first:
        factor_ref, acc_ref, side_ref, out_ref, keep_ref, send_ref, acc = rest
        acc[...] = acc_ref[...]
    else:
        (out_ref,) = rest
    along = jnp.zeros((8, rhs), F32)
    energy = jnp.zeros((8, rhs), F32)
    terms = []
    spots = [(s, spot) for s in range(scens) for spot in (0, 1)]
    halos = []
    for s, spot in spots:
        w = (windows - 1) * spot
        halo = (before_ref, after_ref)[spot][s]
        halos.append(dot(wide2(split(pair_ref[s, w, spot])), tall2((halo, halo))))
    for (s, spot), halo in zip(spots, halos):
        w = (windows - 1) * spot
        at = w if first else spot
        image = halo + image_ref[s, at]
        along += fold(res_ref[s, at] * image)
        energy += fold(image * image)
        if first:
            side_ref[s, spot] = image
            terms.append((s, w, dot(factor_ref[s, w], tall3(split(image)))))
    out_ref[0:8, :] = dots_ref[0:8, :] + along
    out_ref[8:16, :] = dots_ref[8:16, :] + energy
    if first:
        half = keep_ref.shape[0]
        for s, w, term in terms:
            acc[address(block_ref, core_ref, half, s, w)] += term
        keep_ref[...] = acc[0:half]
        send_ref[...] = acc[half:]


def first_image(weight, step, summed):
    size = step.shape[0]
    top = jnp.dot(weight[:, :size], step, precision=EXACT, preferred_element_type=F32)
    low = jnp.dot(weight[:, size:], step, precision=EXACT, preferred_element_type=F32)
    return jnp.concatenate([top, low], axis=0) - summed


def local_dots(dots, res, image):
    along = jnp.sum(dots[0:8] + fold(res * image), axis=0, keepdims=True)
    energy = jnp.sum(dots[8:16] + fold(image * image), axis=0, keepdims=True)
    return along, energy


def turn_kernel(arrived_ref, step_ref, sum_ref, weight_ref, first_ref, dots_ref, turn_ref, image_ref, message_ref):
    size = step_ref.shape[0]
    turn = jnp.sum(arrived_ref[...], axis=0)
    image = first_image(weight_ref[...], step_ref[...], sum_ref[...])
    turn_ref[...] = turn
    image_ref[...] = image
    change = (first_ref[...] + sum_ref[...]) - (image + turn)
    pieces = pieces_of(local_dots(dots_ref[...], first_ref[...], image)).astype(HALF)
    message = jnp.concatenate([change.astype(HALF), pieces], axis=0)
    message_ref[...] = jnp.broadcast_to(message[None], message_ref.shape)


def next_kernel(arrived_ref, step_ref, size_ref, next_ref, message_ref):
    rows = step_ref.shape[0]
    total = jnp.sum(arrived_ref[...].astype(F32), axis=0)
    along, energy = join_pieces(total[rows:])
    size = along / (energy + 1e-06)
    size_ref[...] = jnp.broadcast_to(size, size_ref.shape)
    step = ((1.0 - size) * step_ref[...] + size * total[:rows]).astype(HALF)
    next_ref[...] = step.astype(F32)
    message_ref[...] = jnp.broadcast_to(step[None], message_ref.shape)


def ending_kernel(
    size_ref, step_ref, sum_ref, turn_ref, weight_ref, first_ref, image_ref, dots_ref, next_ref, res_ref, out_ref
):
    size = size_ref[0:1]
    image = first_image(weight_ref[...], step_ref[...], sum_ref[...] - size * turn_ref[...])
    res = first_ref[...] - size * image_ref[...]
    next_ref[...] = image
    res_ref[...] = res
    along, energy = local_dots(dots_ref[...], res, image)
    row = lax.broadcasted_iota(jnp.int32, (2, along.shape[1]), 0)
    both = jnp.where(row == 0, jnp.broadcast_to(along, row.shape), jnp.broadcast_to(energy, row.shape))
    out_ref[...] = both


def final_kernel(
    arrived_ref, size_ref, step_ref, later_ref, first_ref, next_ref, res_ref, image_ref, sol_ref, head_ref, out_ref, later_size
):
    scen = pl.program_id(0)
    size = size_ref[0:1]

    @pl.when(scen == 0)
    def _():
        total = jnp.sum(arrived_ref[...], axis=0)
        later = total[0:1] / (total[1:2] + 1e-06)
        later_size[...] = jnp.broadcast_to(later, later_size.shape)
        head_ref[...] = size * first_ref[...] + later * next_ref[...]
        out_ref[...] = res_ref[...] - later * image_ref[...]

    scens = sol_ref.shape[0]
    for s in range(scens):
        at = scen * scens + s
        sol_ref[s] = size * step_ref[at] + later_size[0:1] * later_ref[at]


def shape(*dims, kind=F32):
    return jax.ShapeDtypeStruct(dims, kind)


def in_hbm(*arrays):
    return [pltpu.with_memory_space_constraint(array, pltpu.HBM) for array in arrays]


def per_device(
    scen_rhs,
    first_rhs,
    diag_blocks,
    diag_inverse,
    couplings,
    border,
    border_block,
    first_diag,
    schur_inverse,
):
    core = lax.axis_index("core").astype(jnp.int32)
    scen_local, window_local, size, rhs = scen_rhs.shape
    group_rows = schur_inverse.shape[-1]
    blocks = group_rows // size
    half = blocks // CORES
    groups = lax.axis_size("fs")
    plane = CHIP_X * CHIP_Y
    columns = schur_inverse.shape[0] * schur_inverse.shape[1]
    schur_flat = schur_inverse.reshape(columns, group_rows)
    first_res = first_rhs.reshape(size, rhs)
    core_table = core.reshape(1)
    field = (window_local, size, rhs)
    tile = (window_local, size, size)
    grid = (scen_local,)
    fields = shape(scen_local, *field)
    edges = shape(scen_local, size, rhs)
    vector = shape(size, rhs)

    def swap(values):
        return lax.ppermute(values, "core", SWAP)

    def spread_plane(values):
        return lax.all_to_all(values, PLANE, 0, 0)

    def spread_fs(values):
        return lax.all_to_all(values, "fs", 0, 0)

    def solve(arrived, with_dots):
        rows = arrived.shape[1]
        tiles = 4
        wide = group_rows // tiles
        extra = 1 if with_dots else 0
        out_shape = [shape(half, size, rhs), shape(half + extra, size, rhs)]
        if with_dots:
            out_shape.append(shape(DOT_ROWS, rhs))
        out = pl.pallas_call(
            functools.partial(solve_kernel, with_dots=with_dots),
            out_shape=out_shape,
            grid=(tiles,),
            in_specs=[table(), whole(groups, rows, rhs), pl.BlockSpec((columns, wide), lambda t: (0, t))],
            out_specs=[whole(*o.shape) for o in out_shape],
            scratch_shapes=[pltpu.VMEM((columns, rhs), HALF)],
            compiler_params=PARAMS,
            name="solve",
        )(core_table, arrived, schur_flat)
        got = swap(out[1])
        rows_out = size + (DOT_ROWS if with_dots else 0)
        message = pl.pallas_call(
            pair_kernel,
            out_shape=shape(plane, rows_out, rhs, kind=HALF),
            compiler_params=PLAIN,
            name="pair",
        )(out[0], got, *out[2:])
        return spread_plane(message)

    def window_pass(message, last):
        first = last is None
        mine = spread_plane(message)
        other = swap(mine)
        extra = () if first else last
        args = (core_table, border_block, mine, other, border, diag_inverse, scen_rhs)
        head, tail = resident(
            edge_kernel, [shape(scen_local, size, rhs, kind=HALF)] * 2, 2, (), *args, *extra
        )
        ends = groups - 1
        before = lax.ppermute(tail, "fs", [(i, i + 1) for i in range(ends)])
        after = lax.ppermute(head, "fs", [(i + 1, i) for i in range(ends)])
        sides_shape = shape(scen_local, 2, size, rhs)
        dots_shape = shape(DOT_ROWS, rhs)
        args = (core_table, border_block, mine, other, border, diag_inverse, scen_rhs, diag_blocks, couplings)
        kernel = functools.partial(step_kernel, first=first)
        finish = functools.partial(finish_kernel, first=first)
        if first:
            out_shape = [fields, fields, dots_shape, shape(blocks, size, rhs)]
            step, image, dots, acc = resident(kernel, out_shape, 2, (), *args, factor)
            out_shape = [sides_shape, dots_shape] + [shape(half, size, rhs)] * 2
            scratch = (pltpu.VMEM((blocks, size, rhs), F32),)
            args = (core_table, border_block, image, before, after, couplings, scen_rhs, dots, factor, acc)
            side, dots, keep, send = resident(finish, out_shape, 2, scratch, *args)
            return step, image, side, dots, keep, send
        out_shape = [fields, sides_shape, sides_shape, dots_shape]
        step, left, image, dots = resident(kernel, out_shape, 2, (), *args, *extra)
        args = (core_table, border_block, image, before, after, couplings, left, dots)
        (dots,) = resident(finish, [dots_shape], 2, (), *args)
        return step, dots

    def resident(kernel, out_shape, tables, scratch, *args):
        vmem = pl.BlockSpec(memory_space=pltpu.VMEM)
        return pl.pallas_call(
            kernel,
            out_shape=out_shape,
            in_specs=[table()] * tables + [vmem] * (len(args) - tables),
            out_specs=[vmem] * len(out_shape),
            scratch_shapes=scratch,
            compiler_params=PLAIN,
            name=getattr(kernel, "func", kernel).__name__,
        )(*args)

    def small(kernel, out_shape, *args):
        return pl.pallas_call(
            kernel, out_shape=out_shape, compiler_params=PLAIN, name=kernel.__name__
        )(*args)

    tall = size + size // 2

    def batch_block(*dims):
        return pl.BlockSpec((BATCH,) + dims, lambda s: (s,) + (0,) * len(dims))

    vmem = pl.BlockSpec(memory_space=pltpu.VMEM)
    factor, keep, send = pl.pallas_call(
        prepare_kernel,
        out_shape=[shape(*scen_rhs.shape[:3], 3 * size, kind=HALF)] + [shape(half, tall, rhs)] * 2,
        in_specs=[table()] * 2 + [pl.BlockSpec(memory_space=pltpu.HBM)] * 3,
        out_specs=[vmem] * 3,
        scratch_shapes=[
            pltpu.VMEM(scen_rhs.shape, F32),
            pltpu.VMEM(diag_inverse.shape, HALF),
            pltpu.VMEM(border.shape, F32),
            pltpu.VMEM((blocks, size, rhs + size), F32),
            pltpu.SemaphoreType.DMA((scen_local // BATCH, 3)),
        ],
        compiler_params=PLAIN,
        name="prepare",
    )(core_table, *in_hbm(border_block, scen_rhs, diag_inverse, border))
    arrived = spread_plane(keep + swap(send))
    guess_sum, weight, message = small(
        begin_kernel,
        [vector, shape(size // 2, 2 * size), shape(groups, size, rhs, kind=HALF)],
        arrived,
        first_res,
        first_diag,
    )
    arrived = solve(spread_fs(message), False)
    first_step, message = small(owned_kernel, [vector, shape(plane, size, rhs, kind=HALF)], arrived)
    scen_step, image, side, dots, keep, send = window_pass(message, None)
    arrived = spread_plane(keep + swap(send))
    turn, image_first, message = small(
        turn_kernel,
        [vector, vector, shape(groups, size + DOT_ROWS, rhs, kind=HALF)],
        arrived,
        first_step,
        guess_sum,
        weight,
        first_res,
        dots,
    )
    arrived = solve(spread_fs(message), True)
    step_size, next_step, message = small(
        next_kernel, [shape(8, rhs), vector, shape(plane, size, rhs, kind=HALF)], arrived, first_step
    )
    later_step, dots = window_pass(message, (image, side, step_size))
    next_image, first_left, both = small(
        ending_kernel,
        [vector, vector, shape(2, rhs)],
        step_size,
        next_step,
        guess_sum,
        turn,
        weight,
        first_res,
        image_first,
        dots,
    )
    both = both + swap(both)
    message = jnp.broadcast_to(both[None], (plane * groups, 2, rhs))
    arrived = lax.all_to_all(message, ("x", "y", "fs"), 0, 0)
    scen_sol, first_sol, first_left = pl.pallas_call(
        final_kernel,
        out_shape=[fields, vector, vector],
        grid=(scen_local // BATCH,),
        in_specs=[vmem] * 8,
        out_specs=[batch_block(*field), whole(size, rhs), whole(size, rhs)],
        scratch_shapes=[pltpu.VMEM((8, rhs), F32)],
        compiler_params=PARAMS,
        name="final",
    )(arrived, step_size, scen_step, later_step, first_step, next_step, first_left, next_image)
    return (scen_sol, first_sol.reshape(1, size, rhs), first_left.reshape(1, size, rhs))


def solution(mesh):
    groups = mesh.shape["fs"]
    grid = Mesh(
        mesh.devices.reshape(CHIP_X, CHIP_Y, CORES, groups), ("x", "y", "core", "fs")
    )
    return jax.shard_map(
        per_device,
        mesh=grid,
        in_specs=(
            P(SCEN, "fs", None, None),
            P("fs", SCEN, None),
            P(SCEN, "fs", None, None),
            P(SCEN, "fs", None, None),
            P(SCEN, "fs", None, None, None),
            P(SCEN, "fs", None, None),
            P(SCEN, "fs"),
            P("fs", SCEN),
            P(None, SCEN, "fs", None),
        ),
        out_specs=(
            P(SCEN, "fs", None, None),
            P("fs", SCEN, None),
            P("fs", SCEN, None),
        ),
        check_vma=False,
    )
```

```python
import functools

import jax
import jax.numpy as jnp
from jax import lax
from jax.experimental import pallas as pl
from jax.experimental.pallas import tpu as pltpu
from jax.sharding import Mesh
from jax.sharding import PartitionSpec as P

CHIP_X = 4
CHIP_Y = 4
CORES = 2
PLANE = ("x", "y")
SCEN = ("x", "y", "core")
SWAP = [(0, 1), (1, 0)]
F32 = jnp.float32
HALF = jnp.bfloat16
DOT_ROWS = 16
BATCH = 2
STEP_BATCH = 4
TILE_BLOCKS = 8
EXACT = lax.Precision.HIGHEST
PARAMS = pltpu.CompilerParams(
    dimension_semantics=("arbitrary",), vmem_limit_bytes=24 * 1024 * 1024
)
PLAIN = pltpu.CompilerParams(vmem_limit_bytes=16 * 1024 * 1024)


def split(values):
    high = values.astype(HALF)
    return high, (values - high.astype(F32)).astype(HALF)


def dot(left, right):
    return jnp.dot(left, right, preferred_element_type=F32)


def dot_t(left, right):
    return lax.dot_general(left, right, (((0,), (0,)), ((), ())), preferred_element_type=F32)


def wide2(pieces):
    return jnp.concatenate([pieces[0], pieces[1]], axis=1)


def wide3(pieces):
    return jnp.concatenate([pieces[0], pieces[0], pieces[1]], axis=1)


def tall2(pieces):
    return jnp.concatenate([pieces[0], pieces[1]], axis=0)


def tall3(pieces):
    return jnp.concatenate([pieces[0], pieces[1], pieces[0]], axis=0)


def pieces_of(vectors):
    rows = []
    for vector in vectors:
        high = vector.astype(HALF).astype(F32)
        rest = vector - high
        mid = rest.astype(HALF).astype(F32)
        rows += [high, mid, rest - mid]
    return stack_rows(rows)


def stack_rows(rows):
    width = rows[0].shape[-1]
    place = lax.broadcasted_iota(jnp.int32, (DOT_ROWS, width), 0)
    total = jnp.zeros((DOT_ROWS, width), F32)
    for index, row in enumerate(rows):
        total = jnp.where(place == index, jnp.broadcast_to(row, (DOT_ROWS, width)), total)
    return total


def join_pieces(rows):
    return rows[0:1] + rows[1:2] + rows[2:3], rows[3:4] + rows[4:5] + rows[5:6]


def fold(values):
    return jnp.sum(values.reshape(values.shape[0] // 8, 8, values.shape[1]), axis=0)


def first_block(*shape):
    return pl.BlockSpec((1,) + shape, lambda s, *_: (s,) + (0,) * len(shape))


def whole(*shape):
    return pl.BlockSpec(shape, lambda *_: (0,) * len(shape))


def table():
    return pl.BlockSpec(memory_space=pltpu.SMEM)


def place(block_ref, core_ref, s, w):
    block = block_ref[s, w]
    return block >> 1, jnp.bitwise_xor(block & 1, core_ref[0])


def address(block_ref, core_ref, half, s, w):
    slot, side = place(block_ref, core_ref, s, w)
    return side * half + slot


def prepare_kernel(
    core_ref, block_ref, res_hbm, inv_hbm, border_hbm, factor_ref, keep_ref, send_ref, res_ref, inv_ref, border_ref, acc, sem
):
    scens, windows, size, rhs = res_ref.shape
    half = keep_ref.shape[0]
    batches = scens // BATCH
    pairs = ((res_hbm, res_ref), (inv_hbm, inv_ref), (border_hbm, border_ref))

    def copies(batch):
        part = pl.ds(batch * BATCH, BATCH)
        return [
            pltpu.make_async_copy(source.at[part], target.at[part], sem.at[batch, index])
            for index, (source, target) in enumerate(pairs)
        ]

    for batch in range(batches):
        for copy in copies(batch):
            copy.start()
    acc[...] = jnp.zeros_like(acc)

    def body(batch, carry):
        for copy in copies(batch):
            copy.wait()
        spots = [(batch * BATCH + s, w) for s in range(BATCH) for w in range(windows)]
        tiles = [split(border_ref[s, w]) for s, w in spots]
        products = []
        for (s, w), tile in zip(spots, tiles):
            inverse = inv_ref[s, w]
            products.append(dot_t(tall2(tile), tall2((inverse, inverse))))
        terms = []
        for (s, w), tile, product in zip(spots, tiles, products):
            factor = wide3(split(product))
            factor_ref[s, w] = factor
            right = jnp.concatenate([tall3(split(res_ref[s, w])), tall3(tile)], axis=1)
            terms.append(dot(factor, right))
        for (s, w), term in zip(spots, terms):
            acc[address(block_ref, core_ref, half, s, w)] += term
        return carry

    lax.fori_loop(0, batches, body, 0)
    for start, out in ((0, keep_ref), (half, send_ref)):
        out[:, 0:size, :] = acc[start : start + half, :, 0:rhs]
        out[:, size:, 0:size] = acc[start : start + half, 0 : size // 2, rhs : rhs + size]
        out[:, size:, size:] = acc[start : start + half, size // 2 :, rhs : rhs + size]


def begin_kernel(arrived_ref, first_ref, diag_ref, sum_ref, weight_ref, message_ref):
    size = first_ref.shape[0]
    total = jnp.sum(arrived_ref[...], axis=0)
    summed = total[:size]
    sum_ref[...] = summed
    side = size // 2
    diag = jnp.concatenate([diag_ref[...], diag_ref[...]], axis=1)
    row = lax.broadcasted_iota(jnp.int32, (side, 2 * size), 0)
    lane = lax.broadcasted_iota(jnp.int32, (side, 2 * size), 1)
    spot = jnp.logical_or(lane == row, lane == row + side + size)
    weight_ref[...] = total[size:] + jnp.where(spot, jnp.broadcast_to(diag, (side, 2 * size)), 0.0)
    message = (first_ref[...] + summed).astype(HALF)
    message_ref[...] = jnp.broadcast_to(message[None], message_ref.shape)


def solve_kernel(core_ref, arrived_ref, schur_ref, mine_ref, theirs_ref, *rest, with_dots):
    groups = arrived_ref.shape[0]
    size = mine_ref.shape[1]
    wide = TILE_BLOCKS * size
    operand = jnp.concatenate([arrived_ref[g, 0:size, :] for g in range(groups)], axis=0)
    if with_dots:
        rows = jnp.sum(arrived_ref[:, size:, :].astype(F32), axis=0)
        dots = stack_rows(list(join_pieces(rows)))
        rest[0][...] = dots
        theirs_ref[theirs_ref.shape[0] - 1, 0:DOT_ROWS, :] = dots
    flipped = operand.T
    values = []
    for tile in range(schur_ref.shape[1] // wide):
        values.append(dot(flipped, schur_ref[:, tile * wide : (tile + 1) * wide]).T)

    def write(evens_ref, odds_ref):
        for tile, value in enumerate(values):
            for pair in range(TILE_BLOCKS // CORES):
                slot = tile * (TILE_BLOCKS // CORES) + pair
                evens_ref[slot] = value[(2 * pair) * size : (2 * pair + 1) * size]
                odds_ref[slot] = value[(2 * pair + 1) * size : (2 * pair + 2) * size]

    @pl.when(core_ref[0] == 0)
    def _():
        write(mine_ref, theirs_ref)

    @pl.when(core_ref[0] != 0)
    def _():
        write(theirs_ref, mine_ref)


def pair_kernel(mine_ref, got_ref, *rest):
    message_ref = rest[-1]
    plane, size, rhs = mine_ref.shape
    message_ref[:, 0:size, :] = (mine_ref[...] + got_ref[0:plane]).astype(HALF)
    if len(rest) > 1:
        dots = rest[0][...] + got_ref[plane, 0:DOT_ROWS, :]
        pieces = pieces_of([dots[0:1], dots[1:2]]).astype(HALF)
        message_ref[:, size:, :] = jnp.broadcast_to(pieces[None], (plane,) + pieces.shape)


def owned_kernel(arrived_ref, step_ref, message_ref):
    total = jnp.sum(arrived_ref[...].astype(F32), axis=0).astype(HALF)
    step_ref[...] = total.astype(F32)
    message_ref[...] = jnp.broadcast_to(total[None], message_ref.shape)


def residual(res_ref, last, s, w):
    if last is None:
        return res_ref[s, w]
    image_ref, side_ref, size_ref = last
    windows = res_ref.shape[1]
    if w == 0:
        image = side_ref[s, 0]
    elif w == windows - 1:
        image = side_ref[s, 1]
    else:
        image = image_ref[s, w]
    return res_ref[s, w] - size_ref[0:1] * image


def window_steps(tables, mine_ref, other_ref, border_ref, inv_ref, spots, values):
    core_ref, block_ref = tables
    lifts = []
    for s, w in spots:
        slot, side = place(block_ref, core_ref, s, w)
        mine = mine_ref[slot].astype(F32)
        other = other_ref[slot].astype(F32)
        block = jnp.where(side == 0, mine, other).astype(HALF)
        lifts.append(dot(wide2(split(border_ref[s, w])), tall2((block, block))))
    steps = []
    for (s, w), res, lift in zip(spots, values, lifts):
        inverse = inv_ref[s, w]
        steps.append(dot(wide2((inverse, inverse)), tall2(split(res - lift))))
    return steps


def edge_kernel(core_ref, block_ref, mine_ref, other_ref, border_ref, inv_ref, res_ref, *rest):
    head_ref, tail_ref = rest[-2:]
    last = rest[:3] if len(rest) > 2 else None
    scens, windows = res_ref.shape[:2]
    tables = (core_ref, block_ref)
    spots = [(s, w) for s in range(scens) for w in (0, windows - 1)]
    values = [residual(res_ref, last, s, w) for s, w in spots]
    steps = window_steps(tables, mine_ref, other_ref, border_ref, inv_ref, spots, values)
    for (s, w), step in zip(spots, steps):
        out = head_ref if w == 0 else tail_ref
        out[s] = step.astype(HALF)


def step_kernel(core_ref, block_ref, mine_ref, other_ref, border_ref, inv_ref, res_ref, diag_ref, pair_ref, *rest, first):
    scens, windows, size, rhs = res_ref.shape
    if first:
        factor_ref, step_ref, image_ref, dots_ref, acc_ref, pack_ref = rest
        last = None
        acc_ref[...] = jnp.zeros_like(acc_ref)
    else:
        last = rest[:3]
        pack_ref, step_ref, left_ref, image_ref, dots_ref = rest[3:]
    nothing = jnp.zeros((size, rhs), HALF)
    side = 2 * size

    def body(batch, totals):
        along, energy = totals
        spots = [(batch * STEP_BATCH + s, w) for s in range(STEP_BATCH) for w in range(windows)]
        left = [residual(res_ref, last, s, w) for s, w in spots]
        packs, blocks, lifts = [], [], []
        for s, w in spots:
            slot, core_side = place(block_ref, core_ref, s, w)
            mine = mine_ref[slot].astype(F32)
            other = other_ref[slot].astype(F32)
            block = jnp.where(core_side == 0, mine, other).astype(HALF)
            if first:
                one = split(jnp.concatenate([pair_ref[s, w, 0], diag_ref[s, w]], axis=1))
                two = split(jnp.concatenate([pair_ref[s, w, 1], border_ref[s, w]], axis=1))
                pack = [one[0], two[0], one[1], two[1]]
                for part in range(4):
                    pack_ref[s, w, :, part * side : (part + 1) * side] = pack[part]
            else:
                pack = [pack_ref[s, w, :, part * side : (part + 1) * side] for part in range(4)]
            packs.append(pack)
            blocks.append(block)
            lifts.append(dot(wide2((pack[1], pack[3])), jnp.concatenate([nothing, block] * 2, axis=0)))
        found = []
        for (s, w), res, lift in zip(spots, left, lifts):
            inverse = inv_ref[s, w]
            found.append(dot(wide2((inverse, inverse)), tall2(split(res - lift))))
        steps = []
        for (s, w), value in zip(spots, found):
            step_ref[s, w] = value
            steps.append(split(value))
        images = []
        for at, (s, w) in enumerate(spots):
            before = steps[at - 1] if w > 0 else (nothing, nothing)
            after = steps[at + 1] if w < windows - 1 else (nothing, nothing)
            high = [before[0], steps[at][0], after[0], blocks[at]]
            low = [before[1], steps[at][1], after[1], nothing]
            one_high, two_high, one_low, two_low = packs[at]
            mats = [one_high, two_high, one_high, two_high, one_low, two_low]
            images.append(dot(jnp.concatenate(mats, axis=1), jnp.concatenate(high + low + high, axis=0)))
        terms = []
        for (s, w), res, image in zip(spots, left, images):
            inner = 0 < w < windows - 1
            if inner:
                along += fold(res * image)
                energy += fold(image * image)
            if first:
                image_ref[s, w] = image
                if inner:
                    terms.append((s, w, dot(factor_ref[s, w], tall3(split(image)))))
            elif not inner:
                spot = 0 if w == 0 else 1
                image_ref[s, spot] = image
                left_ref[s, spot] = res
        for s, w, term in terms:
            acc_ref[address(block_ref, core_ref, acc_ref.shape[0] // CORES, s, w)] += term
        return along, energy

    zero = jnp.zeros((8, rhs), F32)
    along, energy = lax.fori_loop(0, scens // STEP_BATCH, body, (zero, zero))
    dots_ref[0:8, :] = along
    dots_ref[8:16, :] = energy


def finish_kernel(core_ref, block_ref, image_ref, before_ref, after_ref, pair_ref, res_ref, dots_ref, *rest, first):
    scens, windows, _, size, _ = pair_ref.shape
    rhs = before_ref.shape[2]
    if first:
        factor_ref, acc_ref, side_ref, out_ref, keep_ref, send_ref, acc = rest
        acc[...] = acc_ref[...]
    else:
        (out_ref,) = rest
    along = jnp.zeros((8, rhs), F32)
    energy = jnp.zeros((8, rhs), F32)
    terms = []
    spots = [(s, spot) for s in range(scens) for spot in (0, 1)]
    halos = []
    for s, spot in spots:
        w = (windows - 1) * spot
        halo = (before_ref, after_ref)[spot][s]
        halos.append(dot(wide2(split(pair_ref[s, w, spot])), tall2((halo, halo))))
    for (s, spot), halo in zip(spots, halos):
        w = (windows - 1) * spot
        at = w if first else spot
        image = halo + image_ref[s, at]
        along += fold(res_ref[s, at] * image)
        energy += fold(image * image)
        if first:
            side_ref[s, spot] = image
            terms.append((s, w, dot(factor_ref[s, w], tall3(split(image)))))
    out_ref[0:8, :] = dots_ref[0:8, :] + along
    out_ref[8:16, :] = dots_ref[8:16, :] + energy
    if first:
        half = keep_ref.shape[0]
        for s, w, term in terms:
            acc[address(block_ref, core_ref, half, s, w)] += term
        keep_ref[...] = acc[0:half]
        send_ref[...] = acc[half:]


def first_image(weight, step, summed):
    size = step.shape[0]
    top = jnp.dot(weight[:, :size], step, precision=EXACT, preferred_element_type=F32)
    low = jnp.dot(weight[:, size:], step, precision=EXACT, preferred_element_type=F32)
    return jnp.concatenate([top, low], axis=0) - summed


def local_dots(dots, res, image):
    along = jnp.sum(dots[0:8] + fold(res * image), axis=0, keepdims=True)
    energy = jnp.sum(dots[8:16] + fold(image * image), axis=0, keepdims=True)
    return along, energy


def turn_kernel(arrived_ref, step_ref, sum_ref, weight_ref, first_ref, dots_ref, turn_ref, image_ref, message_ref):
    size = step_ref.shape[0]
    turn = jnp.sum(arrived_ref[...], axis=0)
    image = first_image(weight_ref[...], step_ref[...], sum_ref[...])
    turn_ref[...] = turn
    image_ref[...] = image
    change = (first_ref[...] + sum_ref[...]) - (image + turn)
    pieces = pieces_of(local_dots(dots_ref[...], first_ref[...], image)).astype(HALF)
    message = jnp.concatenate([change.astype(HALF), pieces], axis=0)
    message_ref[...] = jnp.broadcast_to(message[None], message_ref.shape)


def next_kernel(arrived_ref, step_ref, size_ref, next_ref, message_ref):
    rows = step_ref.shape[0]
    total = jnp.sum(arrived_ref[...].astype(F32), axis=0)
    along, energy = join_pieces(total[rows:])
    size = along / (energy + 1e-06)
    size_ref[...] = jnp.broadcast_to(size, size_ref.shape)
    step = ((1.0 - size) * step_ref[...] + size * total[:rows]).astype(HALF)
    next_ref[...] = step.astype(F32)
    message_ref[...] = jnp.broadcast_to(step[None], message_ref.shape)


def ending_kernel(
    size_ref, step_ref, sum_ref, turn_ref, weight_ref, first_ref, image_ref, dots_ref, next_ref, res_ref, out_ref
):
    size = size_ref[0:1]
    image = first_image(weight_ref[...], step_ref[...], sum_ref[...] - size * turn_ref[...])
    res = first_ref[...] - size * image_ref[...]
    next_ref[...] = image
    res_ref[...] = res
    along, energy = local_dots(dots_ref[...], res, image)
    row = lax.broadcasted_iota(jnp.int32, (2, along.shape[1]), 0)
    both = jnp.where(row == 0, jnp.broadcast_to(along, row.shape), jnp.broadcast_to(energy, row.shape))
    out_ref[...] = both


def final_kernel(
    arrived_ref, size_ref, step_ref, later_ref, first_ref, next_ref, res_ref, image_ref, sol_ref, head_ref, out_ref, later_size
):
    scen = pl.program_id(0)
    size = size_ref[0:1]

    @pl.when(scen == 0)
    def _():
        total = jnp.sum(arrived_ref[...], axis=0)
        later = total[0:1] / (total[1:2] + 1e-06)
        later_size[...] = jnp.broadcast_to(later, later_size.shape)
        head_ref[...] = size * first_ref[...] + later * next_ref[...]
        out_ref[...] = res_ref[...] - later * image_ref[...]

    scens = sol_ref.shape[0]
    for s in range(scens):
        at = scen * scens + s
        sol_ref[s] = size * step_ref[at] + later_size[0:1] * later_ref[at]


def shape(*dims, kind=F32):
    return jax.ShapeDtypeStruct(dims, kind)


def in_hbm(*arrays):
    return [pltpu.with_memory_space_constraint(array, pltpu.HBM) for array in arrays]


def per_device(
    scen_rhs,
    first_rhs,
    diag_blocks,
    diag_inverse,
    couplings,
    border,
    border_block,
    first_diag,
    schur_inverse,
):
    core = lax.axis_index("core").astype(jnp.int32)
    scen_local, window_local, size, rhs = scen_rhs.shape
    group_rows = schur_inverse.shape[-1]
    blocks = group_rows // size
    half = blocks // CORES
    groups = lax.axis_size("fs")
    plane = CHIP_X * CHIP_Y
    columns = schur_inverse.shape[0] * schur_inverse.shape[1]
    schur_flat = schur_inverse.reshape(columns, group_rows)
    first_res = first_rhs.reshape(size, rhs)
    core_table = core.reshape(1)
    field = (window_local, size, rhs)
    tile = (window_local, size, size)
    grid = (scen_local,)
    fields = shape(scen_local, *field)
    edges = shape(scen_local, size, rhs)
    vector = shape(size, rhs)

    def swap(values):
        return lax.ppermute(values, "core", SWAP)

    def spread_plane(values):
        return lax.all_to_all(values, PLANE, 0, 0)

    def spread_fs(values):
        return lax.all_to_all(values, "fs", 0, 0)

    def solve(arrived, with_dots):
        extra = 1 if with_dots else 0
        out_shape = [shape(half, size, rhs), shape(half + extra, size, rhs)]
        if with_dots:
            out_shape.append(shape(DOT_ROWS, rhs))
        kernel = functools.partial(solve_kernel, with_dots=with_dots)
        out = resident(kernel, out_shape, 1, (), core_table, arrived, schur_flat)
        got = swap(out[1])
        rows_out = size + (DOT_ROWS if with_dots else 0)
        message = pl.pallas_call(
            pair_kernel,
            out_shape=shape(plane, rows_out, rhs, kind=HALF),
            compiler_params=PLAIN,
            name="pair",
        )(out[0], got, *out[2:])
        return spread_plane(message)

    def window_pass(message, last, pack=None):
        first = last is None
        mine = spread_plane(message)
        other = swap(mine)
        extra = () if first else last
        args = (core_table, border_block, mine, other, border, diag_inverse, scen_rhs)
        head, tail = resident(
            edge_kernel, [shape(scen_local, size, rhs, kind=HALF)] * 2, 2, (), *args, *extra
        )
        ends = groups - 1
        before = lax.ppermute(tail, "fs", [(i, i + 1) for i in range(ends)])
        after = lax.ppermute(head, "fs", [(i + 1, i) for i in range(ends)])
        sides_shape = shape(scen_local, 2, size, rhs)
        dots_shape = shape(DOT_ROWS, rhs)
        args = (core_table, border_block, mine, other, border, diag_inverse, scen_rhs, diag_blocks, couplings)
        kernel = functools.partial(step_kernel, first=first)
        finish = functools.partial(finish_kernel, first=first)
        if first:
            out_shape = [fields, fields, dots_shape, shape(blocks, size, rhs)]
            out_shape.append(shape(*scen_rhs.shape[:3], 8 * size, kind=HALF))
            step, image, dots, acc, pack = resident(kernel, out_shape, 2, (), *args, factor)
            out_shape = [sides_shape, dots_shape] + [shape(half, size, rhs)] * 2
            scratch = (pltpu.VMEM((blocks, size, rhs), F32),)
            args = (core_table, border_block, image, before, after, couplings, scen_rhs, dots, factor, acc)
            side, dots, keep, send = resident(finish, out_shape, 2, scratch, *args)
            return step, image, side, dots, keep, send, pack
        out_shape = [fields, sides_shape, sides_shape, dots_shape]
        step, left, image, dots = resident(kernel, out_shape, 2, (), *args, *extra, pack)
        args = (core_table, border_block, image, before, after, couplings, left, dots)
        (dots,) = resident(finish, [dots_shape], 2, (), *args)
        return step, dots

    def resident(kernel, out_shape, tables, scratch, *args):
        vmem = pl.BlockSpec(memory_space=pltpu.VMEM)
        return pl.pallas_call(
            kernel,
            out_shape=out_shape,
            in_specs=[table()] * tables + [vmem] * (len(args) - tables),
            out_specs=[vmem] * len(out_shape),
            scratch_shapes=scratch,
            compiler_params=PLAIN,
            name=getattr(kernel, "func", kernel).__name__,
        )(*args)

    def small(kernel, out_shape, *args):
        return pl.pallas_call(
            kernel, out_shape=out_shape, compiler_params=PLAIN, name=kernel.__name__
        )(*args)

    tall = size + size // 2

    def batch_block(*dims):
        return pl.BlockSpec((BATCH,) + dims, lambda s: (s,) + (0,) * len(dims))

    vmem = pl.BlockSpec(memory_space=pltpu.VMEM)
    factor, keep, send = pl.pallas_call(
        prepare_kernel,
        out_shape=[shape(*scen_rhs.shape[:3], 3 * size, kind=HALF)] + [shape(half, tall, rhs)] * 2,
        in_specs=[table()] * 2 + [pl.BlockSpec(memory_space=pltpu.HBM)] * 3,
        out_specs=[vmem] * 3,
        scratch_shapes=[
            pltpu.VMEM(scen_rhs.shape, F32),
            pltpu.VMEM(diag_inverse.shape, HALF),
            pltpu.VMEM(border.shape, F32),
            pltpu.VMEM((blocks, size, rhs + size), F32),
            pltpu.SemaphoreType.DMA((scen_local // BATCH, 3)),
        ],
        compiler_params=PLAIN,
        name="prepare",
    )(core_table, *in_hbm(border_block, scen_rhs, diag_inverse, border))
    arrived = spread_plane(keep + swap(send))
    guess_sum, weight, message = small(
        begin_kernel,
        [vector, shape(size // 2, 2 * size), shape(groups, size, rhs, kind=HALF)],
        arrived,
        first_res,
        first_diag,
    )
    arrived = solve(spread_fs(message), False)
    first_step, message = small(owned_kernel, [vector, shape(plane, size, rhs, kind=HALF)], arrived)
    scen_step, image, side, dots, keep, send, pack = window_pass(message, None)
    arrived = spread_plane(keep + swap(send))
    turn, image_first, message = small(
        turn_kernel,
        [vector, vector, shape(groups, size + DOT_ROWS, rhs, kind=HALF)],
        arrived,
        first_step,
        guess_sum,
        weight,
        first_res,
        dots,
    )
    arrived = solve(spread_fs(message), True)
    step_size, next_step, message = small(
        next_kernel, [shape(8, rhs), vector, shape(plane, size, rhs, kind=HALF)], arrived, first_step
    )
    later_step, dots = window_pass(message, (image, side, step_size), pack)
    next_image, first_left, both = small(
        ending_kernel,
        [vector, vector, shape(2, rhs)],
        step_size,
        next_step,
        guess_sum,
        turn,
        weight,
        first_res,
        image_first,
        dots,
    )
    both = both + swap(both)
    message = jnp.broadcast_to(both[None], (plane * groups, 2, rhs))
    arrived = lax.all_to_all(message, ("x", "y", "fs"), 0, 0)
    scen_sol, first_sol, first_left = pl.pallas_call(
        final_kernel,
        out_shape=[fields, vector, vector],
        grid=(scen_local // BATCH,),
        in_specs=[vmem] * 8,
        out_specs=[batch_block(*field), whole(size, rhs), whole(size, rhs)],
        scratch_shapes=[pltpu.VMEM((8, rhs), F32)],
        compiler_params=PARAMS,
        name="final",
    )(arrived, step_size, scen_step, later_step, first_step, next_step, first_left, next_image)
    return (scen_sol, first_sol.reshape(1, size, rhs), first_left.reshape(1, size, rhs))


def solution(mesh):
    groups = mesh.shape["fs"]
    grid = Mesh(
        mesh.devices.reshape(CHIP_X, CHIP_Y, CORES, groups), ("x", "y", "core", "fs")
    )
    return jax.shard_map(
        per_device,
        mesh=grid,
        in_specs=(
            P(SCEN, "fs", None, None),
            P("fs", SCEN, None),
            P(SCEN, "fs", None, None),
            P(SCEN, "fs", None, None),
            P(SCEN, "fs", None, None, None),
            P(SCEN, "fs", None, None),
            P(SCEN, "fs"),
            P("fs", SCEN),
            P(None, SCEN, "fs", None),
        ),
        out_specs=(
            P(SCEN, "fs", None, None),
            P("fs", SCEN, None),
            P("fs", SCEN, None),
        ),
        check_vma=False,
    )
```

```python
import functools

import jax
import jax.numpy as jnp
from jax import lax
from jax.experimental import pallas as pl
from jax.experimental.pallas import tpu as pltpu
from jax.sharding import Mesh
from jax.sharding import PartitionSpec as P

CHIP_X = 4
CHIP_Y = 4
CORES = 2
PLANE = ("x", "y")
SCEN = ("x", "y", "core")
SWAP = [(0, 1), (1, 0)]
F32 = jnp.float32
HALF = jnp.bfloat16
DOT_ROWS = 16
BATCH = 2
STEP_BATCH = 4
TILE_BLOCKS = 8
EXACT = lax.Precision.HIGHEST
PARAMS = pltpu.CompilerParams(
    dimension_semantics=("arbitrary",), vmem_limit_bytes=24 * 1024 * 1024
)
PLAIN = pltpu.CompilerParams(vmem_limit_bytes=16 * 1024 * 1024)


def split(values):
    high = values.astype(HALF)
    return high, (values - high.astype(F32)).astype(HALF)


def dot(left, right):
    return jnp.dot(left, right, preferred_element_type=F32)


def dot_t(left, right):
    return lax.dot_general(left, right, (((0,), (0,)), ((), ())), preferred_element_type=F32)


def wide2(pieces):
    return jnp.concatenate([pieces[0], pieces[1]], axis=1)


def wide3(pieces):
    return jnp.concatenate([pieces[0], pieces[0], pieces[1]], axis=1)


def tall2(pieces):
    return jnp.concatenate([pieces[0], pieces[1]], axis=0)


def tall3(pieces):
    return jnp.concatenate([pieces[0], pieces[1], pieces[0]], axis=0)


def pieces_of(vectors):
    rows = []
    for vector in vectors:
        high = vector.astype(HALF).astype(F32)
        rest = vector - high
        mid = rest.astype(HALF).astype(F32)
        rows += [high, mid, rest - mid]
    return stack_rows(rows)


def stack_rows(rows):
    width = rows[0].shape[-1]
    place = lax.broadcasted_iota(jnp.int32, (DOT_ROWS, width), 0)
    total = jnp.zeros((DOT_ROWS, width), F32)
    for index, row in enumerate(rows):
        total = jnp.where(place == index, jnp.broadcast_to(row, (DOT_ROWS, width)), total)
    return total


def join_pieces(rows):
    return rows[0:1] + rows[1:2] + rows[2:3], rows[3:4] + rows[4:5] + rows[5:6]


def fold(values):
    return jnp.sum(values.reshape(values.shape[0] // 8, 8, values.shape[1]), axis=0)


def first_block(*shape):
    return pl.BlockSpec((1,) + shape, lambda s, *_: (s,) + (0,) * len(shape))


def whole(*shape):
    return pl.BlockSpec(shape, lambda *_: (0,) * len(shape))


def table():
    return pl.BlockSpec(memory_space=pltpu.SMEM)


def place(block_ref, core_ref, s, w):
    block = block_ref[s, w]
    return block >> 1, jnp.bitwise_xor(block & 1, core_ref[0])


def address(block_ref, core_ref, half, s, w):
    slot, side = place(block_ref, core_ref, s, w)
    return side * half + slot


def prepare_kernel(
    core_ref, block_ref, res_hbm, inv_hbm, border_hbm, factor_ref, keep_ref, send_ref, res_ref, inv_ref, border_ref, acc, sem
):
    scens, windows, size, rhs = res_ref.shape
    half = keep_ref.shape[0]
    batches = scens // BATCH
    pairs = ((res_hbm, res_ref), (inv_hbm, inv_ref), (border_hbm, border_ref))

    def copies(batch):
        part = pl.ds(batch * BATCH, BATCH)
        return [
            pltpu.make_async_copy(source.at[part], target.at[part], sem.at[batch, index])
            for index, (source, target) in enumerate(pairs)
        ]

    for batch in range(batches):
        for copy in copies(batch):
            copy.start()
    acc[...] = jnp.zeros_like(acc)

    def body(batch, carry):
        for copy in copies(batch):
            copy.wait()
        spots = [(batch * BATCH + s, w) for s in range(BATCH) for w in range(windows)]
        tiles = [split(border_ref[s, w]) for s, w in spots]
        products = []
        for (s, w), tile in zip(spots, tiles):
            inverse = inv_ref[s, w]
            products.append(dot_t(tall2(tile), tall2((inverse, inverse))))
        terms = []
        for (s, w), tile, product in zip(spots, tiles, products):
            factor = wide3(split(product))
            factor_ref[s, w] = factor
            right = jnp.concatenate([tall3(split(res_ref[s, w])), tall3(tile)], axis=1)
            terms.append(dot(factor, right))
        for (s, w), term in zip(spots, terms):
            acc[address(block_ref, core_ref, half, s, w)] += term
        return carry

    lax.fori_loop(0, batches, body, 0)
    for start, out in ((0, keep_ref), (half, send_ref)):
        out[:, 0:size, :] = acc[start : start + half, :, 0:rhs]
        out[:, size:, 0:size] = acc[start : start + half, 0 : size // 2, rhs : rhs + size]
        out[:, size:, size:] = acc[start : start + half, size // 2 :, rhs : rhs + size]


def begin_kernel(arrived_ref, first_ref, diag_ref, sum_ref, weight_ref, message_ref):
    size = first_ref.shape[0]
    total = jnp.sum(arrived_ref[...], axis=0)
    summed = total[:size]
    sum_ref[...] = summed
    side = size // 2
    diag = jnp.concatenate([diag_ref[...], diag_ref[...]], axis=1)
    row = lax.broadcasted_iota(jnp.int32, (side, 2 * size), 0)
    lane = lax.broadcasted_iota(jnp.int32, (side, 2 * size), 1)
    spot = jnp.logical_or(lane == row, lane == row + side + size)
    weight_ref[...] = total[size:] + jnp.where(spot, jnp.broadcast_to(diag, (side, 2 * size)), 0.0)
    message = (first_ref[...] + summed).astype(HALF)
    message_ref[...] = jnp.broadcast_to(message[None], message_ref.shape)


def solve_kernel(core_ref, arrived_ref, schur_ref, mine_ref, theirs_ref, *rest, with_dots):
    groups = arrived_ref.shape[0]
    size = mine_ref.shape[1]
    wide = TILE_BLOCKS * size
    operand = jnp.concatenate([arrived_ref[g, 0:size, :] for g in range(groups)], axis=0)
    if with_dots:
        rows = jnp.sum(arrived_ref[:, size:, :].astype(F32), axis=0)
        dots = stack_rows(list(join_pieces(rows)))
        rest[0][...] = dots
        theirs_ref[theirs_ref.shape[0] - 1, 0:DOT_ROWS, :] = dots
    flipped = operand.T
    values = []
    for tile in range(schur_ref.shape[1] // wide):
        values.append(dot(flipped, schur_ref[:, tile * wide : (tile + 1) * wide]).T)

    def write(evens_ref, odds_ref):
        for tile, value in enumerate(values):
            for pair in range(TILE_BLOCKS // CORES):
                slot = tile * (TILE_BLOCKS // CORES) + pair
                evens_ref[slot] = value[(2 * pair) * size : (2 * pair + 1) * size]
                odds_ref[slot] = value[(2 * pair + 1) * size : (2 * pair + 2) * size]

    @pl.when(core_ref[0] == 0)
    def _():
        write(mine_ref, theirs_ref)

    @pl.when(core_ref[0] != 0)
    def _():
        write(theirs_ref, mine_ref)


def pair_kernel(mine_ref, got_ref, *rest):
    message_ref = rest[-1]
    plane, size, rhs = mine_ref.shape
    message_ref[:, 0:size, :] = (mine_ref[...] + got_ref[0:plane]).astype(HALF)
    if len(rest) > 1:
        dots = rest[0][...] + got_ref[plane, 0:DOT_ROWS, :]
        pieces = pieces_of([dots[0:1], dots[1:2]]).astype(HALF)
        message_ref[:, size:, :] = jnp.broadcast_to(pieces[None], (plane,) + pieces.shape)


def owned_kernel(arrived_ref, step_ref, message_ref):
    total = jnp.sum(arrived_ref[...].astype(F32), axis=0).astype(HALF)
    step_ref[...] = total.astype(F32)
    message_ref[...] = jnp.broadcast_to(total[None], message_ref.shape)


def residual(res_ref, last, s, w):
    if last is None:
        return res_ref[s, w]
    image_ref, side_ref, size_ref = last
    windows = res_ref.shape[1]
    if w == 0:
        image = side_ref[s, 0]
    elif w == windows - 1:
        image = side_ref[s, 1]
    else:
        image = image_ref[s, w]
    return res_ref[s, w] - size_ref[0:1] * image


def window_steps(tables, mine_ref, other_ref, border_ref, inv_ref, spots, values):
    core_ref, block_ref = tables
    lifts = []
    for s, w in spots:
        slot, side = place(block_ref, core_ref, s, w)
        mine = mine_ref[slot].astype(F32)
        other = other_ref[slot].astype(F32)
        block = jnp.where(side == 0, mine, other).astype(HALF)
        lifts.append(dot(wide2(split(border_ref[s, w])), tall2((block, block))))
    steps = []
    for (s, w), res, lift in zip(spots, values, lifts):
        inverse = inv_ref[s, w]
        steps.append(dot(wide2((inverse, inverse)), tall2(split(res - lift))))
    return steps


def edge_kernel(core_ref, block_ref, mine_ref, other_ref, border_ref, inv_ref, res_ref, *rest):
    head_ref, tail_ref = rest[-2:]
    last = rest[:3] if len(rest) > 2 else None
    scens, windows = res_ref.shape[:2]
    tables = (core_ref, block_ref)
    spots = [(s, w) for s in range(scens) for w in (0, windows - 1)]
    values = [residual(res_ref, last, s, w) for s, w in spots]
    steps = window_steps(tables, mine_ref, other_ref, border_ref, inv_ref, spots, values)
    for (s, w), step in zip(spots, steps):
        out = head_ref if w == 0 else tail_ref
        out[s] = step.astype(HALF)


def pack_kernel(border_ref, diag_ref, pair_ref, pack_ref):
    scens, windows, size, _ = diag_ref.shape
    side = 2 * size

    def body(s, carry):
        for w in range(windows):
            one = split(jnp.concatenate([pair_ref[s, w, 0], diag_ref[s, w]], axis=1))
            two = split(jnp.concatenate([pair_ref[s, w, 1], border_ref[s, w]], axis=1))
            for part, piece in enumerate((one[0], two[0], one[1], two[1])):
                pack_ref[s, w, :, part * side : (part + 1) * side] = piece
        return carry

    lax.fori_loop(0, scens, body, 0)


def step_kernel(core_ref, block_ref, mine_ref, other_ref, pack_ref, inv_ref, res_ref, *rest, first):
    scens, windows, size, rhs = res_ref.shape
    if first:
        factor_ref, step_ref, image_ref, dots_ref, acc_ref = rest
        last = None
        acc_ref[...] = jnp.zeros_like(acc_ref)
    else:
        last = rest[:3]
        step_ref, left_ref, image_ref, dots_ref = rest[3:]
    nothing = jnp.zeros((size, rhs), HALF)
    side = 2 * size

    def body(batch, totals):
        along, energy = totals
        spots = [(batch * STEP_BATCH + s, w) for s in range(STEP_BATCH) for w in range(windows)]
        left = [residual(res_ref, last, s, w) for s, w in spots]
        packs, blocks, lifts = [], [], []
        for s, w in spots:
            slot, core_side = place(block_ref, core_ref, s, w)
            mine = mine_ref[slot].astype(F32)
            other = other_ref[slot].astype(F32)
            block = jnp.where(core_side == 0, mine, other).astype(HALF)
            pack = [pack_ref[s, w, :, part * side : (part + 1) * side] for part in range(4)]
            packs.append(pack)
            blocks.append(block)
            lifts.append(dot(wide2((pack[1], pack[3])), jnp.concatenate([nothing, block] * 2, axis=0)))
        found = []
        for (s, w), res, lift in zip(spots, left, lifts):
            inverse = inv_ref[s, w]
            found.append(dot(wide2((inverse, inverse)), tall2(split(res - lift))))
        steps = []
        for (s, w), value in zip(spots, found):
            step_ref[s, w] = value
            steps.append(split(value))
        images = []
        for at, (s, w) in enumerate(spots):
            before = steps[at - 1] if w > 0 else (nothing, nothing)
            after = steps[at + 1] if w < windows - 1 else (nothing, nothing)
            high = [before[0], steps[at][0], after[0], blocks[at]]
            low = [before[1], steps[at][1], after[1], nothing]
            one_high, two_high, one_low, two_low = packs[at]
            mats = [one_high, two_high, one_high, two_high, one_low, two_low]
            images.append(dot(jnp.concatenate(mats, axis=1), jnp.concatenate(high + low + high, axis=0)))
        terms = []
        for (s, w), res, image in zip(spots, left, images):
            inner = 0 < w < windows - 1
            if inner:
                along += fold(res * image)
                energy += fold(image * image)
            if first:
                image_ref[s, w] = image
                if inner:
                    terms.append((s, w, dot(factor_ref[s, w], tall3(split(image)))))
            elif not inner:
                spot = 0 if w == 0 else 1
                image_ref[s, spot] = image
                left_ref[s, spot] = res
        for s, w, term in terms:
            acc_ref[address(block_ref, core_ref, acc_ref.shape[0] // CORES, s, w)] += term
        return along, energy

    zero = jnp.zeros((8, rhs), F32)
    along, energy = lax.fori_loop(0, scens // STEP_BATCH, body, (zero, zero))
    dots_ref[0:8, :] = along
    dots_ref[8:16, :] = energy


def finish_kernel(core_ref, block_ref, image_ref, before_ref, after_ref, pair_ref, res_ref, dots_ref, *rest, first):
    scens, windows, _, size, _ = pair_ref.shape
    rhs = before_ref.shape[2]
    if first:
        factor_ref, acc_ref, side_ref, out_ref, keep_ref, send_ref, acc = rest
        acc[...] = acc_ref[...]
    else:
        (out_ref,) = rest
    along = jnp.zeros((8, rhs), F32)
    energy = jnp.zeros((8, rhs), F32)
    terms = []
    spots = [(s, spot) for s in range(scens) for spot in (0, 1)]
    halos = []
    for s, spot in spots:
        w = (windows - 1) * spot
        halo = (before_ref, after_ref)[spot][s]
        halos.append(dot(wide2(split(pair_ref[s, w, spot])), tall2((halo, halo))))
    for (s, spot), halo in zip(spots, halos):
        w = (windows - 1) * spot
        at = w if first else spot
        image = halo + image_ref[s, at]
        along += fold(res_ref[s, at] * image)
        energy += fold(image * image)
        if first:
            side_ref[s, spot] = image
            terms.append((s, w, dot(factor_ref[s, w], tall3(split(image)))))
    out_ref[0:8, :] = dots_ref[0:8, :] + along
    out_ref[8:16, :] = dots_ref[8:16, :] + energy
    if first:
        half = keep_ref.shape[0]
        for s, w, term in terms:
            acc[address(block_ref, core_ref, half, s, w)] += term
        keep_ref[...] = acc[0:half]
        send_ref[...] = acc[half:]


def first_image(weight, step, summed):
    size = step.shape[0]
    top = jnp.dot(weight[:, :size], step, precision=EXACT, preferred_element_type=F32)
    low = jnp.dot(weight[:, size:], step, precision=EXACT, preferred_element_type=F32)
    return jnp.concatenate([top, low], axis=0) - summed


def local_dots(dots, res, image):
    along = jnp.sum(dots[0:8] + fold(res * image), axis=0, keepdims=True)
    energy = jnp.sum(dots[8:16] + fold(image * image), axis=0, keepdims=True)
    return along, energy


def turn_kernel(arrived_ref, step_ref, sum_ref, weight_ref, first_ref, dots_ref, turn_ref, image_ref, message_ref):
    size = step_ref.shape[0]
    turn = jnp.sum(arrived_ref[...], axis=0)
    image = first_image(weight_ref[...], step_ref[...], sum_ref[...])
    turn_ref[...] = turn
    image_ref[...] = image
    change = (first_ref[...] + sum_ref[...]) - (image + turn)
    pieces = pieces_of(local_dots(dots_ref[...], first_ref[...], image)).astype(HALF)
    message = jnp.concatenate([change.astype(HALF), pieces], axis=0)
    message_ref[...] = jnp.broadcast_to(message[None], message_ref.shape)


def next_kernel(arrived_ref, step_ref, size_ref, next_ref, message_ref):
    rows = step_ref.shape[0]
    total = jnp.sum(arrived_ref[...].astype(F32), axis=0)
    along, energy = join_pieces(total[rows:])
    size = along / (energy + 1e-06)
    size_ref[...] = jnp.broadcast_to(size, size_ref.shape)
    step = ((1.0 - size) * step_ref[...] + size * total[:rows]).astype(HALF)
    next_ref[...] = step.astype(F32)
    message_ref[...] = jnp.broadcast_to(step[None], message_ref.shape)


def ending_kernel(
    size_ref, step_ref, sum_ref, turn_ref, weight_ref, first_ref, image_ref, dots_ref, next_ref, res_ref, out_ref
):
    size = size_ref[0:1]
    image = first_image(weight_ref[...], step_ref[...], sum_ref[...] - size * turn_ref[...])
    res = first_ref[...] - size * image_ref[...]
    next_ref[...] = image
    res_ref[...] = res
    along, energy = local_dots(dots_ref[...], res, image)
    row = lax.broadcasted_iota(jnp.int32, (2, along.shape[1]), 0)
    both = jnp.where(row == 0, jnp.broadcast_to(along, row.shape), jnp.broadcast_to(energy, row.shape))
    out_ref[...] = both


def final_kernel(
    arrived_ref, size_ref, step_ref, later_ref, first_ref, next_ref, res_ref, image_ref, sol_ref, head_ref, out_ref, later_size
):
    scen = pl.program_id(0)
    size = size_ref[0:1]

    @pl.when(scen == 0)
    def _():
        total = jnp.sum(arrived_ref[...], axis=0)
        later = total[0:1] / (total[1:2] + 1e-06)
        later_size[...] = jnp.broadcast_to(later, later_size.shape)
        head_ref[...] = size * first_ref[...] + later * next_ref[...]
        out_ref[...] = res_ref[...] - later * image_ref[...]

    scens = sol_ref.shape[0]
    for s in range(scens):
        at = scen * scens + s
        sol_ref[s] = size * step_ref[at] + later_size[0:1] * later_ref[at]


def shape(*dims, kind=F32):
    return jax.ShapeDtypeStruct(dims, kind)


def in_hbm(*arrays):
    return [pltpu.with_memory_space_constraint(array, pltpu.HBM) for array in arrays]


def per_device(
    scen_rhs,
    first_rhs,
    diag_blocks,
    diag_inverse,
    couplings,
    border,
    border_block,
    first_diag,
    schur_inverse,
):
    core = lax.axis_index("core").astype(jnp.int32)
    scen_local, window_local, size, rhs = scen_rhs.shape
    group_rows = schur_inverse.shape[-1]
    blocks = group_rows // size
    half = blocks // CORES
    groups = lax.axis_size("fs")
    plane = CHIP_X * CHIP_Y
    columns = schur_inverse.shape[0] * schur_inverse.shape[1]
    schur_flat = schur_inverse.reshape(columns, group_rows)
    first_res = first_rhs.reshape(size, rhs)
    core_table = core.reshape(1)
    vmem = pl.BlockSpec(memory_space=pltpu.VMEM)
    field = (window_local, size, rhs)
    tile = (window_local, size, size)
    grid = (scen_local,)
    fields = shape(scen_local, *field)
    edges = shape(scen_local, size, rhs)
    vector = shape(size, rhs)

    def swap(values):
        return lax.ppermute(values, "core", SWAP)

    def spread_plane(values):
        return lax.all_to_all(values, PLANE, 0, 0)

    def spread_fs(values):
        return lax.all_to_all(values, "fs", 0, 0)

    def solve(arrived, with_dots):
        extra = 1 if with_dots else 0
        out_shape = [shape(half, size, rhs), shape(half + extra, size, rhs)]
        if with_dots:
            out_shape.append(shape(DOT_ROWS, rhs))
        kernel = functools.partial(solve_kernel, with_dots=with_dots)
        out = resident(kernel, out_shape, 1, (), core_table, arrived, schur_flat)
        theirs, pack = out[1], None
        if not with_dots:
            theirs, *tiles = lax.optimization_barrier((theirs, border, diag_blocks, couplings))
            pack = pl.pallas_call(
                pack_kernel,
                out_shape=shape(*scen_rhs.shape[:3], 8 * size, kind=HALF),
                in_specs=[vmem] * 3,
                out_specs=vmem,
                compiler_params=PLAIN,
                cost_estimate=pl.CostEstimate(flops=1 << 22, bytes_accessed=12 << 20, transcendentals=0),
                name="pack",
            )(*tiles)
        got = swap(theirs)
        if pack is not None:
            got, pack = lax.optimization_barrier((got, pack))
        rows_out = size + (DOT_ROWS if with_dots else 0)
        message = pl.pallas_call(
            pair_kernel,
            out_shape=shape(plane, rows_out, rhs, kind=HALF),
            compiler_params=PLAIN,
            name="pair",
        )(out[0], got, *out[2:])
        return spread_plane(message), pack

    def window_pass(message, last, pack):
        first = last is None
        mine = spread_plane(message)
        other = swap(mine)
        extra = () if first else last
        args = (core_table, border_block, mine, other, border, diag_inverse, scen_rhs)
        head, tail = resident(
            edge_kernel, [shape(scen_local, size, rhs, kind=HALF)] * 2, 2, (), *args, *extra
        )
        ends = groups - 1
        before = lax.ppermute(tail, "fs", [(i, i + 1) for i in range(ends)])
        after = lax.ppermute(head, "fs", [(i + 1, i) for i in range(ends)])
        sides_shape = shape(scen_local, 2, size, rhs)
        dots_shape = shape(DOT_ROWS, rhs)
        args = (core_table, border_block, mine, other, pack, diag_inverse, scen_rhs)
        kernel = functools.partial(step_kernel, first=first)
        finish = functools.partial(finish_kernel, first=first)
        if first:
            out_shape = [fields, fields, dots_shape, shape(blocks, size, rhs)]
            step, image, dots, acc = resident(kernel, out_shape, 2, (), *args, factor)
            out_shape = [sides_shape, dots_shape] + [shape(half, size, rhs)] * 2
            scratch = (pltpu.VMEM((blocks, size, rhs), F32),)
            args = (core_table, border_block, image, before, after, couplings, scen_rhs, dots, factor, acc)
            side, dots, keep, send = resident(finish, out_shape, 2, scratch, *args)
            return step, image, side, dots, keep, send
        out_shape = [fields, sides_shape, sides_shape, dots_shape]
        step, left, image, dots = resident(kernel, out_shape, 2, (), *args, *extra)
        args = (core_table, border_block, image, before, after, couplings, left, dots)
        (dots,) = resident(finish, [dots_shape], 2, (), *args)
        return step, dots

    def resident(kernel, out_shape, tables, scratch, *args):
        return pl.pallas_call(
            kernel,
            out_shape=out_shape,
            in_specs=[table()] * tables + [vmem] * (len(args) - tables),
            out_specs=[vmem] * len(out_shape),
            scratch_shapes=scratch,
            compiler_params=PLAIN,
            name=getattr(kernel, "func", kernel).__name__,
        )(*args)

    def small(kernel, out_shape, *args):
        return pl.pallas_call(
            kernel, out_shape=out_shape, compiler_params=PLAIN, name=kernel.__name__
        )(*args)

    tall = size + size // 2

    def batch_block(*dims):
        return pl.BlockSpec((BATCH,) + dims, lambda s: (s,) + (0,) * len(dims))

    factor, keep, send = pl.pallas_call(
        prepare_kernel,
        out_shape=[shape(*scen_rhs.shape[:3], 3 * size, kind=HALF)] + [shape(half, tall, rhs)] * 2,
        in_specs=[table()] * 2 + [pl.BlockSpec(memory_space=pltpu.HBM)] * 3,
        out_specs=[vmem] * 3,
        scratch_shapes=[
            pltpu.VMEM(scen_rhs.shape, F32),
            pltpu.VMEM(diag_inverse.shape, HALF),
            pltpu.VMEM(border.shape, F32),
            pltpu.VMEM((blocks, size, rhs + size), F32),
            pltpu.SemaphoreType.DMA((scen_local // BATCH, 3)),
        ],
        compiler_params=PLAIN,
        name="prepare",
    )(core_table, *in_hbm(border_block, scen_rhs, diag_inverse, border))
    arrived = spread_plane(keep + swap(send))
    guess_sum, weight, message = small(
        begin_kernel,
        [vector, shape(size // 2, 2 * size), shape(groups, size, rhs, kind=HALF)],
        arrived,
        first_res,
        first_diag,
    )
    arrived, pack = solve(spread_fs(message), False)
    first_step, message = small(owned_kernel, [vector, shape(plane, size, rhs, kind=HALF)], arrived)
    scen_step, image, side, dots, keep, send = window_pass(message, None, pack)
    arrived = spread_plane(keep + swap(send))
    turn, image_first, message = small(
        turn_kernel,
        [vector, vector, shape(groups, size + DOT_ROWS, rhs, kind=HALF)],
        arrived,
        first_step,
        guess_sum,
        weight,
        first_res,
        dots,
    )
    arrived, _ = solve(spread_fs(message), True)
    step_size, next_step, message = small(
        next_kernel, [shape(8, rhs), vector, shape(plane, size, rhs, kind=HALF)], arrived, first_step
    )
    later_step, dots = window_pass(message, (image, side, step_size), pack)
    next_image, first_left, both = small(
        ending_kernel,
        [vector, vector, shape(2, rhs)],
        step_size,
        next_step,
        guess_sum,
        turn,
        weight,
        first_res,
        image_first,
        dots,
    )
    both = both + swap(both)
    message = jnp.broadcast_to(both[None], (plane * groups, 2, rhs))
    arrived = lax.all_to_all(message, ("x", "y", "fs"), 0, 0)
    scen_sol, first_sol, first_left = pl.pallas_call(
        final_kernel,
        out_shape=[fields, vector, vector],
        grid=(scen_local // BATCH,),
        in_specs=[vmem] * 8,
        out_specs=[batch_block(*field), whole(size, rhs), whole(size, rhs)],
        scratch_shapes=[pltpu.VMEM((8, rhs), F32)],
        compiler_params=PARAMS,
        name="final",
    )(arrived, step_size, scen_step, later_step, first_step, next_step, first_left, next_image)
    return (scen_sol, first_sol.reshape(1, size, rhs), first_left.reshape(1, size, rhs))


def solution(mesh):
    groups = mesh.shape["fs"]
    grid = Mesh(
        mesh.devices.reshape(CHIP_X, CHIP_Y, CORES, groups), ("x", "y", "core", "fs")
    )
    return jax.shard_map(
        per_device,
        mesh=grid,
        in_specs=(
            P(SCEN, "fs", None, None),
            P("fs", SCEN, None),
            P(SCEN, "fs", None, None),
            P(SCEN, "fs", None, None),
            P(SCEN, "fs", None, None, None),
            P(SCEN, "fs", None, None),
            P(SCEN, "fs"),
            P("fs", SCEN),
            P(None, SCEN, "fs", None),
        ),
        out_specs=(
            P(SCEN, "fs", None, None),
            P("fs", SCEN, None),
            P("fs", SCEN, None),
        ),
        check_vma=False,
    )
```

```python
import functools

import jax
import jax.numpy as jnp
from jax import lax
from jax.experimental import pallas as pl
from jax.experimental.pallas import tpu as pltpu
from jax.sharding import Mesh
from jax.sharding import PartitionSpec as P

CHIP_X = 4
CHIP_Y = 4
CORES = 2
PLANE = ("x", "y")
SCEN = ("x", "y", "core")
SWAP = [(0, 1), (1, 0)]
F32 = jnp.float32
HALF = jnp.bfloat16
DOT_ROWS = 16
BATCH = 2
STEP_BATCH = 4
TILE_BLOCKS = 8
EXACT = lax.Precision.HIGHEST
PARAMS = pltpu.CompilerParams(
    dimension_semantics=("arbitrary",), vmem_limit_bytes=24 * 1024 * 1024
)
PLAIN = pltpu.CompilerParams(vmem_limit_bytes=16 * 1024 * 1024)


def split(values):
    high = values.astype(HALF)
    return high, (values - high.astype(F32)).astype(HALF)


def dot(left, right):
    return jnp.dot(left, right, preferred_element_type=F32)


def dot_t(left, right):
    return lax.dot_general(left, right, (((0,), (0,)), ((), ())), preferred_element_type=F32)


def wide2(pieces):
    return jnp.concatenate([pieces[0], pieces[1]], axis=1)


def wide3(pieces):
    return jnp.concatenate([pieces[0], pieces[0], pieces[1]], axis=1)


def tall2(pieces):
    return jnp.concatenate([pieces[0], pieces[1]], axis=0)


def tall3(pieces):
    return jnp.concatenate([pieces[0], pieces[1], pieces[0]], axis=0)


def pieces_of(vectors):
    rows = []
    for vector in vectors:
        high = vector.astype(HALF).astype(F32)
        rest = vector - high
        mid = rest.astype(HALF).astype(F32)
        rows += [high, mid, rest - mid]
    return stack_rows(rows)


def stack_rows(rows):
    width = rows[0].shape[-1]
    place = lax.broadcasted_iota(jnp.int32, (DOT_ROWS, width), 0)
    total = jnp.zeros((DOT_ROWS, width), F32)
    for index, row in enumerate(rows):
        total = jnp.where(place == index, jnp.broadcast_to(row, (DOT_ROWS, width)), total)
    return total


def join_pieces(rows):
    return rows[0:1] + rows[1:2] + rows[2:3], rows[3:4] + rows[4:5] + rows[5:6]


def fold(values):
    return jnp.sum(values.reshape(values.shape[0] // 8, 8, values.shape[1]), axis=0)


def first_block(*shape):
    return pl.BlockSpec((1,) + shape, lambda s, *_: (s,) + (0,) * len(shape))


def whole(*shape):
    return pl.BlockSpec(shape, lambda *_: (0,) * len(shape))


def table():
    return pl.BlockSpec(memory_space=pltpu.SMEM)


def place(block_ref, core_ref, s, w):
    block = block_ref[s, w]
    return block >> 1, jnp.bitwise_xor(block & 1, core_ref[0])


def address(block_ref, core_ref, half, s, w):
    slot, side = place(block_ref, core_ref, s, w)
    return side * half + slot


def prepare_kernel(
    core_ref, block_ref, res_hbm, inv_hbm, border_hbm, factor_ref, keep_ref, send_ref, res_ref, inv_ref, border_ref, acc, sem
):
    scens, windows, size, rhs = res_ref.shape
    half = keep_ref.shape[0]
    batches = scens // BATCH
    pairs = ((res_hbm, res_ref), (inv_hbm, inv_ref), (border_hbm, border_ref))

    def copies(batch):
        part = pl.ds(batch * BATCH, BATCH)
        return [
            pltpu.make_async_copy(source.at[part], target.at[part], sem.at[batch, index])
            for index, (source, target) in enumerate(pairs)
        ]

    for batch in range(batches):
        for copy in copies(batch):
            copy.start()
    acc[...] = jnp.zeros_like(acc)

    def body(batch, carry):
        for copy in copies(batch):
            copy.wait()
        spots = [(batch * BATCH + s, w) for s in range(BATCH) for w in range(windows)]
        tiles = [split(border_ref[s, w]) for s, w in spots]
        products = []
        for (s, w), tile in zip(spots, tiles):
            inverse = inv_ref[s, w]
            products.append(dot_t(tall2(tile), tall2((inverse, inverse))))
        terms = []
        for (s, w), product in zip(spots, products):
            factor = wide3(split(product))
            factor_ref[s, w] = factor
            terms.append(dot(factor, tall3(split(res_ref[s, w]))))
        for (s, w), term in zip(spots, terms):
            acc[address(block_ref, core_ref, half, s, w)] += term
        return carry

    lax.fori_loop(0, batches, body, 0)
    keep_ref[...] = acc[0:half]
    send_ref[...] = acc[half:]


def weight_kernel(core_ref, block_ref, factor_ref, border_ref, keep_ref, send_ref, acc):
    scens, windows, size, _ = border_ref.shape
    half = keep_ref.shape[0]
    acc[...] = jnp.zeros_like(acc)

    def body(batch, carry):
        spots = [(batch * BATCH + s, w) for s in range(BATCH) for w in range(windows)]
        terms = [dot(factor_ref[s, w], tall3(split(border_ref[s, w]))) for s, w in spots]
        for (s, w), term in zip(spots, terms):
            acc[address(block_ref, core_ref, half, s, w)] += term
        return carry

    lax.fori_loop(0, scens // BATCH, body, 0)
    for start, out in ((0, keep_ref), (half, send_ref)):
        out[:, :, 0:size] = acc[start : start + half, 0 : size // 2]
        out[:, :, size:] = acc[start : start + half, size // 2 :]


def begin_kernel(arrived_ref, first_ref, sum_ref, message_ref):
    summed = jnp.sum(arrived_ref[...], axis=0)
    sum_ref[...] = summed
    message = (first_ref[...] + summed).astype(HALF)
    message_ref[...] = jnp.broadcast_to(message[None], message_ref.shape)


def with_diag(rows, diag):
    side = rows.shape[0]
    twice = jnp.concatenate([diag, diag], axis=1)
    row = lax.broadcasted_iota(jnp.int32, rows.shape, 0)
    lane = lax.broadcasted_iota(jnp.int32, rows.shape, 1)
    spot = jnp.logical_or(lane == row, lane == row + 3 * side)
    return rows + jnp.where(spot, jnp.broadcast_to(twice, rows.shape), 0.0)


def join_kernel(keep_ref, got_ref, weight_ref, other_ref, message_ref):
    size = keep_ref.shape[1]
    message_ref[:, 0:size, :] = keep_ref[...] + got_ref[...]
    message_ref[:, size:, :] = weight_ref[...] + other_ref[...]


def solve_kernel(core_ref, arrived_ref, schur_ref, mine_ref, theirs_ref, *rest, with_dots):
    groups = arrived_ref.shape[0]
    size = mine_ref.shape[1]
    wide = TILE_BLOCKS * size
    operand = jnp.concatenate([arrived_ref[g, 0:size, :] for g in range(groups)], axis=0)
    if with_dots:
        rows = jnp.sum(arrived_ref[:, size:, :].astype(F32), axis=0)
        dots = stack_rows(list(join_pieces(rows)))
        rest[0][...] = dots
        theirs_ref[theirs_ref.shape[0] - 1, 0:DOT_ROWS, :] = dots
    flipped = operand.T
    values = []
    for tile in range(schur_ref.shape[1] // wide):
        values.append(dot(flipped, schur_ref[:, tile * wide : (tile + 1) * wide]).T)

    def write(evens_ref, odds_ref):
        for tile, value in enumerate(values):
            for pair in range(TILE_BLOCKS // CORES):
                slot = tile * (TILE_BLOCKS // CORES) + pair
                evens_ref[slot] = value[(2 * pair) * size : (2 * pair + 1) * size]
                odds_ref[slot] = value[(2 * pair + 1) * size : (2 * pair + 2) * size]

    @pl.when(core_ref[0] == 0)
    def _():
        write(mine_ref, theirs_ref)

    @pl.when(core_ref[0] != 0)
    def _():
        write(theirs_ref, mine_ref)


def pair_kernel(mine_ref, got_ref, *rest):
    message_ref = rest[-1]
    plane, size, rhs = mine_ref.shape
    message_ref[:, 0:size, :] = (mine_ref[...] + got_ref[0:plane]).astype(HALF)
    if len(rest) > 1:
        dots = rest[0][...] + got_ref[plane, 0:DOT_ROWS, :]
        pieces = pieces_of([dots[0:1], dots[1:2]]).astype(HALF)
        message_ref[:, size:, :] = jnp.broadcast_to(pieces[None], (plane,) + pieces.shape)


def owned_kernel(arrived_ref, step_ref, message_ref):
    total = jnp.sum(arrived_ref[...].astype(F32), axis=0).astype(HALF)
    step_ref[...] = total.astype(F32)
    message_ref[...] = jnp.broadcast_to(total[None], message_ref.shape)


def residual(res_ref, last, s, w):
    if last is None:
        return res_ref[s, w]
    image_ref, side_ref, size_ref = last
    windows = res_ref.shape[1]
    if w == 0:
        image = side_ref[s, 0]
    elif w == windows - 1:
        image = side_ref[s, 1]
    else:
        image = image_ref[s, w]
    return res_ref[s, w] - size_ref[0:1] * image


def window_steps(tables, mine_ref, other_ref, border_ref, inv_ref, spots, values):
    core_ref, block_ref = tables
    lifts = []
    for s, w in spots:
        slot, side = place(block_ref, core_ref, s, w)
        mine = mine_ref[slot].astype(F32)
        other = other_ref[slot].astype(F32)
        block = jnp.where(side == 0, mine, other).astype(HALF)
        lifts.append(dot(wide2(split(border_ref[s, w])), tall2((block, block))))
    steps = []
    for (s, w), res, lift in zip(spots, values, lifts):
        inverse = inv_ref[s, w]
        steps.append(dot(wide2((inverse, inverse)), tall2(split(res - lift))))
    return steps


def edge_kernel(core_ref, block_ref, mine_ref, other_ref, border_ref, inv_ref, res_ref, *rest):
    head_ref, tail_ref = rest[-2:]
    last = rest[:3] if len(rest) > 2 else None
    scens, windows = res_ref.shape[:2]
    tables = (core_ref, block_ref)
    spots = [(s, w) for s in range(scens) for w in (0, windows - 1)]
    values = [residual(res_ref, last, s, w) for s, w in spots]
    steps = window_steps(tables, mine_ref, other_ref, border_ref, inv_ref, spots, values)
    for (s, w), step in zip(spots, steps):
        out = head_ref if w == 0 else tail_ref
        out[s] = step.astype(HALF)


def pack_kernel(border_ref, diag_ref, pair_ref, pack_ref):
    scens, windows, size, _ = diag_ref.shape
    side = 2 * size

    def body(s, carry):
        for w in range(windows):
            one = split(jnp.concatenate([pair_ref[s, w, 0], diag_ref[s, w]], axis=1))
            two = split(jnp.concatenate([pair_ref[s, w, 1], border_ref[s, w]], axis=1))
            for part, piece in enumerate((one[0], two[0], one[1], two[1])):
                pack_ref[s, w, :, part * side : (part + 1) * side] = piece
        return carry

    lax.fori_loop(0, scens, body, 0)


def step_kernel(core_ref, block_ref, mine_ref, other_ref, pack_ref, inv_ref, res_ref, *rest, first):
    scens, windows, size, rhs = res_ref.shape
    if first:
        factor_ref, step_ref, image_ref, dots_ref, acc_ref = rest
        last = None
        acc_ref[...] = jnp.zeros_like(acc_ref)
    else:
        last = rest[:3]
        step_ref, left_ref, image_ref, dots_ref = rest[3:]
    nothing = jnp.zeros((size, rhs), HALF)
    side = 2 * size

    def body(batch, totals):
        along, energy = totals
        spots = [(batch * STEP_BATCH + s, w) for s in range(STEP_BATCH) for w in range(windows)]
        left = [residual(res_ref, last, s, w) for s, w in spots]
        packs, blocks, lifts = [], [], []
        for s, w in spots:
            slot, core_side = place(block_ref, core_ref, s, w)
            mine = mine_ref[slot].astype(F32)
            other = other_ref[slot].astype(F32)
            block = jnp.where(core_side == 0, mine, other).astype(HALF)
            pack = [pack_ref[s, w, :, part * side : (part + 1) * side] for part in range(4)]
            packs.append(pack)
            blocks.append(block)
            lifts.append(dot(wide2((pack[1], pack[3])), jnp.concatenate([nothing, block] * 2, axis=0)))
        found = []
        for (s, w), res, lift in zip(spots, left, lifts):
            inverse = inv_ref[s, w]
            found.append(dot(wide2((inverse, inverse)), tall2(split(res - lift))))
        steps = []
        for (s, w), value in zip(spots, found):
            step_ref[s, w] = value
            steps.append(split(value))
        images = []
        for at, (s, w) in enumerate(spots):
            before = steps[at - 1] if w > 0 else (nothing, nothing)
            after = steps[at + 1] if w < windows - 1 else (nothing, nothing)
            high = [before[0], steps[at][0], after[0], blocks[at]]
            low = [before[1], steps[at][1], after[1], nothing]
            one_high, two_high, one_low, two_low = packs[at]
            mats = [one_high, two_high, one_high, two_high, one_low, two_low]
            images.append(dot(jnp.concatenate(mats, axis=1), jnp.concatenate(high + low + high, axis=0)))
        terms = []
        for (s, w), res, image in zip(spots, left, images):
            inner = 0 < w < windows - 1
            if inner:
                along += fold(res * image)
                energy += fold(image * image)
            if first:
                image_ref[s, w] = image
                if inner:
                    terms.append((s, w, dot(factor_ref[s, w], tall3(split(image)))))
            elif not inner:
                spot = 0 if w == 0 else 1
                image_ref[s, spot] = image
                left_ref[s, spot] = res
        for s, w, term in terms:
            acc_ref[address(block_ref, core_ref, acc_ref.shape[0] // CORES, s, w)] += term
        return along, energy

    zero = jnp.zeros((8, rhs), F32)
    along, energy = lax.fori_loop(0, scens // STEP_BATCH, body, (zero, zero))
    dots_ref[0:8, :] = along
    dots_ref[8:16, :] = energy


def finish_kernel(core_ref, block_ref, image_ref, before_ref, after_ref, pair_ref, res_ref, dots_ref, *rest, first):
    scens, windows, _, size, _ = pair_ref.shape
    rhs = before_ref.shape[2]
    if first:
        factor_ref, acc_ref, side_ref, out_ref, keep_ref, send_ref, acc = rest
        acc[...] = acc_ref[...]
    else:
        (out_ref,) = rest
    along = jnp.zeros((8, rhs), F32)
    energy = jnp.zeros((8, rhs), F32)
    terms = []
    spots = [(s, spot) for s in range(scens) for spot in (0, 1)]
    halos = []
    for s, spot in spots:
        w = (windows - 1) * spot
        halo = (before_ref, after_ref)[spot][s]
        halos.append(dot(wide2(split(pair_ref[s, w, spot])), tall2((halo, halo))))
    for (s, spot), halo in zip(spots, halos):
        w = (windows - 1) * spot
        at = w if first else spot
        image = halo + image_ref[s, at]
        along += fold(res_ref[s, at] * image)
        energy += fold(image * image)
        if first:
            side_ref[s, spot] = image
            terms.append((s, w, dot(factor_ref[s, w], tall3(split(image)))))
    out_ref[0:8, :] = dots_ref[0:8, :] + along
    out_ref[8:16, :] = dots_ref[8:16, :] + energy
    if first:
        half = keep_ref.shape[0]
        for s, w, term in terms:
            acc[address(block_ref, core_ref, half, s, w)] += term
        keep_ref[...] = acc[0:half]
        send_ref[...] = acc[half:]


def first_image(weight, step, summed):
    size = step.shape[0]
    top = jnp.dot(weight[:, :size], step, precision=EXACT, preferred_element_type=F32)
    low = jnp.dot(weight[:, size:], step, precision=EXACT, preferred_element_type=F32)
    return jnp.concatenate([top, low], axis=0) - summed


def local_dots(dots, res, image):
    along = jnp.sum(dots[0:8] + fold(res * image), axis=0, keepdims=True)
    energy = jnp.sum(dots[8:16] + fold(image * image), axis=0, keepdims=True)
    return along, energy


def turn_kernel(
    arrived_ref, step_ref, sum_ref, diag_ref, first_ref, dots_ref, turn_ref, image_ref, weight_ref, message_ref
):
    size = step_ref.shape[0]
    total = jnp.sum(arrived_ref[...], axis=0)
    turn = total[:size]
    weight = with_diag(total[size:], diag_ref[...])
    image = first_image(weight, step_ref[...], sum_ref[...])
    turn_ref[...] = turn
    image_ref[...] = image
    weight_ref[...] = weight
    change = (first_ref[...] + sum_ref[...]) - (image + turn)
    pieces = pieces_of(local_dots(dots_ref[...], first_ref[...], image)).astype(HALF)
    message = jnp.concatenate([change.astype(HALF), pieces], axis=0)
    message_ref[...] = jnp.broadcast_to(message[None], message_ref.shape)


def next_kernel(arrived_ref, step_ref, size_ref, next_ref, message_ref):
    rows = step_ref.shape[0]
    total = jnp.sum(arrived_ref[...].astype(F32), axis=0)
    along, energy = join_pieces(total[rows:])
    size = along / (energy + 1e-06)
    size_ref[...] = jnp.broadcast_to(size, size_ref.shape)
    step = ((1.0 - size) * step_ref[...] + size * total[:rows]).astype(HALF)
    next_ref[...] = step.astype(F32)
    message_ref[...] = jnp.broadcast_to(step[None], message_ref.shape)


def ending_kernel(
    size_ref, step_ref, sum_ref, turn_ref, weight_ref, first_ref, image_ref, dots_ref, next_ref, res_ref, out_ref
):
    size = size_ref[0:1]
    image = first_image(weight_ref[...], step_ref[...], sum_ref[...] - size * turn_ref[...])
    res = first_ref[...] - size * image_ref[...]
    next_ref[...] = image
    res_ref[...] = res
    along, energy = local_dots(dots_ref[...], res, image)
    row = lax.broadcasted_iota(jnp.int32, (2, along.shape[1]), 0)
    both = jnp.where(row == 0, jnp.broadcast_to(along, row.shape), jnp.broadcast_to(energy, row.shape))
    out_ref[...] = both


def final_kernel(
    arrived_ref, size_ref, step_ref, later_ref, first_ref, next_ref, res_ref, image_ref, sol_hbm, head_ref, out_ref, buffer, sem
):
    size = size_ref[0:1]
    total = jnp.sum(arrived_ref[...], axis=0)
    later = total[0:1] / (total[1:2] + 1e-06)
    scens = step_ref.shape[0]
    copies = [pltpu.make_async_copy(buffer.at[s], sol_hbm.at[s], sem.at[s]) for s in range(scens)]
    for s in range(scens):
        buffer[s] = size * step_ref[s] + later * later_ref[s]
        copies[s].start()
    head_ref[...] = size * first_ref[...] + later * next_ref[...]
    out_ref[...] = res_ref[...] - later * image_ref[...]
    for s in range(scens):
        copies[s].wait()


def shape(*dims, kind=F32):
    return jax.ShapeDtypeStruct(dims, kind)


def in_hbm(*arrays):
    return [pltpu.with_memory_space_constraint(array, pltpu.HBM) for array in arrays]


def per_device(
    scen_rhs,
    first_rhs,
    diag_blocks,
    diag_inverse,
    couplings,
    border,
    border_block,
    first_diag,
    schur_inverse,
):
    core = lax.axis_index("core").astype(jnp.int32)
    scen_local, window_local, size, rhs = scen_rhs.shape
    group_rows = schur_inverse.shape[-1]
    blocks = group_rows // size
    half = blocks // CORES
    groups = lax.axis_size("fs")
    plane = CHIP_X * CHIP_Y
    columns = schur_inverse.shape[0] * schur_inverse.shape[1]
    schur_flat = schur_inverse.reshape(columns, group_rows)
    first_res = first_rhs.reshape(size, rhs)
    core_table = core.reshape(1)
    vmem = pl.BlockSpec(memory_space=pltpu.VMEM)
    field = (window_local, size, rhs)
    tile = (window_local, size, size)
    grid = (scen_local,)
    fields = shape(scen_local, *field)
    edges = shape(scen_local, size, rhs)
    vector = shape(size, rhs)

    def swap(values):
        return lax.ppermute(values, "core", SWAP)

    def spread_plane(values):
        return lax.all_to_all(values, PLANE, 0, 0)

    def spread_fs(values):
        return lax.all_to_all(values, "fs", 0, 0)

    def solve(arrived, with_dots, ride=None):
        extra = 1 if with_dots else 0
        out_shape = [shape(half, size, rhs), shape(half + extra, size, rhs)]
        if with_dots:
            out_shape.append(shape(DOT_ROWS, rhs))
        kernel = functools.partial(solve_kernel, with_dots=with_dots)
        out = resident(kernel, out_shape, 1, (), core_table, arrived, schur_flat)
        theirs, pack = out[1], None
        if not with_dots:
            theirs, *mats = lax.optimization_barrier((theirs, tiles, diag_blocks, couplings))
            pack = pl.pallas_call(
                pack_kernel,
                out_shape=shape(*scen_rhs.shape[:3], 8 * size, kind=HALF),
                in_specs=[vmem] * 3,
                out_specs=vmem,
                compiler_params=PLAIN,
                cost_estimate=pl.CostEstimate(flops=1 << 22, bytes_accessed=12 << 20, transcendentals=0),
                name="pack",
            )(*mats)
        got = swap(theirs)
        if pack is not None:
            got, pack, ride = lax.optimization_barrier((got, pack, swap(ride)))
        rows_out = size + (DOT_ROWS if with_dots else 0)
        message = pl.pallas_call(
            pair_kernel,
            out_shape=shape(plane, rows_out, rhs, kind=HALF),
            compiler_params=PLAIN,
            name="pair",
        )(out[0], got, *out[2:])
        return spread_plane(message), pack, ride

    def window_pass(message, last, pack):
        first = last is None
        mine = spread_plane(message)
        other = swap(mine)
        extra = () if first else last
        args = (core_table, border_block, mine, other, tiles, inverse, scen_res)
        head, tail = resident(
            edge_kernel, [shape(scen_local, size, rhs, kind=HALF)] * 2, 2, (), *args, *extra
        )
        ends = groups - 1
        before = lax.ppermute(tail, "fs", [(i, i + 1) for i in range(ends)])
        after = lax.ppermute(head, "fs", [(i + 1, i) for i in range(ends)])
        sides_shape = shape(scen_local, 2, size, rhs)
        dots_shape = shape(DOT_ROWS, rhs)
        args = (core_table, border_block, mine, other, pack, inverse, scen_res)
        kernel = functools.partial(step_kernel, first=first)
        finish = functools.partial(finish_kernel, first=first)
        if first:
            out_shape = [fields, fields, dots_shape, shape(blocks, size, rhs)]
            step, image, dots, acc = resident(kernel, out_shape, 2, (), *args, factor)
            out_shape = [sides_shape, dots_shape] + [shape(half, size, rhs)] * 2
            scratch = (pltpu.VMEM((blocks, size, rhs), F32),)
            args = (core_table, border_block, image, before, after, couplings, scen_res, dots, factor, acc)
            side, dots, keep, send = resident(finish, out_shape, 2, scratch, *args)
            return step, image, side, dots, keep, send
        out_shape = [fields, sides_shape, sides_shape, dots_shape]
        step, left, image, dots = resident(kernel, out_shape, 2, (), *args, *extra)
        args = (core_table, border_block, image, before, after, couplings, left, dots)
        (dots,) = resident(finish, [dots_shape], 2, (), *args)
        return step, dots

    def resident(kernel, out_shape, tables, scratch, *args):
        return pl.pallas_call(
            kernel,
            out_shape=out_shape,
            in_specs=[table()] * tables + [vmem] * (len(args) - tables),
            out_specs=[vmem] * len(out_shape),
            scratch_shapes=scratch,
            compiler_params=PLAIN,
            name=getattr(kernel, "func", kernel).__name__,
        )(*args)

    def small(kernel, out_shape, *args):
        return pl.pallas_call(
            kernel, out_shape=out_shape, compiler_params=PLAIN, name=kernel.__name__
        )(*args)

    parts = (scen_rhs, diag_inverse, border)
    sums = shape(half, size, rhs)
    factor, keep, send, scen_res, inverse, tiles = pl.pallas_call(
        prepare_kernel,
        out_shape=[shape(*scen_rhs.shape[:3], 3 * size, kind=HALF), sums, sums]
        + [shape(*part.shape, kind=part.dtype) for part in parts],
        in_specs=[table()] * 2 + [pl.BlockSpec(memory_space=pltpu.HBM)] * 3,
        out_specs=[vmem] * 6,
        scratch_shapes=[
            pltpu.VMEM((blocks, size, rhs), F32),
            pltpu.SemaphoreType.DMA((scen_local // BATCH, 3)),
        ],
        compiler_params=PLAIN,
        name="prepare",
    )(core_table, *in_hbm(border_block, *parts))
    got = swap(send)
    packed = shape(half, size // 2, 2 * size)
    scratch = (pltpu.VMEM((blocks, size, size), F32),)
    weight_keep, weight_send = resident(
        weight_kernel, [packed, packed], 2, scratch, core_table, border_block, factor, tiles
    )
    got, weight_keep, weight_send = lax.optimization_barrier((got, weight_keep, weight_send))
    arrived = spread_plane(keep + got)
    guess_sum, message = small(
        begin_kernel, [vector, shape(groups, size, rhs, kind=HALF)], arrived, first_res
    )
    arrived, pack, weight_got = solve(spread_fs(message), False, weight_send)
    first_step, message = small(owned_kernel, [vector, shape(plane, size, rhs, kind=HALF)], arrived)
    scen_step, image, side, dots, keep, send = window_pass(message, None, pack)
    message = small(
        join_kernel, shape(half, size + size // 2, rhs), keep, swap(send), weight_keep, weight_got
    )
    arrived = spread_plane(message)
    turn, image_first, weight, message = small(
        turn_kernel,
        [vector, vector, shape(size // 2, 2 * size), shape(groups, size + DOT_ROWS, rhs, kind=HALF)],
        arrived,
        first_step,
        guess_sum,
        first_diag,
        first_res,
        dots,
    )
    arrived, _, _ = solve(spread_fs(message), True)
    step_size, next_step, message = small(
        next_kernel, [shape(8, rhs), vector, shape(plane, size, rhs, kind=HALF)], arrived, first_step
    )
    later_step, dots = window_pass(message, (image, side, step_size), pack)
    next_image, first_left, both = small(
        ending_kernel,
        [vector, vector, shape(2, rhs)],
        step_size,
        next_step,
        guess_sum,
        turn,
        weight,
        first_res,
        image_first,
        dots,
    )
    both = both + swap(both)
    message = jnp.broadcast_to(both[None], (plane * groups, 2, rhs))
    arrived = lax.all_to_all(message, ("x", "y", "fs"), 0, 0)
    scen_sol, first_sol, first_left = pl.pallas_call(
        final_kernel,
        out_shape=[fields, vector, vector],
        in_specs=[vmem] * 8,
        out_specs=[pl.BlockSpec(memory_space=pltpu.HBM), vmem, vmem],
        scratch_shapes=[pltpu.VMEM(scen_rhs.shape, F32), pltpu.SemaphoreType.DMA((scen_local,))],
        compiler_params=PLAIN,
        name="final",
    )(arrived, step_size, scen_step, later_step, first_step, next_step, first_left, next_image)
    return (scen_sol, first_sol.reshape(1, size, rhs), first_left.reshape(1, size, rhs))


def solution(mesh):
    groups = mesh.shape["fs"]
    grid = Mesh(
        mesh.devices.reshape(CHIP_X, CHIP_Y, CORES, groups), ("x", "y", "core", "fs")
    )
    return jax.shard_map(
        per_device,
        mesh=grid,
        in_specs=(
            P(SCEN, "fs", None, None),
            P("fs", SCEN, None),
            P(SCEN, "fs", None, None),
            P(SCEN, "fs", None, None),
            P(SCEN, "fs", None, None, None),
            P(SCEN, "fs", None, None),
            P(SCEN, "fs"),
            P("fs", SCEN),
            P(None, SCEN, "fs", None),
        ),
        out_specs=(
            P(SCEN, "fs", None, None),
            P("fs", SCEN, None),
            P("fs", SCEN, None),
        ),
        check_vma=False,
    )
```

```python
import functools

import jax
import jax.numpy as jnp
from jax import lax
from jax.experimental import pallas as pl
from jax.experimental.pallas import tpu as pltpu
from jax.sharding import Mesh
from jax.sharding import PartitionSpec as P

CHIP_X = 4
CHIP_Y = 4
CORES = 2
PLANE = ("x", "y")
SCEN = ("x", "y", "core")
SWAP = [(0, 1), (1, 0)]
F32 = jnp.float32
HALF = jnp.bfloat16
DOT_ROWS = 16
BATCH = 2
STEP_BATCH = 4
TILE_BLOCKS = 8
EXACT = lax.Precision.HIGHEST
PARAMS = pltpu.CompilerParams(
    dimension_semantics=("arbitrary",), vmem_limit_bytes=24 * 1024 * 1024
)
PLAIN = pltpu.CompilerParams(vmem_limit_bytes=16 * 1024 * 1024)


def split(values):
    high = values.astype(HALF)
    return high, (values - high.astype(F32)).astype(HALF)


def dot(left, right):
    return jnp.dot(left, right, preferred_element_type=F32)


def dot_t(left, right):
    return lax.dot_general(left, right, (((0,), (0,)), ((), ())), preferred_element_type=F32)


def wide2(pieces):
    return jnp.concatenate([pieces[0], pieces[1]], axis=1)


def wide3(pieces):
    return jnp.concatenate([pieces[0], pieces[0], pieces[1]], axis=1)


def tall2(pieces):
    return jnp.concatenate([pieces[0], pieces[1]], axis=0)


def tall3(pieces):
    return jnp.concatenate([pieces[0], pieces[1], pieces[0]], axis=0)


def pieces_of(vectors):
    rows = []
    for vector in vectors:
        high = vector.astype(HALF).astype(F32)
        rest = vector - high
        mid = rest.astype(HALF).astype(F32)
        rows += [high, mid, rest - mid]
    return stack_rows(rows)


def stack_rows(rows):
    width = rows[0].shape[-1]
    place = lax.broadcasted_iota(jnp.int32, (DOT_ROWS, width), 0)
    total = jnp.zeros((DOT_ROWS, width), F32)
    for index, row in enumerate(rows):
        total = jnp.where(place == index, jnp.broadcast_to(row, (DOT_ROWS, width)), total)
    return total


def join_pieces(rows):
    return rows[0:1] + rows[1:2] + rows[2:3], rows[3:4] + rows[4:5] + rows[5:6]


def fold(values):
    return jnp.sum(values.reshape(values.shape[0] // 8, 8, values.shape[1]), axis=0)


def first_block(*shape):
    return pl.BlockSpec((1,) + shape, lambda s, *_: (s,) + (0,) * len(shape))


def whole(*shape):
    return pl.BlockSpec(shape, lambda *_: (0,) * len(shape))


def table():
    return pl.BlockSpec(memory_space=pltpu.SMEM)


def place(block_ref, core_ref, s, w):
    block = block_ref[s, w]
    return block >> 1, jnp.bitwise_xor(block & 1, core_ref[0])


def address(block_ref, core_ref, half, s, w):
    slot, side = place(block_ref, core_ref, s, w)
    return side * half + slot


def prepare_kernel(
    core_ref, block_ref, res_hbm, inv_hbm, border_hbm, factor_ref, keep_ref, send_ref, res_ref, inv_ref, border_ref, acc, sem
):
    scens, windows, size, rhs = res_ref.shape
    half = keep_ref.shape[0]
    batches = scens // BATCH
    pairs = ((res_hbm, res_ref), (inv_hbm, inv_ref), (border_hbm, border_ref))

    def copies(batch):
        part = pl.ds(batch * BATCH, BATCH)
        return [
            pltpu.make_async_copy(source.at[part], target.at[part], sem.at[batch, index])
            for index, (source, target) in enumerate(pairs)
        ]

    for batch in range(batches):
        for copy in copies(batch):
            copy.start()
    acc[...] = jnp.zeros_like(acc)

    def body(batch, carry):
        for copy in copies(batch):
            copy.wait()
        spots = [(batch * BATCH + s, w) for s in range(BATCH) for w in range(windows)]
        tiles = [split(border_ref[s, w]) for s, w in spots]
        products = []
        for (s, w), tile in zip(spots, tiles):
            inverse = inv_ref[s, w]
            products.append(dot_t(tall2(tile), tall2((inverse, inverse))))
        terms = []
        for (s, w), tile, product in zip(spots, tiles, products):
            factor = wide3(split(product))
            factor_ref[s, w] = factor
            right = jnp.concatenate([tall3(split(res_ref[s, w])), tall3(tile)], axis=1)
            terms.append(dot(factor, right))
        for (s, w), term in zip(spots, terms):
            acc[address(block_ref, core_ref, half, s, w)] += term
        return carry

    lax.fori_loop(0, batches, body, 0)
    for start, out in ((0, keep_ref), (half, send_ref)):
        out[:, 0:size, :] = acc[start : start + half, :, 0:rhs]
        out[:, size:, 0:size] = acc[start : start + half, 0 : size // 2, rhs : rhs + size]
        out[:, size:, size:] = acc[start : start + half, size // 2 :, rhs : rhs + size]


def begin_kernel(arrived_ref, first_ref, diag_ref, sum_ref, weight_ref, message_ref):
    size = first_ref.shape[0]
    total = jnp.sum(arrived_ref[...], axis=0)
    summed = total[:size]
    sum_ref[...] = summed
    side = size // 2
    diag = jnp.concatenate([diag_ref[...], diag_ref[...]], axis=1)
    row = lax.broadcasted_iota(jnp.int32, (side, 2 * size), 0)
    lane = lax.broadcasted_iota(jnp.int32, (side, 2 * size), 1)
    spot = jnp.logical_or(lane == row, lane == row + side + size)
    weight_ref[...] = total[size:] + jnp.where(spot, jnp.broadcast_to(diag, (side, 2 * size)), 0.0)
    message = (first_ref[...] + summed).astype(HALF)
    message_ref[...] = jnp.broadcast_to(message[None], message_ref.shape)


def solve_kernel(core_ref, arrived_ref, schur_ref, mine_ref, theirs_ref, *rest, with_dots):
    groups = arrived_ref.shape[0]
    size = mine_ref.shape[1]
    wide = TILE_BLOCKS * size
    operand = jnp.concatenate([arrived_ref[g, 0:size, :] for g in range(groups)], axis=0)
    if with_dots:
        rows = jnp.sum(arrived_ref[:, size:, :].astype(F32), axis=0)
        dots = stack_rows(list(join_pieces(rows)))
        rest[0][...] = dots
        theirs_ref[theirs_ref.shape[0] - 1, 0:DOT_ROWS, :] = dots
    flipped = operand.T
    values = []
    for tile in range(schur_ref.shape[1] // wide):
        values.append(dot(flipped, schur_ref[:, tile * wide : (tile + 1) * wide]).T)

    def write(evens_ref, odds_ref):
        for tile, value in enumerate(values):
            for pair in range(TILE_BLOCKS // CORES):
                slot = tile * (TILE_BLOCKS // CORES) + pair
                evens_ref[slot] = value[(2 * pair) * size : (2 * pair + 1) * size]
                odds_ref[slot] = value[(2 * pair + 1) * size : (2 * pair + 2) * size]

    @pl.when(core_ref[0] == 0)
    def _():
        write(mine_ref, theirs_ref)

    @pl.when(core_ref[0] != 0)
    def _():
        write(theirs_ref, mine_ref)


def pair_kernel(mine_ref, got_ref, *rest):
    message_ref = rest[-1]
    plane, size, rhs = mine_ref.shape
    message_ref[:, 0:size, :] = (mine_ref[...] + got_ref[0:plane]).astype(HALF)
    if len(rest) > 1:
        dots = rest[0][...] + got_ref[plane, 0:DOT_ROWS, :]
        pieces = pieces_of([dots[0:1], dots[1:2]]).astype(HALF)
        message_ref[:, size:, :] = jnp.broadcast_to(pieces[None], (plane,) + pieces.shape)


def owned_kernel(arrived_ref, step_ref, message_ref):
    total = jnp.sum(arrived_ref[...].astype(F32), axis=0).astype(HALF)
    step_ref[...] = total.astype(F32)
    message_ref[...] = jnp.broadcast_to(total[None], message_ref.shape)


def residual(res_ref, last, s, w):
    if last is None:
        return res_ref[s, w]
    image_ref, side_ref, size_ref = last
    windows = res_ref.shape[1]
    if w == 0:
        image = side_ref[s, 0]
    elif w == windows - 1:
        image = side_ref[s, 1]
    else:
        image = image_ref[s, w]
    return res_ref[s, w] - size_ref[0:1] * image


def window_steps(tables, mine_ref, other_ref, border_ref, inv_ref, spots, values):
    core_ref, block_ref = tables
    lifts = []
    for s, w in spots:
        slot, side = place(block_ref, core_ref, s, w)
        mine = mine_ref[slot].astype(F32)
        other = other_ref[slot].astype(F32)
        block = jnp.where(side == 0, mine, other).astype(HALF)
        lifts.append(dot(wide2(split(border_ref[s, w])), tall2((block, block))))
    steps = []
    for (s, w), res, lift in zip(spots, values, lifts):
        inverse = inv_ref[s, w]
        steps.append(dot(wide2((inverse, inverse)), tall2(split(res - lift))))
    return steps


def edge_kernel(core_ref, block_ref, mine_ref, other_ref, border_ref, inv_ref, res_ref, *rest):
    head_ref, tail_ref = rest[-2:]
    last = rest[:3] if len(rest) > 2 else None
    scens, windows = res_ref.shape[:2]
    tables = (core_ref, block_ref)
    spots = [(s, w) for s in range(scens) for w in (0, windows - 1)]
    values = [residual(res_ref, last, s, w) for s, w in spots]
    steps = window_steps(tables, mine_ref, other_ref, border_ref, inv_ref, spots, values)
    for (s, w), step in zip(spots, steps):
        out = head_ref if w == 0 else tail_ref
        out[s] = step.astype(HALF)


def pack_kernel(border_ref, diag_ref, pair_ref, pack_ref):
    scens, windows, size, _ = diag_ref.shape
    side = 2 * size

    def body(s, carry):
        for w in range(windows):
            one = split(jnp.concatenate([pair_ref[s, w, 0], diag_ref[s, w]], axis=1))
            two = split(jnp.concatenate([pair_ref[s, w, 1], border_ref[s, w]], axis=1))
            for part, piece in enumerate((one[0], two[0], one[1], two[1])):
                pack_ref[s, w, :, part * side : (part + 1) * side] = piece
        return carry

    lax.fori_loop(0, scens, body, 0)


def step_kernel(core_ref, block_ref, mine_ref, other_ref, pack_ref, inv_ref, res_ref, *rest, first):
    scens, windows, size, rhs = res_ref.shape
    if first:
        factor_ref, step_ref, image_ref, dots_ref, acc_ref = rest
        last = None
        acc_ref[...] = jnp.zeros_like(acc_ref)
    else:
        last = rest[:3]
        step_ref, left_ref, image_ref, dots_ref = rest[3:]
    nothing = jnp.zeros((size, rhs), HALF)
    side = 2 * size

    def body(batch, totals):
        along, energy = totals
        spots = [(batch * STEP_BATCH + s, w) for s in range(STEP_BATCH) for w in range(windows)]
        left = [residual(res_ref, last, s, w) for s, w in spots]
        packs, blocks, lifts = [], [], []
        for s, w in spots:
            slot, core_side = place(block_ref, core_ref, s, w)
            mine = mine_ref[slot].astype(F32)
            other = other_ref[slot].astype(F32)
            block = jnp.where(core_side == 0, mine, other).astype(HALF)
            pack = [pack_ref[s, w, :, part * side : (part + 1) * side] for part in range(4)]
            packs.append(pack)
            blocks.append(block)
            lifts.append(dot(wide2((pack[1], pack[3])), jnp.concatenate([nothing, block] * 2, axis=0)))
        found = []
        for (s, w), res, lift in zip(spots, left, lifts):
            inverse = inv_ref[s, w]
            found.append(dot(wide2((inverse, inverse)), tall2(split(res - lift))))
        steps = []
        for (s, w), value in zip(spots, found):
            step_ref[s, w] = value
            steps.append(split(value))
        images = []
        for at, (s, w) in enumerate(spots):
            before = steps[at - 1] if w > 0 else (nothing, nothing)
            after = steps[at + 1] if w < windows - 1 else (nothing, nothing)
            high = [before[0], steps[at][0], after[0], blocks[at]]
            low = [before[1], steps[at][1], after[1], nothing]
            one_high, two_high, one_low, two_low = packs[at]
            mats = [one_high, two_high, one_high, two_high, one_low, two_low]
            images.append(dot(jnp.concatenate(mats, axis=1), jnp.concatenate(high + low + high, axis=0)))
        terms = []
        for (s, w), res, image in zip(spots, left, images):
            inner = 0 < w < windows - 1
            if inner:
                along += fold(res * image)
                energy += fold(image * image)
            if first:
                image_ref[s, w] = image
                if inner:
                    terms.append((s, w, dot(factor_ref[s, w], tall3(split(image)))))
            elif not inner:
                spot = 0 if w == 0 else 1
                image_ref[s, spot] = image
                left_ref[s, spot] = res
        for s, w, term in terms:
            acc_ref[address(block_ref, core_ref, acc_ref.shape[0] // CORES, s, w)] += term
        return along, energy

    zero = jnp.zeros((8, rhs), F32)
    along, energy = lax.fori_loop(0, scens // STEP_BATCH, body, (zero, zero))
    dots_ref[0:8, :] = along
    dots_ref[8:16, :] = energy


def finish_kernel(core_ref, block_ref, image_ref, before_ref, after_ref, pair_ref, res_ref, dots_ref, *rest, first):
    scens, windows, _, size, _ = pair_ref.shape
    rhs = before_ref.shape[2]
    if first:
        factor_ref, acc_ref, side_ref, out_ref, keep_ref, send_ref, acc = rest
        acc[...] = acc_ref[...]
    else:
        (out_ref,) = rest
    along = jnp.zeros((8, rhs), F32)
    energy = jnp.zeros((8, rhs), F32)
    terms = []
    spots = [(s, spot) for s in range(scens) for spot in (0, 1)]
    halos = []
    for s, spot in spots:
        w = (windows - 1) * spot
        halo = (before_ref, after_ref)[spot][s]
        halos.append(dot(wide2(split(pair_ref[s, w, spot])), tall2((halo, halo))))
    for (s, spot), halo in zip(spots, halos):
        w = (windows - 1) * spot
        at = w if first else spot
        image = halo + image_ref[s, at]
        along += fold(res_ref[s, at] * image)
        energy += fold(image * image)
        if first:
            side_ref[s, spot] = image
            terms.append((s, w, dot(factor_ref[s, w], tall3(split(image)))))
    out_ref[0:8, :] = dots_ref[0:8, :] + along
    out_ref[8:16, :] = dots_ref[8:16, :] + energy
    if first:
        half = keep_ref.shape[0]
        for s, w, term in terms:
            acc[address(block_ref, core_ref, half, s, w)] += term
        keep_ref[...] = acc[0:half]
        send_ref[...] = acc[half:]


def first_image(weight, step, summed):
    size = step.shape[0]
    top = jnp.dot(weight[:, :size], step, precision=EXACT, preferred_element_type=F32)
    low = jnp.dot(weight[:, size:], step, precision=EXACT, preferred_element_type=F32)
    return jnp.concatenate([top, low], axis=0) - summed


def local_dots(dots, res, image):
    along = jnp.sum(dots[0:8] + fold(res * image), axis=0, keepdims=True)
    energy = jnp.sum(dots[8:16] + fold(image * image), axis=0, keepdims=True)
    return along, energy


def turn_kernel(arrived_ref, step_ref, sum_ref, weight_ref, first_ref, dots_ref, turn_ref, image_ref, message_ref):
    size = step_ref.shape[0]
    turn = jnp.sum(arrived_ref[...], axis=0)
    image = first_image(weight_ref[...], step_ref[...], sum_ref[...])
    turn_ref[...] = turn
    image_ref[...] = image
    change = (first_ref[...] + sum_ref[...]) - (image + turn)
    pieces = pieces_of(local_dots(dots_ref[...], first_ref[...], image)).astype(HALF)
    message = jnp.concatenate([change.astype(HALF), pieces], axis=0)
    message_ref[...] = jnp.broadcast_to(message[None], message_ref.shape)


def next_kernel(arrived_ref, step_ref, size_ref, next_ref, message_ref):
    rows = step_ref.shape[0]
    total = jnp.sum(arrived_ref[...].astype(F32), axis=0)
    along, energy = join_pieces(total[rows:])
    size = along / (energy + 1e-06)
    size_ref[...] = jnp.broadcast_to(size, size_ref.shape)
    step = ((1.0 - size) * step_ref[...] + size * total[:rows]).astype(HALF)
    next_ref[...] = step.astype(F32)
    message_ref[...] = jnp.broadcast_to(step[None], message_ref.shape)


def ending_kernel(
    size_ref, step_ref, sum_ref, turn_ref, weight_ref, first_ref, image_ref, dots_ref, next_ref, res_ref, out_ref
):
    size = size_ref[0:1]
    image = first_image(weight_ref[...], step_ref[...], sum_ref[...] - size * turn_ref[...])
    res = first_ref[...] - size * image_ref[...]
    next_ref[...] = image
    res_ref[...] = res
    along, energy = local_dots(dots_ref[...], res, image)
    row = lax.broadcasted_iota(jnp.int32, (2, along.shape[1]), 0)
    both = jnp.where(row == 0, jnp.broadcast_to(along, row.shape), jnp.broadcast_to(energy, row.shape))
    out_ref[...] = both


def final_kernel(
    arrived_ref, size_ref, step_ref, later_ref, first_ref, next_ref, res_ref, image_ref, sol_hbm, head_ref, out_ref, buffer, sem
):
    size = size_ref[0:1]
    total = fold(arrived_ref[...])
    along = total[0:1] + total[2:3] + total[4:5] + total[6:7]
    energy = total[1:2] + total[3:4] + total[5:6] + total[7:8]
    later = along / (energy + 1e-06)
    scens = step_ref.shape[0]
    copies = [pltpu.make_async_copy(buffer.at[s], sol_hbm.at[s], sem.at[s]) for s in range(scens)]
    for s in range(scens):
        buffer[s] = size * step_ref[s] + later * later_ref[s]
        copies[s].start()
    head_ref[...] = size * first_ref[...] + later * next_ref[...]
    out_ref[...] = res_ref[...] - later * image_ref[...]
    for s in range(scens):
        copies[s].wait()


def shape(*dims, kind=F32):
    return jax.ShapeDtypeStruct(dims, kind)


def in_hbm(*arrays):
    return [pltpu.with_memory_space_constraint(array, pltpu.HBM) for array in arrays]


def per_device(
    scen_rhs,
    first_rhs,
    diag_blocks,
    diag_inverse,
    couplings,
    border,
    border_block,
    first_diag,
    schur_inverse,
):
    core = lax.axis_index("core").astype(jnp.int32)
    scen_local, window_local, size, rhs = scen_rhs.shape
    group_rows = schur_inverse.shape[-1]
    blocks = group_rows // size
    half = blocks // CORES
    groups = lax.axis_size("fs")
    plane = CHIP_X * CHIP_Y
    columns = schur_inverse.shape[0] * schur_inverse.shape[1]
    schur_flat = schur_inverse.reshape(columns, group_rows)
    first_res = first_rhs.reshape(size, rhs)
    core_table = core.reshape(1)
    vmem = pl.BlockSpec(memory_space=pltpu.VMEM)
    field = (window_local, size, rhs)
    tile = (window_local, size, size)
    grid = (scen_local,)
    fields = shape(scen_local, *field)
    edges = shape(scen_local, size, rhs)
    vector = shape(size, rhs)

    def swap(values):
        return lax.ppermute(values, "core", SWAP)

    def spread_plane(values):
        return lax.all_to_all(values, PLANE, 0, 0)

    def spread_fs(values):
        return lax.all_to_all(values, "fs", 0, 0)

    def solve(arrived, with_dots):
        extra = 1 if with_dots else 0
        out_shape = [shape(half, size, rhs), shape(half + extra, size, rhs)]
        if with_dots:
            out_shape.append(shape(DOT_ROWS, rhs))
        kernel = functools.partial(solve_kernel, with_dots=with_dots)
        out = resident(kernel, out_shape, 1, (), core_table, arrived, schur_flat)
        theirs, pack = out[1], None
        if not with_dots:
            theirs, *tiles = lax.optimization_barrier((theirs, border, diag_blocks, couplings))
            pack = pl.pallas_call(
                pack_kernel,
                out_shape=shape(*scen_rhs.shape[:3], 8 * size, kind=HALF),
                in_specs=[vmem] * 3,
                out_specs=vmem,
                compiler_params=PLAIN,
                cost_estimate=pl.CostEstimate(flops=1 << 22, bytes_accessed=12 << 20, transcendentals=0),
                name="pack",
            )(*tiles)
        got = swap(theirs)
        if pack is not None:
            got, pack = lax.optimization_barrier((got, pack))
        rows_out = size + (DOT_ROWS if with_dots else 0)
        message = pl.pallas_call(
            pair_kernel,
            out_shape=shape(plane, rows_out, rhs, kind=HALF),
            compiler_params=PLAIN,
            name="pair",
        )(out[0], got, *out[2:])
        return spread_plane(message), pack

    def window_pass(message, last, pack):
        first = last is None
        mine = spread_plane(message)
        other = swap(mine)
        extra = () if first else last
        args = (core_table, border_block, mine, other, border, diag_inverse, scen_rhs)
        head, tail = resident(
            edge_kernel, [shape(scen_local, size, rhs, kind=HALF)] * 2, 2, (), *args, *extra
        )
        ends = groups - 1
        before = lax.ppermute(tail, "fs", [(i, i + 1) for i in range(ends)])
        after = lax.ppermute(head, "fs", [(i + 1, i) for i in range(ends)])
        sides_shape = shape(scen_local, 2, size, rhs)
        dots_shape = shape(DOT_ROWS, rhs)
        args = (core_table, border_block, mine, other, pack, diag_inverse, scen_rhs)
        kernel = functools.partial(step_kernel, first=first)
        finish = functools.partial(finish_kernel, first=first)
        if first:
            out_shape = [fields, fields, dots_shape, shape(blocks, size, rhs)]
            step, image, dots, acc = resident(kernel, out_shape, 2, (), *args, factor)
            out_shape = [sides_shape, dots_shape] + [shape(half, size, rhs)] * 2
            scratch = (pltpu.VMEM((blocks, size, rhs), F32),)
            args = (core_table, border_block, image, before, after, couplings, scen_rhs, dots, factor, acc)
            side, dots, keep, send = resident(finish, out_shape, 2, scratch, *args)
            return step, image, side, dots, keep, send
        out_shape = [fields, sides_shape, sides_shape, dots_shape]
        step, left, image, dots = resident(kernel, out_shape, 2, (), *args, *extra)
        args = (core_table, border_block, image, before, after, couplings, left, dots)
        (dots,) = resident(finish, [dots_shape], 2, (), *args)
        return step, dots

    def resident(kernel, out_shape, tables, scratch, *args):
        return pl.pallas_call(
            kernel,
            out_shape=out_shape,
            in_specs=[table()] * tables + [vmem] * (len(args) - tables),
            out_specs=[vmem] * len(out_shape),
            scratch_shapes=scratch,
            compiler_params=PLAIN,
            name=getattr(kernel, "func", kernel).__name__,
        )(*args)

    def small(kernel, out_shape, *args):
        return pl.pallas_call(
            kernel, out_shape=out_shape, compiler_params=PLAIN, name=kernel.__name__
        )(*args)

    tall = size + size // 2

    def batch_block(*dims):
        return pl.BlockSpec((BATCH,) + dims, lambda s: (s,) + (0,) * len(dims))

    factor, keep, send = pl.pallas_call(
        prepare_kernel,
        out_shape=[shape(*scen_rhs.shape[:3], 3 * size, kind=HALF)] + [shape(half, tall, rhs)] * 2,
        in_specs=[table()] * 2 + [pl.BlockSpec(memory_space=pltpu.HBM)] * 3,
        out_specs=[vmem] * 3,
        scratch_shapes=[
            pltpu.VMEM(scen_rhs.shape, F32),
            pltpu.VMEM(diag_inverse.shape, HALF),
            pltpu.VMEM(border.shape, F32),
            pltpu.VMEM((blocks, size, rhs + size), F32),
            pltpu.SemaphoreType.DMA((scen_local // BATCH, 3)),
        ],
        compiler_params=PLAIN,
        name="prepare",
    )(core_table, *in_hbm(border_block, scen_rhs, diag_inverse, border))
    arrived = spread_plane(keep + swap(send))
    guess_sum, weight, message = small(
        begin_kernel,
        [vector, shape(size // 2, 2 * size), shape(groups, size, rhs, kind=HALF)],
        arrived,
        first_res,
        first_diag,
    )
    arrived, pack = solve(spread_fs(message), False)
    first_step, message = small(owned_kernel, [vector, shape(plane, size, rhs, kind=HALF)], arrived)
    scen_step, image, side, dots, keep, send = window_pass(message, None, pack)
    arrived = spread_plane(keep + swap(send))
    turn, image_first, message = small(
        turn_kernel,
        [vector, vector, shape(groups, size + DOT_ROWS, rhs, kind=HALF)],
        arrived,
        first_step,
        guess_sum,
        weight,
        first_res,
        dots,
    )
    arrived, _ = solve(spread_fs(message), True)
    step_size, next_step, message = small(
        next_kernel, [shape(8, rhs), vector, shape(plane, size, rhs, kind=HALF)], arrived, first_step
    )
    later_step, dots = window_pass(message, (image, side, step_size), pack)
    next_image, first_left, both = small(
        ending_kernel,
        [vector, vector, shape(2, rhs)],
        step_size,
        next_step,
        guess_sum,
        turn,
        weight,
        first_res,
        image_first,
        dots,
    )
    both = both + swap(both)
    message = jnp.broadcast_to(both[None], (plane * groups, 2, rhs))
    arrived = lax.all_to_all(message, ("x", "y", "fs"), 0, 0).reshape(-1, rhs)
    scen_sol, first_sol, first_left = pl.pallas_call(
        final_kernel,
        out_shape=[fields, vector, vector],
        in_specs=[vmem] * 8,
        out_specs=[pl.BlockSpec(memory_space=pltpu.HBM), vmem, vmem],
        scratch_shapes=[pltpu.VMEM(scen_rhs.shape, F32), pltpu.SemaphoreType.DMA((scen_local,))],
        compiler_params=PLAIN,
        name="final",
    )(arrived, step_size, scen_step, later_step, first_step, next_step, first_left, next_image)
    return (scen_sol, first_sol.reshape(1, size, rhs), first_left.reshape(1, size, rhs))


def solution(mesh):
    groups = mesh.shape["fs"]
    grid = Mesh(
        mesh.devices.reshape(CHIP_X, CHIP_Y, CORES, groups), ("x", "y", "core", "fs")
    )
    return jax.shard_map(
        per_device,
        mesh=grid,
        in_specs=(
            P(SCEN, "fs", None, None),
            P("fs", SCEN, None),
            P(SCEN, "fs", None, None),
            P(SCEN, "fs", None, None),
            P(SCEN, "fs", None, None, None),
            P(SCEN, "fs", None, None),
            P(SCEN, "fs"),
            P("fs", SCEN),
            P(None, SCEN, "fs", None),
        ),
        out_specs=(
            P(SCEN, "fs", None, None),
            P("fs", SCEN, None),
            P("fs", SCEN, None),
        ),
        check_vma=False,
    )
```

```python
import functools

import jax
import jax.numpy as jnp
from jax import lax
from jax.experimental import pallas as pl
from jax.experimental.pallas import tpu as pltpu
from jax.sharding import Mesh
from jax.sharding import PartitionSpec as P

CHIP_X = 4
CHIP_Y = 4
CORES = 2
PLANE = ("x", "y")
SCEN = ("x", "y", "core")
SWAP = [(0, 1), (1, 0)]
F32 = jnp.float32
HALF = jnp.bfloat16
DOT_ROWS = 16
BATCH = 2
STEP_BATCH = 8
TILE_BLOCKS = 8
EXACT = lax.Precision.HIGHEST
PARAMS = pltpu.CompilerParams(
    dimension_semantics=("arbitrary",), vmem_limit_bytes=24 * 1024 * 1024
)
PLAIN = pltpu.CompilerParams(vmem_limit_bytes=16 * 1024 * 1024)


def split(values):
    high = values.astype(HALF)
    return high, (values - high.astype(F32)).astype(HALF)


def dot(left, right):
    return jnp.dot(left, right, preferred_element_type=F32)


def dot_t(left, right):
    return lax.dot_general(left, right, (((0,), (0,)), ((), ())), preferred_element_type=F32)


def wide2(pieces):
    return jnp.concatenate([pieces[0], pieces[1]], axis=1)


def wide3(pieces):
    return jnp.concatenate([pieces[0], pieces[0], pieces[1]], axis=1)


def tall2(pieces):
    return jnp.concatenate([pieces[0], pieces[1]], axis=0)


def tall3(pieces):
    return jnp.concatenate([pieces[0], pieces[1], pieces[0]], axis=0)


def pieces_of(vectors):
    rows = []
    for vector in vectors:
        high = vector.astype(HALF).astype(F32)
        rest = vector - high
        mid = rest.astype(HALF).astype(F32)
        rows += [high, mid, rest - mid]
    return stack_rows(rows)


def stack_rows(rows):
    width = rows[0].shape[-1]
    place = lax.broadcasted_iota(jnp.int32, (DOT_ROWS, width), 0)
    total = jnp.zeros((DOT_ROWS, width), F32)
    for index, row in enumerate(rows):
        total = jnp.where(place == index, jnp.broadcast_to(row, (DOT_ROWS, width)), total)
    return total


def join_pieces(rows):
    return rows[0:1] + rows[1:2] + rows[2:3], rows[3:4] + rows[4:5] + rows[5:6]


def fold(values):
    return jnp.sum(values.reshape(values.shape[0] // 8, 8, values.shape[1]), axis=0)


def first_block(*shape):
    return pl.BlockSpec((1,) + shape, lambda s, *_: (s,) + (0,) * len(shape))


def whole(*shape):
    return pl.BlockSpec(shape, lambda *_: (0,) * len(shape))


def table():
    return pl.BlockSpec(memory_space=pltpu.SMEM)


def place(block_ref, core_ref, s, w):
    block = block_ref[s, w]
    return block >> 1, jnp.bitwise_xor(block & 1, core_ref[0])


def address(block_ref, core_ref, half, s, w):
    slot, side = place(block_ref, core_ref, s, w)
    return side * half + slot


def prepare_kernel(
    core_ref, block_ref, res_hbm, inv_hbm, border_hbm, factor_ref, keep_ref, send_ref, res_ref, inv_ref, border_ref, acc, sem
):
    scens, windows, size, rhs = res_ref.shape
    half = keep_ref.shape[0]
    batches = scens // BATCH
    pairs = ((res_hbm, res_ref), (inv_hbm, inv_ref), (border_hbm, border_ref))

    def copies(batch):
        part = pl.ds(batch * BATCH, BATCH)
        return [
            pltpu.make_async_copy(source.at[part], target.at[part], sem.at[batch, index])
            for index, (source, target) in enumerate(pairs)
        ]

    for batch in range(batches):
        for copy in copies(batch):
            copy.start()
    acc[...] = jnp.zeros_like(acc)

    def body(batch, carry):
        for copy in copies(batch):
            copy.wait()
        spots = [(batch * BATCH + s, w) for s in range(BATCH) for w in range(windows)]
        tiles = [split(border_ref[s, w]) for s, w in spots]
        products = []
        for (s, w), tile in zip(spots, tiles):
            inverse = inv_ref[s, w]
            products.append(dot_t(tall2(tile), tall2((inverse, inverse))))
        terms = []
        for (s, w), tile, product in zip(spots, tiles, products):
            factor = wide3(split(product))
            factor_ref[s, w] = factor
            right = jnp.concatenate([tall3(split(res_ref[s, w])), tall3(tile)], axis=1)
            terms.append(dot(factor, right))
        for (s, w), term in zip(spots, terms):
            acc[address(block_ref, core_ref, half, s, w)] += term
        return carry

    lax.fori_loop(0, batches, body, 0)
    for start, out in ((0, keep_ref), (half, send_ref)):
        out[:, 0:size, :] = acc[start : start + half, :, 0:rhs]
        out[:, size:, 0:size] = acc[start : start + half, 0 : size // 2, rhs : rhs + size]
        out[:, size:, size:] = acc[start : start + half, size // 2 :, rhs : rhs + size]


def begin_kernel(arrived_ref, first_ref, diag_ref, sum_ref, weight_ref, message_ref):
    size = first_ref.shape[0]
    total = jnp.sum(arrived_ref[...], axis=0)
    summed = total[:size]
    sum_ref[...] = summed
    side = size // 2
    diag = jnp.concatenate([diag_ref[...], diag_ref[...]], axis=1)
    row = lax.broadcasted_iota(jnp.int32, (side, 2 * size), 0)
    lane = lax.broadcasted_iota(jnp.int32, (side, 2 * size), 1)
    spot = jnp.logical_or(lane == row, lane == row + side + size)
    weight_ref[...] = total[size:] + jnp.where(spot, jnp.broadcast_to(diag, (side, 2 * size)), 0.0)
    message = (first_ref[...] + summed).astype(HALF)
    message_ref[...] = jnp.broadcast_to(message[None], message_ref.shape)


def solve_kernel(core_ref, arrived_ref, schur_ref, mine_ref, theirs_ref, *rest, with_dots):
    groups = arrived_ref.shape[0]
    size = mine_ref.shape[1]
    wide = TILE_BLOCKS * size
    operand = jnp.concatenate([arrived_ref[g, 0:size, :] for g in range(groups)], axis=0)
    if with_dots:
        rows = jnp.sum(arrived_ref[:, size:, :].astype(F32), axis=0)
        dots = stack_rows(list(join_pieces(rows)))
        rest[0][...] = dots
        theirs_ref[theirs_ref.shape[0] - 1, 0:DOT_ROWS, :] = dots
    flipped = operand.T
    values = []
    for tile in range(schur_ref.shape[1] // wide):
        values.append(dot(flipped, schur_ref[:, tile * wide : (tile + 1) * wide]).T)

    def write(evens_ref, odds_ref):
        for tile, value in enumerate(values):
            for pair in range(TILE_BLOCKS // CORES):
                slot = tile * (TILE_BLOCKS // CORES) + pair
                evens_ref[slot] = value[(2 * pair) * size : (2 * pair + 1) * size]
                odds_ref[slot] = value[(2 * pair + 1) * size : (2 * pair + 2) * size]

    @pl.when(core_ref[0] == 0)
    def _():
        write(mine_ref, theirs_ref)

    @pl.when(core_ref[0] != 0)
    def _():
        write(theirs_ref, mine_ref)


def pair_kernel(mine_ref, got_ref, *rest):
    message_ref = rest[-1]
    plane, size, rhs = mine_ref.shape
    message_ref[:, 0:size, :] = (mine_ref[...] + got_ref[0:plane]).astype(HALF)
    if len(rest) > 1:
        dots = rest[0][...] + got_ref[plane, 0:DOT_ROWS, :]
        pieces = pieces_of([dots[0:1], dots[1:2]]).astype(HALF)
        message_ref[:, size:, :] = jnp.broadcast_to(pieces[None], (plane,) + pieces.shape)


def owned_kernel(arrived_ref, step_ref, message_ref):
    total = jnp.sum(arrived_ref[...].astype(F32), axis=0).astype(HALF)
    step_ref[...] = total.astype(F32)
    message_ref[...] = jnp.broadcast_to(total[None], message_ref.shape)


def residual(res_ref, last, s, w):
    if last is None:
        return res_ref[s, w]
    image_ref, side_ref, size_ref = last
    windows = res_ref.shape[1]
    if w == 0:
        image = side_ref[s, 0]
    elif w == windows - 1:
        image = side_ref[s, 1]
    else:
        image = image_ref[s, w]
    return res_ref[s, w] - size_ref[0:1] * image


def window_steps(tables, mine_ref, other_ref, border_ref, inv_ref, spots, values):
    core_ref, block_ref = tables
    lifts = []
    for s, w in spots:
        slot, side = place(block_ref, core_ref, s, w)
        mine = mine_ref[slot].astype(F32)
        other = other_ref[slot].astype(F32)
        block = jnp.where(side == 0, mine, other).astype(HALF)
        lifts.append(dot(wide2(split(border_ref[s, w])), tall2((block, block))))
    steps = []
    for (s, w), res, lift in zip(spots, values, lifts):
        inverse = inv_ref[s, w]
        steps.append(dot(wide2((inverse, inverse)), tall2(split(res - lift))))
    return steps


def edge_kernel(core_ref, block_ref, mine_ref, other_ref, border_ref, inv_ref, res_ref, *rest):
    head_ref, tail_ref = rest[-2:]
    last = rest[:3] if len(rest) > 2 else None
    scens, windows = res_ref.shape[:2]
    tables = (core_ref, block_ref)
    spots = [(s, w) for s in range(scens) for w in (0, windows - 1)]
    values = [residual(res_ref, last, s, w) for s, w in spots]
    steps = window_steps(tables, mine_ref, other_ref, border_ref, inv_ref, spots, values)
    for (s, w), step in zip(spots, steps):
        out = head_ref if w == 0 else tail_ref
        out[s] = step.astype(HALF)


def pack_kernel(border_ref, diag_ref, pair_ref, pack_ref):
    scens, windows, size, _ = diag_ref.shape
    side = 2 * size

    def body(s, carry):
        for w in range(windows):
            one = split(jnp.concatenate([pair_ref[s, w, 0], diag_ref[s, w]], axis=1))
            two = split(jnp.concatenate([pair_ref[s, w, 1], border_ref[s, w]], axis=1))
            for part, piece in enumerate((one[0], two[0], one[1], two[1])):
                pack_ref[s, w, :, part * side : (part + 1) * side] = piece
        return carry

    lax.fori_loop(0, scens, body, 0)


def step_kernel(core_ref, block_ref, mine_ref, other_ref, pack_ref, inv_ref, res_ref, *rest, first):
    scens, windows, size, rhs = res_ref.shape
    if first:
        factor_ref, step_ref, image_ref, dots_ref, acc_ref = rest
        last = None
        acc_ref[...] = jnp.zeros_like(acc_ref)
    else:
        last = rest[:3]
        step_ref, left_ref, image_ref, dots_ref = rest[3:]
    nothing = jnp.zeros((size, rhs), HALF)
    side = 2 * size

    def body(batch, totals):
        along, energy = totals
        spots = [(batch * STEP_BATCH + s, w) for s in range(STEP_BATCH) for w in range(windows)]
        left = [residual(res_ref, last, s, w) for s, w in spots]
        packs, blocks, lifts = [], [], []
        for s, w in spots:
            slot, core_side = place(block_ref, core_ref, s, w)
            mine = mine_ref[slot].astype(F32)
            other = other_ref[slot].astype(F32)
            block = jnp.where(core_side == 0, mine, other).astype(HALF)
            pack = [pack_ref[s, w, :, part * side : (part + 1) * side] for part in range(4)]
            packs.append(pack)
            blocks.append(block)
            lifts.append(dot(wide2((pack[1], pack[3])), jnp.concatenate([nothing, block] * 2, axis=0)))
        found = []
        for (s, w), res, lift in zip(spots, left, lifts):
            inverse = inv_ref[s, w]
            found.append(dot(wide2((inverse, inverse)), tall2(split(res - lift))))
        steps = []
        for (s, w), value in zip(spots, found):
            step_ref[s, w] = value
            steps.append(split(value))
        images = []
        for at, (s, w) in enumerate(spots):
            before = steps[at - 1] if w > 0 else (nothing, nothing)
            after = steps[at + 1] if w < windows - 1 else (nothing, nothing)
            high = [before[0], steps[at][0], after[0], blocks[at]]
            low = [before[1], steps[at][1], after[1], nothing]
            one_high, two_high, one_low, two_low = packs[at]
            mats = [one_high, two_high, one_high, two_high, one_low, two_low]
            images.append(dot(jnp.concatenate(mats, axis=1), jnp.concatenate(high + low + high, axis=0)))
        terms = []
        for (s, w), res, image in zip(spots, left, images):
            inner = 0 < w < windows - 1
            if inner:
                along += fold(res * image)
                energy += fold(image * image)
            if first:
                image_ref[s, w] = image
                if inner:
                    terms.append((s, w, dot(factor_ref[s, w], tall3(split(image)))))
            elif not inner:
                spot = 0 if w == 0 else 1
                image_ref[s, spot] = image
                left_ref[s, spot] = res
        for s, w, term in terms:
            acc_ref[address(block_ref, core_ref, acc_ref.shape[0] // CORES, s, w)] += term
        return along, energy

    zero = jnp.zeros((8, rhs), F32)
    along, energy = lax.fori_loop(0, scens // STEP_BATCH, body, (zero, zero))
    dots_ref[0:8, :] = along
    dots_ref[8:16, :] = energy


def finish_kernel(core_ref, block_ref, image_ref, before_ref, after_ref, pair_ref, res_ref, dots_ref, *rest, first):
    scens, windows, _, size, _ = pair_ref.shape
    rhs = before_ref.shape[2]
    if first:
        factor_ref, acc_ref, side_ref, out_ref, keep_ref, send_ref, acc = rest
        acc[...] = acc_ref[...]
    else:
        (out_ref,) = rest
    along = jnp.zeros((8, rhs), F32)
    energy = jnp.zeros((8, rhs), F32)
    terms = []
    spots = [(s, spot) for s in range(scens) for spot in (0, 1)]
    halos = []
    for s, spot in spots:
        w = (windows - 1) * spot
        halo = (before_ref, after_ref)[spot][s]
        halos.append(dot(wide2(split(pair_ref[s, w, spot])), tall2((halo, halo))))
    for (s, spot), halo in zip(spots, halos):
        w = (windows - 1) * spot
        at = w if first else spot
        image = halo + image_ref[s, at]
        along += fold(res_ref[s, at] * image)
        energy += fold(image * image)
        if first:
            side_ref[s, spot] = image
            terms.append((s, w, dot(factor_ref[s, w], tall3(split(image)))))
    out_ref[0:8, :] = dots_ref[0:8, :] + along
    out_ref[8:16, :] = dots_ref[8:16, :] + energy
    if first:
        half = keep_ref.shape[0]
        for s, w, term in terms:
            acc[address(block_ref, core_ref, half, s, w)] += term
        keep_ref[...] = acc[0:half]
        send_ref[...] = acc[half:]


def first_image(weight, step, summed):
    size = step.shape[0]
    top = jnp.dot(weight[:, :size], step, precision=EXACT, preferred_element_type=F32)
    low = jnp.dot(weight[:, size:], step, precision=EXACT, preferred_element_type=F32)
    return jnp.concatenate([top, low], axis=0) - summed


def local_dots(dots, res, image):
    along = jnp.sum(dots[0:8] + fold(res * image), axis=0, keepdims=True)
    energy = jnp.sum(dots[8:16] + fold(image * image), axis=0, keepdims=True)
    return along, energy


def turn_kernel(arrived_ref, step_ref, sum_ref, weight_ref, first_ref, dots_ref, turn_ref, image_ref, message_ref):
    size = step_ref.shape[0]
    turn = jnp.sum(arrived_ref[...], axis=0)
    image = first_image(weight_ref[...], step_ref[...], sum_ref[...])
    turn_ref[...] = turn
    image_ref[...] = image
    change = (first_ref[...] + sum_ref[...]) - (image + turn)
    pieces = pieces_of(local_dots(dots_ref[...], first_ref[...], image)).astype(HALF)
    message = jnp.concatenate([change.astype(HALF), pieces], axis=0)
    message_ref[...] = jnp.broadcast_to(message[None], message_ref.shape)


def next_kernel(arrived_ref, step_ref, size_ref, next_ref, message_ref):
    rows = step_ref.shape[0]
    total = jnp.sum(arrived_ref[...].astype(F32), axis=0)
    along, energy = join_pieces(total[rows:])
    size = along / (energy + 1e-06)
    size_ref[...] = jnp.broadcast_to(size, size_ref.shape)
    step = ((1.0 - size) * step_ref[...] + size * total[:rows]).astype(HALF)
    next_ref[...] = step.astype(F32)
    message_ref[...] = jnp.broadcast_to(step[None], message_ref.shape)


def ending_kernel(
    size_ref, step_ref, sum_ref, turn_ref, weight_ref, first_ref, image_ref, dots_ref, next_ref, res_ref, out_ref
):
    size = size_ref[0:1]
    image = first_image(weight_ref[...], step_ref[...], sum_ref[...] - size * turn_ref[...])
    res = first_ref[...] - size * image_ref[...]
    next_ref[...] = image
    res_ref[...] = res
    along, energy = local_dots(dots_ref[...], res, image)
    row = lax.broadcasted_iota(jnp.int32, (2, along.shape[1]), 0)
    both = jnp.where(row == 0, jnp.broadcast_to(along, row.shape), jnp.broadcast_to(energy, row.shape))
    out_ref[...] = both


def final_kernel(
    arrived_ref, size_ref, step_ref, later_ref, first_ref, next_ref, res_ref, image_ref, sol_ref, head_ref, out_ref, later_size
):
    scen = pl.program_id(0)
    size = size_ref[0:1]

    @pl.when(scen == 0)
    def _():
        total = jnp.sum(arrived_ref[...], axis=0)
        later = total[0:1] / (total[1:2] + 1e-06)
        later_size[...] = jnp.broadcast_to(later, later_size.shape)
        head_ref[...] = size * first_ref[...] + later * next_ref[...]
        out_ref[...] = res_ref[...] - later * image_ref[...]

    scens = sol_ref.shape[0]
    for s in range(scens):
        at = scen * scens + s
        sol_ref[s] = size * step_ref[at] + later_size[0:1] * later_ref[at]


def shape(*dims, kind=F32):
    return jax.ShapeDtypeStruct(dims, kind)


def in_hbm(*arrays):
    return [pltpu.with_memory_space_constraint(array, pltpu.HBM) for array in arrays]


def per_device(
    scen_rhs,
    first_rhs,
    diag_blocks,
    diag_inverse,
    couplings,
    border,
    border_block,
    first_diag,
    schur_inverse,
):
    core = lax.axis_index("core").astype(jnp.int32)
    scen_local, window_local, size, rhs = scen_rhs.shape
    group_rows = schur_inverse.shape[-1]
    blocks = group_rows // size
    half = blocks // CORES
    groups = lax.axis_size("fs")
    plane = CHIP_X * CHIP_Y
    columns = schur_inverse.shape[0] * schur_inverse.shape[1]
    schur_flat = schur_inverse.reshape(columns, group_rows)
    first_res = first_rhs.reshape(size, rhs)
    core_table = core.reshape(1)
    vmem = pl.BlockSpec(memory_space=pltpu.VMEM)
    field = (window_local, size, rhs)
    tile = (window_local, size, size)
    grid = (scen_local,)
    fields = shape(scen_local, *field)
    edges = shape(scen_local, size, rhs)
    vector = shape(size, rhs)

    def swap(values):
        return lax.ppermute(values, "core", SWAP)

    def spread_plane(values):
        return lax.all_to_all(values, PLANE, 0, 0)

    def spread_fs(values):
        return lax.all_to_all(values, "fs", 0, 0)

    def solve(arrived, with_dots):
        extra = 1 if with_dots else 0
        out_shape = [shape(half, size, rhs), shape(half + extra, size, rhs)]
        if with_dots:
            out_shape.append(shape(DOT_ROWS, rhs))
        kernel = functools.partial(solve_kernel, with_dots=with_dots)
        out = resident(kernel, out_shape, 1, (), core_table, arrived, schur_flat)
        theirs, pack = out[1], None
        if not with_dots:
            theirs, *tiles = lax.optimization_barrier((theirs, border, diag_blocks, couplings))
            pack = pl.pallas_call(
                pack_kernel,
                out_shape=shape(*scen_rhs.shape[:3], 8 * size, kind=HALF),
                in_specs=[vmem] * 3,
                out_specs=vmem,
                compiler_params=PLAIN,
                cost_estimate=pl.CostEstimate(flops=1 << 22, bytes_accessed=12 << 20, transcendentals=0),
                name="pack",
            )(*tiles)
        got = swap(theirs)
        if pack is not None:
            got, pack = lax.optimization_barrier((got, pack))
        rows_out = size + (DOT_ROWS if with_dots else 0)
        message = pl.pallas_call(
            pair_kernel,
            out_shape=shape(plane, rows_out, rhs, kind=HALF),
            compiler_params=PLAIN,
            name="pair",
        )(out[0], got, *out[2:])
        return spread_plane(message), pack

    def window_pass(message, last, pack):
        first = last is None
        mine = spread_plane(message)
        other = swap(mine)
        extra = () if first else last
        args = (core_table, border_block, mine, other, border, diag_inverse, scen_rhs)
        head, tail = resident(
            edge_kernel, [shape(scen_local, size, rhs, kind=HALF)] * 2, 2, (), *args, *extra
        )
        ends = groups - 1
        before = lax.ppermute(tail, "fs", [(i, i + 1) for i in range(ends)])
        after = lax.ppermute(head, "fs", [(i + 1, i) for i in range(ends)])
        sides_shape = shape(scen_local, 2, size, rhs)
        dots_shape = shape(DOT_ROWS, rhs)
        args = (core_table, border_block, mine, other, pack, diag_inverse, scen_rhs)
        kernel = functools.partial(step_kernel, first=first)
        finish = functools.partial(finish_kernel, first=first)
        if first:
            out_shape = [fields, fields, dots_shape, shape(blocks, size, rhs)]
            step, image, dots, acc = resident(kernel, out_shape, 2, (), *args, factor)
            out_shape = [sides_shape, dots_shape] + [shape(half, size, rhs)] * 2
            scratch = (pltpu.VMEM((blocks, size, rhs), F32),)
            args = (core_table, border_block, image, before, after, couplings, scen_rhs, dots, factor, acc)
            side, dots, keep, send = resident(finish, out_shape, 2, scratch, *args)
            return step, image, side, dots, keep, send
        out_shape = [fields, sides_shape, sides_shape, dots_shape]
        step, left, image, dots = resident(kernel, out_shape, 2, (), *args, *extra)
        args = (core_table, border_block, image, before, after, couplings, left, dots)
        (dots,) = resident(finish, [dots_shape], 2, (), *args)
        return step, dots

    def resident(kernel, out_shape, tables, scratch, *args):
        return pl.pallas_call(
            kernel,
            out_shape=out_shape,
            in_specs=[table()] * tables + [vmem] * (len(args) - tables),
            out_specs=[vmem] * len(out_shape),
            scratch_shapes=scratch,
            compiler_params=PLAIN,
            name=getattr(kernel, "func", kernel).__name__,
        )(*args)

    def small(kernel, out_shape, *args):
        return pl.pallas_call(
            kernel, out_shape=out_shape, compiler_params=PLAIN, name=kernel.__name__
        )(*args)

    tall = size + size // 2

    def batch_block(*dims):
        return pl.BlockSpec((BATCH,) + dims, lambda s: (s,) + (0,) * len(dims))

    factor, keep, send = pl.pallas_call(
        prepare_kernel,
        out_shape=[shape(*scen_rhs.shape[:3], 3 * size, kind=HALF)] + [shape(half, tall, rhs)] * 2,
        in_specs=[table()] * 2 + [pl.BlockSpec(memory_space=pltpu.HBM)] * 3,
        out_specs=[vmem] * 3,
        scratch_shapes=[
            pltpu.VMEM(scen_rhs.shape, F32),
            pltpu.VMEM(diag_inverse.shape, HALF),
            pltpu.VMEM(border.shape, F32),
            pltpu.VMEM((blocks, size, rhs + size), F32),
            pltpu.SemaphoreType.DMA((scen_local // BATCH, 3)),
        ],
        compiler_params=PLAIN,
        name="prepare",
    )(core_table, *in_hbm(border_block, scen_rhs, diag_inverse, border))
    arrived = spread_plane(keep + swap(send))
    guess_sum, weight, message = small(
        begin_kernel,
        [vector, shape(size // 2, 2 * size), shape(groups, size, rhs, kind=HALF)],
        arrived,
        first_res,
        first_diag,
    )
    arrived, pack = solve(spread_fs(message), False)
    first_step, message = small(owned_kernel, [vector, shape(plane, size, rhs, kind=HALF)], arrived)
    scen_step, image, side, dots, keep, send = window_pass(message, None, pack)
    arrived = spread_plane(keep + swap(send))
    turn, image_first, message = small(
        turn_kernel,
        [vector, vector, shape(groups, size + DOT_ROWS, rhs, kind=HALF)],
        arrived,
        first_step,
        guess_sum,
        weight,
        first_res,
        dots,
    )
    arrived, _ = solve(spread_fs(message), True)
    step_size, next_step, message = small(
        next_kernel, [shape(8, rhs), vector, shape(plane, size, rhs, kind=HALF)], arrived, first_step
    )
    later_step, dots = window_pass(message, (image, side, step_size), pack)
    next_image, first_left, both = small(
        ending_kernel,
        [vector, vector, shape(2, rhs)],
        step_size,
        next_step,
        guess_sum,
        turn,
        weight,
        first_res,
        image_first,
        dots,
    )
    both = both + swap(both)
    message = jnp.broadcast_to(both[None], (plane * groups, 2, rhs))
    arrived = lax.all_to_all(message, ("x", "y", "fs"), 0, 0)
    scen_sol, first_sol, first_left = pl.pallas_call(
        final_kernel,
        out_shape=[fields, vector, vector],
        grid=(scen_local // BATCH,),
        in_specs=[vmem] * 8,
        out_specs=[batch_block(*field), whole(size, rhs), whole(size, rhs)],
        scratch_shapes=[pltpu.VMEM((8, rhs), F32)],
        compiler_params=PARAMS,
        name="final",
    )(arrived, step_size, scen_step, later_step, first_step, next_step, first_left, next_image)
    return (scen_sol, first_sol.reshape(1, size, rhs), first_left.reshape(1, size, rhs))


def solution(mesh):
    groups = mesh.shape["fs"]
    grid = Mesh(
        mesh.devices.reshape(CHIP_X, CHIP_Y, CORES, groups), ("x", "y", "core", "fs")
    )
    return jax.shard_map(
        per_device,
        mesh=grid,
        in_specs=(
            P(SCEN, "fs", None, None),
            P("fs", SCEN, None),
            P(SCEN, "fs", None, None),
            P(SCEN, "fs", None, None),
            P(SCEN, "fs", None, None, None),
            P(SCEN, "fs", None, None),
            P(SCEN, "fs"),
            P("fs", SCEN),
            P(None, SCEN, "fs", None),
        ),
        out_specs=(
            P(SCEN, "fs", None, None),
            P("fs", SCEN, None),
            P("fs", SCEN, None),
        ),
        check_vma=False,
    )
```
